256 devices in a mesh: snap: 8 (over x, core), lag: 32 (over z, y).
Axes of the slice: x: 4, y: 4, z: 8, core: 2. Of those that a mesh axis runs over, the one named last changes fastest.
Arguments:
- snapshots: bfloat16 [2, 32768, 256], P(None, 'snap', 'lag')
- positions: int32 [256], replicated, may hold values from 0 to 16383, as said below
- counts: int32 [8], P('snap'), may hold values from 1 to 4096, 16384 in all
- initial: float32 [2, 96, 16384], P(None, None, 'lag'), may hold values from -6 to 6
Outputs:
- lag_corr: float32 [2, 16384], P(None, 'lag')
- subspace: float32 [2, 96, 16384], P(None, None, 'lag')
The draws below stay inside these ranges and needn't reach their ends.
Inputs may be any that keep to these rules, and one draw needn't show every extreme that they name: `positions`: positions are distinct; 0 and 16383 are among them.
All inputs are finite; a program needn't handle non-finite values. No bound on the sum of `counts` on one device may be relied on, other than what follows from the above.
Results may differ from the reference program's by a relative error of at most 0.0003.
Values may be sent and summed in bfloat16 or wider, within the bound.
A program may use at most 64 MiB of HBM per device.

```python
import math
import jax
import jax.numpy as jnp
import numpy as np
from jax import lax

SENSORS = 256
LAGS = 16384
ITERS = 2
SNAP_DEV = 4096
COLUMNS = 96
N_SNAP = 8


wave_count = 128


def sensor_layout(key):
    inner = jax.random.permutation(jax.random.fold_in(key, 7), LAGS - 2)[:SENSORS - 2] + 1
    head = jnp.zeros((1,), jnp.int32)
    tail = jnp.full((1,), LAGS - 1, jnp.int32)
    return jnp.concatenate([head, inner.astype(jnp.int32), tail])


def draw_positions(key, part):
    return sensor_layout(key)


def draw_snapshots(key, part):
    placed = sensor_layout(key).astype(jnp.float32)
    keys = jax.random.split(jax.random.fold_in(key, 29), 4)
    directions = jax.random.uniform(keys[0], (wave_count,), jnp.float32, -1.0, 1.0)
    powers = jnp.exp(jax.random.uniform(keys[1], (wave_count,), jnp.float32, math.log(0.5), math.log(2.0)))
    spread = jnp.sqrt(powers / (2.0 * wave_count))
    amplitude = jax.random.normal(keys[2], (2, SNAP_DEV * N_SNAP, wave_count), jnp.float32)
    noise_level = 0.3
    amplitude = amplitude * spread[None, None, :]
    phase = math.pi * placed[:, None] * directions[None, :]
    cosine = jnp.cos(phase)
    sine = jnp.sin(phase)
    real_part = amplitude[0] @ cosine.T - amplitude[1] @ sine.T
    imag_part = amplitude[0] @ sine.T + amplitude[1] @ cosine.T
    noise = noise_level * jax.random.normal(keys[3], (2, SNAP_DEV * N_SNAP, SENSORS), jnp.float32)
    return (jnp.stack([real_part, imag_part]) + noise).astype(jnp.bfloat16)


def block_scale(stream_key, extent, cuts, smallest, high):
    level, own = 1.0, jax.random.fold_in(stream_key, 6)
    for position, parts in cuts:
        draws = jnp.exp(jax.random.uniform(jax.random.fold_in(own, position), (parts,), jnp.float32, smallest / len(cuts), high / len(cuts)))
        level = level * jnp.repeat(draws, extent[position] // parts).reshape([-1 if axis == position else 1 for axis in range(len(extent))])
    return level


def length_profile(amount, total, limit, slope):
    weights = [(1 << 20) // math.isqrt(grade ** slope) + 1 for grade in range(2, amount + 1)]
    rest, given = total - limit - (amount - 1), [1] * (amount - 1)
    while rest > 0:
        candidates = [i for i in range(amount - 1) if given[i] < limit]
        pool, budget = sum([weights[i] for i in candidates]), rest
        for i in candidates:
            addition = min(limit - given[i], max(1, budget * weights[i] // pool), rest)
            given[i] = given[i] + addition
            rest = rest - addition
    return np.array([limit] + given)


def ragged(key, amount, total, most, slope):
    if amount == 2:
        one = jax.random.randint(key, (), max(1, total - most), min(most, total - 1) + 1)
        return jnp.stack([one, total - one])
    lengths = jnp.asarray(length_profile(amount, total, most, slope), jnp.int32)
    pairs = (amount - 1) // 2
    giver, receiver = lengths[1:1 + 2 * pairs:2], lengths[2:2 + 2 * pairs:2]
    room = jnp.minimum(giver - 1, most - receiver)
    moved = jax.random.randint(jax.random.fold_in(key, 1), (pairs,), 0, 1 << 20) % (room + 1)
    lengths = lengths.at[1:1 + 2 * pairs:2].set(giver - moved).at[2:2 + 2 * pairs:2].set(receiver + moved)
    return lengths[jax.random.permutation(jax.random.fold_in(key, 2), amount)]


def normal_values(stream_key, dims, scale, reach, pieces=(), kind=jnp.bfloat16):
    values = scale * jax.random.normal(stream_key, dims, jnp.float32)
    if pieces:
        values = values * block_scale(stream_key, dims, pieces, -0.22, 0.18)
    return jnp.clip(values, -reach, reach).astype(kind)


def setup_inputs(seed: int = 0) -> dict:
    streams_of = jax.random.split(jax.random.key(seed), 5)
    snapshots = draw_snapshots(jax.random.fold_in(streams_of[4], 71), 0)
    positions = draw_positions(jax.random.fold_in(streams_of[4], 71), 0)
    counts = ragged(streams_of[2], N_SNAP, SNAP_DEV * N_SNAP // 2, SNAP_DEV, 2).astype(jnp.int32)
    initial = normal_values(streams_of[3], (2, COLUMNS, LAGS), 1.0, 6.0, ((2, 32),), jnp.float32)
    return {"snapshots": snapshots, "positions": positions, "counts": counts, "initial": initial}


exact = lax.Precision.HIGHEST

def correlate(former, latter):

    def product(left_rows, right_rows):
        return jnp.dot(left_rows.T.astype(jnp.float32), right_rows.astype(jnp.float32), preferred_element_type=jnp.float32)
    real_part = product(former[0], latter[0]) + product(former[1], latter[1])
    imag_part = product(former[1], latter[0]) - product(former[0], latter[1])
    return (real_part, imag_part)

def toeplitz_apply(columns, spectrum):
    complex_columns = columns[0] + 1j * columns[1]
    transformed = jnp.fft.fft(complex_columns, n=2 * LAGS, axis=1)
    mapped = jnp.fft.ifft(transformed * spectrum[None, :], axis=1)[:, :LAGS]
    return jnp.stack([jnp.real(mapped), jnp.imag(mapped)])

def reference(snapshots, positions, counts, initial):
    row_ids = jnp.arange(snapshots.shape[1], dtype=jnp.int32)
    live_rows = row_ids % SNAP_DEV < counts[row_ids // SNAP_DEV]
    masked = jnp.where(live_rows[None, :, None], snapshots, jnp.zeros((), snapshots.dtype))
    corr_real, corr_imag = correlate(masked, masked)
    pair_lags = positions[:, None] - positions[None, :]
    usable = pair_lags >= 0
    pair_bins = jnp.where(usable, pair_lags, LAGS).reshape(-1).astype(jnp.int32)

    def binned(values):
        return jax.ops.segment_sum(values.reshape(-1), pair_bins, num_segments=LAGS + 1)[:LAGS]
    pair_count = binned(usable.astype(jnp.float32))
    snap_total = jnp.sum(counts).astype(jnp.float32)
    divisor = jnp.maximum(pair_count, 1.0) * snap_total
    lag_corr = jnp.stack([binned(corr_real) / divisor, binned(corr_imag) / divisor])
    halves = jnp.where(jnp.arange(LAGS) == 0, 0.5, 1.0).astype(jnp.float32)
    weighted = lag_corr[0] * halves + 1j * (lag_corr[1] * halves)
    spectrum = 2.0 * jnp.real(jnp.fft.fft(weighted, n=2 * LAGS))
    columns = initial
    for sweep in range(ITERS):
        mapped = toeplitz_apply(columns, spectrum)
        gram_matrix = jnp.einsum('xaj,xbj->ab', mapped, mapped, precision=exact) / LAGS
        factor = jnp.linalg.cholesky(gram_matrix)
        identity = jnp.eye(gram_matrix.shape[0], dtype=gram_matrix.dtype)
        inverse = lax.linalg.triangular_solve(factor, identity, left_side=True, lower=True)
        columns = jnp.einsum('ab,xbj->xaj', inverse, mapped, precision=exact)
    return (lag_corr, columns)
```

```python
import functools
import math

import jax
import jax.numpy as jnp
import numpy as np
from jax import lax
from jax.experimental import pallas as pl
from jax.experimental.pallas import tpu as pltpu
from jax.sharding import PartitionSpec as P

MESH = pl.DeviceIdType.MESH
F32 = jnp.float32
BF16 = jnp.bfloat16
ITERS = 2
SENSORS = 256
LAGS = 16384
ROWS = 4096
COLUMNS = 96
N_SNAP = 8
N_LAG = 32
OWN = COLUMNS // N_SNAP
LANES = 128
PADDED = 2 * LAGS
FIRST = PADDED // LANES
HALF = LAGS // LANES
PER = HALF // N_LAG

SNAPS, CORR, CORR_ALL, BINS, LAGCORR, COLS = range(6)
IMAGE, IMAGE_ALL, GRAM, GRAM_ALL = range(6, 10)
PHASES = 6 + 4 * ITERS


def tables():
    rows = np.arange(2 * HALF)
    owner, part, place = rows // (2 * PER), rows // PER % 2, rows % PER
    lag_row = owner * PER + place
    first = np.arange(FIRST)
    lane = np.arange(LANES)
    turn = 2.0 * math.pi * (np.outer(first, lag_row) % FIRST) / FIRST
    cosine, sine = np.cos(turn), np.sin(turn)
    real = part[None, :] == 0
    forward = np.concatenate([np.where(real, cosine, sine), np.where(real, -sine, cosine)], 0)
    backward = np.concatenate(
        [np.where(real, cosine, sine).T, np.where(real, -sine, cosine).T], 1
    )
    small = 2.0 * math.pi * (np.outer(lane, lane) % LANES) / LANES
    c, s = np.cos(small), np.sin(small)
    across = np.block([[c, -s], [s, c]])
    back = np.block([[c, s], [-s, c]])
    twist = 2.0 * math.pi * np.outer(first, lane) / PADDED
    twists = np.stack([np.cos(twist), np.sin(twist)])
    return tuple(t.astype(np.float32) for t in (forward, across, back, backward, twists))


def dot(a, b, precision=lax.Precision.HIGHEST):
    return lax.dot_general(a, b, (((1,), (0,)), ((), ())), precision=precision, preferred_element_type=F32)


def dot_nt(a, b, precision=lax.Precision.HIGHEST):
    return lax.dot_general(a, b, (((1,), (1,)), ((), ())), precision=precision, preferred_element_type=F32)


def inverse_factor(gram):
    rows = lax.broadcasted_iota(jnp.int32, (COLUMNS, LANES), 0)
    cols = lax.broadcasted_iota(jnp.int32, (COLUMNS, LANES), 1)
    lane = lax.broadcasted_iota(jnp.int32, (1, LANES), 1)
    state = gram
    for j in range(COLUMNS - 1):
        row = state[j : j + 1, :]
        scale = 1.0 / row[:, j : j + 1]
        multiplier = jnp.where(rows[:, :1] > j, state[:, j : j + 1] * scale, 0.0)
        row = jnp.where(lane == j, 1.0, row)
        state = jnp.where((cols == j) & (rows > j), 0.0, state) - multiplier * row
    diagonal = jnp.sum(jnp.where(rows == cols, state, 0.0), axis=1, keepdims=True)
    unit = jnp.where(cols < rows, state, jnp.where(cols == rows, 1.0, 0.0))
    return unit * (1.0 / jnp.sqrt(diagonal))


def kernel(
    counts, positions, snaps, initial, forward, across, back, backward, twists,
    lag_out, sub_out,
    snap_send, snap_recv, corr_send, corr_recv, row_send, row_recv, bin_send, bin_recv,
    lag_send, lag_recv, col_recv, image_send, image_all, gram_send, gram_recv, tile_send, gram_all,
    send_sems, recv_sems,
):
    me, block = lax.axis_index("lag"), lax.axis_index("snap")
    mine = (3 * me + 7) // 8
    active = (8 * mine) // 3 == me
    own_col = jnp.minimum(mine, OWN - 1)

    def along(axis, size, here, act):
        def body(k, carry):
            act(lax.rem(here + k, size))
            return carry

        lax.fori_loop(1, size, body, 0)

    def send(phase, src, dst, axis, peer):
        pltpu.make_async_remote_copy(
            src_ref=src, dst_ref=dst, send_sem=send_sems.at[phase], recv_sem=recv_sems.at[phase],
            device_id={axis: peer}, device_id_type=MESH,
        ).start()

    def to_lags(phase, src_of, dst):
        along("lag", N_LAG, me, lambda p: send(phase, src_of(p), dst, "lag", p))

    def to_snaps(phase, src, dst):
        along("snap", N_SNAP, block, lambda p: send(phase, src, dst, "snap", p))

    def to_owners(phase, src_of, dst):
        def body(k, carry):
            j = lax.rem(own_col + k, OWN)
            owner = (8 * j) // 3

            @pl.when(owner != me)
            def _():
                send(phase, src_of(j), dst, "lag", owner)

            return carry

        lax.fori_loop(0, OWN, body, 0)

    def wait(sems, phase, ref):
        pltpu.make_async_copy(ref, ref, sems.at[phase]).wait()

    barrier = pltpu.get_barrier_semaphore()
    along("lag", N_LAG, me, lambda p: pl.semaphore_signal(
        barrier, inc=1, device_id={"lag": p}, device_id_type=MESH))
    along("snap", N_SNAP, block, lambda p: pl.semaphore_signal(
        barrier, inc=1, device_id={"snap": p}, device_id_type=MESH))

    live = lax.broadcasted_iota(jnp.int32, (8, ROWS), 1) < counts[0]
    for c in range(2):
        snap_send[c] = jnp.where(live, snaps[c].astype(F32), 0.0).astype(BF16)
    pl.semaphore_wait(barrier, N_LAG + N_SNAP - 2)

    def snap_piece(p):
        return snap_send.at[:, :, pl.ds(pl.multiple_of(p * LANES, LANES), LANES)]

    to_lags(SNAPS, snap_piece, snap_recv.at[me])
    snap_recv[me] = snap_send[:, :, pl.ds(pl.multiple_of(me * LANES, LANES), LANES)]
    to_owners(COLS, lambda j: initial.at[j], col_recv.at[me])

    @pl.when(active)
    def _():
        col_recv[me] = initial[own_col]

    wait(recv_sems, SNAPS, snap_recv.at[pl.ds(0, N_LAG - 1)])
    x = [snap_recv[:, c].astype(F32).reshape(SENSORS, LANES) for c in range(2)]
    left = jnp.concatenate([x[0], x[1]], 1).astype(BF16)
    turned = jnp.concatenate([x[1], -x[0]], 1).astype(BF16)
    real = dot_nt(left, left, None)
    imag = dot_nt(turned, left, None)
    square = (SENSORS, SENSORS)
    below = lax.broadcasted_iota(jnp.int32, square, 0) >= lax.broadcasted_iota(jnp.int32, square, 1)
    corr_send[...] = jnp.where(below, real, imag)

    def rows_of(p):
        return pl.ds(pl.multiple_of(p * 8, 8), 8)

    to_lags(CORR, lambda p: corr_send.at[rows_of(p)], corr_recv.at[me])
    corr_recv[me] = corr_send[rows_of(me), :]

    strip = (8, SENSORS)
    sensor = me * 8 + lax.broadcasted_iota(jnp.int32, strip, 0)
    other = lax.broadcasted_iota(jnp.int32, strip, 1)
    place = jnp.broadcast_to(positions[...], strip).astype(F32)
    own_place = jnp.sum(jnp.where(sensor == other, place, 0.0), axis=1, keepdims=True)
    gap = own_place - place
    lags = jnp.abs(gap).astype(jnp.int32)
    lower = sensor >= other
    high = lags // LANES
    target = (high // PER) * (2 * PER) + jnp.where(lower, 0, PER) + high % PER
    low = lags % LANES
    sign = jnp.where(lower | (gap > 0.0), 1.0, -1.0)

    wait(recv_sems, CORR, corr_recv.at[pl.ds(0, N_LAG - 1)])
    row_send[:, :SENSORS] = jnp.sum(corr_recv[...], axis=0)
    row_send[:, SENSORS:] = jnp.full((8, LANES), counts[0].astype(F32), F32)
    row_recv[block] = row_send[...]
    to_snaps(CORR_ALL, row_send, row_recv.at[block])
    wait(recv_sems, CORR_ALL, row_recv.at[pl.ds(0, N_SNAP - 1)])
    summed = jnp.sum(row_recv[...], axis=0)
    values = summed[:, :SENSORS] * sign
    total = summed[:, SENSORS:]

    row_ids = lax.broadcasted_iota(jnp.int32, (2 * HALF, SENSORS), 0)
    lane_ids = lax.broadcasted_iota(jnp.int32, (LANES, SENSORS), 0)
    part_0 = values.astype(BF16).astype(F32)
    part_1 = (values - part_0).astype(BF16).astype(F32)
    part_2 = values - part_0 - part_1
    high_hot, low_hot = [], []
    for r in range(8):
        one = slice(r, r + 1)
        high_hot.append(jnp.where(row_ids == target[one], 1.0, 0.0).astype(BF16))
        hit = lane_ids == low[one]
        low_hot.append(
            jnp.concatenate(
                [jnp.where(hit, part[one], 0.0).astype(BF16) for part in (part_0, part_1, part_2)]
                + [jnp.where(hit, 1.0, 0.0).astype(BF16)],
                0,
            )
        )
    bins = dot_nt(jnp.concatenate(high_hot, 1), jnp.concatenate(low_hot, 1), None)
    bin_send[:, :LANES] = bins[:, :LANES] + bins[:, LANES : 2 * LANES] + bins[:, 2 * LANES : 3 * LANES]
    bin_send[:, LANES:] = bins[:, 3 * LANES :]
    to_lags(BINS, lambda p: bin_send.at[rows_of(p)], bin_recv.at[me])
    bin_recv[me] = bin_send[rows_of(me), :]
    wait(recv_sems, BINS, bin_recv.at[pl.ds(0, N_LAG - 1)])
    lag_sums = jnp.sum(bin_recv[...], axis=0)
    lag_corr = lag_sums[:, :LANES] / (jnp.maximum(lag_sums[:, LANES:], 1.0) * total)
    lag_send[...] = lag_corr
    to_lags(LAGCORR, lambda p: lag_send, lag_recv.at[me])
    lag_recv[me] = lag_corr
    for c in range(2):
        for r in range(PER):
            lag_out[c : c + 1, r * LANES : (r + 1) * LANES] = lag_corr[c * PER + r : c * PER + r + 1, :]
    wait(recv_sems, LAGCORR, lag_recv.at[pl.ds(0, N_LAG - 1)])

    def rising(v):
        a = dot(forward[...], v)
        ar, ai = a[:FIRST], a[FIRST:]
        tc, ts = twists[0], twists[1]
        return jnp.concatenate([ar * tc + ai * ts, ai * tc - ar * ts], 1)

    def apply(v, spectrum):
        e = dot(dot(rising(v), across[...]) * spectrum, back[...])
        er, ei = e[:, :LANES], e[:, LANES:]
        tc, ts = twists[0], twists[1]
        return dot(backward[...], jnp.concatenate([er * tc - ei * ts, ei * tc + er * ts], 0))

    whole = lag_recv[...].reshape(2 * HALF, LANES)
    ids = [lax.broadcasted_iota(jnp.int32, (2 * HALF, LANES), d) for d in range(2)]
    head = (ids[0] == 0) & (ids[1] == 0)
    whole = jnp.where(head, 0.5 * whole, whole)
    half_spectrum = dot(rising(whole), across[:, :LANES]) * (2.0 / PADDED)
    spectrum = jnp.concatenate([half_spectrum, half_spectrum], 1)

    @pl.when(active)
    def _():
        wait(recv_sems, COLS, col_recv.at[pl.ds(0, N_LAG - 1)])

    column = jnp.where(active, col_recv[...].reshape(2 * HALF, LANES), 0.0)
    for sweep in range(ITERS):
        column = apply(column, spectrum)
        image_send[sweep] = column
        slot = image_all.at[sweep, block * OWN + own_col]

        @pl.when(active)
        def _():
            to_lags(IMAGE + 4 * sweep, lambda p: image_send.at[sweep, rows_of(p)], slot)
            image_all[sweep, block * OWN + own_col] = image_send[sweep, rows_of(me), :]

    def gathered(sweep):
        group = image_all.at[sweep, pl.ds(block * OWN, OWN)]

        @pl.when(active)
        def _():
            wait(recv_sems, IMAGE + 4 * sweep, image_all.at[sweep, pl.ds(0, OWN - 1)])

        @pl.when(jnp.logical_not(active))
        def _():
            wait(recv_sems, IMAGE + 4 * sweep, image_all.at[sweep, pl.ds(0, OWN)])

        to_snaps(IMAGE_ALL + 4 * sweep, group, group)
        wait(recv_sems, IMAGE_ALL + 4 * sweep, image_all.at[sweep, pl.ds(0, COLUMNS - OWN)])
        return jnp.concatenate([image_all[sweep, :, i, :] for i in range(2 * PER)], 1)

    def orthonormal(sweep, mapped):
        partial = dot_nt(mapped, mapped) * (1.0 / LAGS)
        gram_send[sweep, :, :COLUMNS] = partial
        gram_send[sweep, :, COLUMNS:] = jnp.zeros((COLUMNS, LANES - COLUMNS), F32)
        to_owners(GRAM + 4 * sweep, lambda j: gram_send.at[sweep, rows_of(j)], gram_recv.at[sweep, me])

        @pl.when(active)
        def _():
            gram_recv[sweep, me] = gram_send[sweep, rows_of(own_col), :]
            wait(recv_sems, GRAM + 4 * sweep, gram_recv.at[sweep, pl.ds(0, N_LAG - 1)])
            tile_send[sweep] = jnp.sum(gram_recv[sweep], axis=0)
            gram_all[sweep, own_col] = tile_send[sweep]
            to_lags(GRAM_ALL + 4 * sweep, lambda p: tile_send.at[sweep], gram_all.at[sweep, own_col])
            wait(recv_sems, GRAM_ALL + 4 * sweep, gram_all.at[sweep, pl.ds(0, OWN - 1)])

        @pl.when(jnp.logical_not(active))
        def _():
            wait(recv_sems, GRAM_ALL + 4 * sweep, gram_all.at[sweep, pl.ds(0, OWN)])

        inverse = inverse_factor(gram_all[sweep].reshape(COLUMNS, LANES))
        return inverse[:, :COLUMNS]

    inverse = orthonormal(0, gathered(0))
    mapped = dot(inverse, gathered(1))
    result = dot(orthonormal(1, mapped), mapped)
    for c in range(2):
        sub_out[c] = result[:, c * PER * LANES : (c + 1) * PER * LANES]

    wait(send_sems, SNAPS, snap_recv.at[pl.ds(0, N_LAG - 1)])
    wait(send_sems, CORR, corr_recv.at[pl.ds(0, N_LAG - 1)])
    wait(send_sems, CORR_ALL, row_recv.at[pl.ds(0, N_SNAP - 1)])
    wait(send_sems, BINS, bin_recv.at[pl.ds(0, N_LAG - 1)])
    wait(send_sems, LAGCORR, lag_recv.at[pl.ds(0, N_LAG - 1)])

    @pl.when(active)
    def _():
        wait(send_sems, COLS, col_recv.at[pl.ds(0, OWN - 1)])
        for sweep in range(ITERS):
            wait(send_sems, IMAGE + 4 * sweep, image_send.at[sweep, pl.ds(0, 2 * HALF - 8)])
            wait(send_sems, GRAM + 4 * sweep, gram_recv.at[sweep, pl.ds(0, OWN - 1)])
            wait(send_sems, GRAM_ALL + 4 * sweep, gram_recv.at[sweep, pl.ds(0, N_LAG - 1)])

    @pl.when(jnp.logical_not(active))
    def _():
        wait(send_sems, COLS, col_recv.at[pl.ds(0, OWN)])
        for sweep in range(ITERS):
            wait(send_sems, GRAM + 4 * sweep, gram_recv.at[sweep, pl.ds(0, OWN)])

    for sweep in range(ITERS):
        wait(send_sems, IMAGE_ALL + 4 * sweep, image_all.at[sweep, pl.ds(0, COLUMNS - OWN)])


def on_device(snapshots, positions, counts, initial):
    snaps = jnp.transpose(snapshots, (0, 2, 1))
    start = lax.axis_index("snap") * OWN
    own = lax.dynamic_slice_in_dim(initial, start, OWN, 1)
    own = jnp.transpose(own.reshape(2, OWN, PER, LANES), (1, 0, 2, 3)).reshape(OWN, 2 * PER, LANES)
    vmem = pl.BlockSpec(memory_space=pltpu.VMEM)
    tile = (2 * PER, LANES)
    return pl.pallas_call(
        kernel,
        out_shape=(
            jax.ShapeDtypeStruct((2, PER * LANES), F32),
            jax.ShapeDtypeStruct((2, COLUMNS, PER * LANES), F32),
        ),
        in_specs=[pl.BlockSpec(memory_space=pltpu.SMEM)] + [vmem] * 8,
        out_specs=(vmem, vmem),
        scratch_shapes=[
            pltpu.VMEM((2, 8, ROWS), BF16),
            pltpu.VMEM((N_LAG, 2, 8, LANES), BF16),
            pltpu.VMEM((SENSORS, SENSORS), F32),
            pltpu.VMEM((N_LAG, 8, SENSORS), F32),
            pltpu.VMEM((8, SENSORS + LANES), F32),
            pltpu.VMEM((N_SNAP, 8, SENSORS + LANES), F32),
            pltpu.VMEM((2 * HALF, 2 * LANES), F32),
            pltpu.VMEM((N_LAG, 8, 2 * LANES), F32),
            pltpu.VMEM(tile, F32),
            pltpu.VMEM((N_LAG, *tile), F32),
            pltpu.VMEM((N_LAG, *tile), F32),
            pltpu.VMEM((ITERS, 2 * HALF, LANES), F32),
            pltpu.VMEM((ITERS, COLUMNS, *tile), F32),
            pltpu.VMEM((ITERS, COLUMNS, LANES), F32),
            pltpu.VMEM((ITERS, N_LAG, *tile), F32),
            pltpu.VMEM((ITERS, *tile), F32),
            pltpu.VMEM((ITERS, OWN, *tile), F32),
            pltpu.SemaphoreType.DMA((PHASES,)),
            pltpu.SemaphoreType.DMA((PHASES,)),
        ],
        compiler_params=pltpu.CompilerParams(
            collective_id=0, has_side_effects=True, vmem_limit_bytes=48 << 20
        ),
        name="coarray_subspace",
    )(counts, positions.reshape(1, SENSORS), snaps, own, *(jnp.asarray(t) for t in tables()))


def solution(mesh):
    return jax.shard_map(
        on_device,
        mesh=mesh,
        in_specs=(P(None, "snap", "lag"), P(None), P("snap"), P(None, None, "lag")),
        out_specs=(P(None, "lag"), P(None, None, "lag")),
        check_vma=False,
    )
```

```python
import functools
import math

import jax
import jax.numpy as jnp
import numpy as np
from jax import lax
from jax.experimental import pallas as pl
from jax.experimental.pallas import tpu as pltpu
from jax.sharding import PartitionSpec as P

MESH = pl.DeviceIdType.MESH
F32 = jnp.float32
BF16 = jnp.bfloat16
ITERS = 2
SENSORS = 256
LAGS = 16384
ROWS = 4096
COLUMNS = 96
N_SNAP = 8
LAG_Z, LAG_Y = 8, 4
N_LAG = LAG_Z * LAG_Y
OWN = COLUMNS // N_SNAP
LANES = 128
PADDED = 2 * LAGS
FIRST = PADDED // LANES
HALF = LAGS // LANES
PER = HALF // N_LAG

SNAPS, CORR, CORR_ALL, BINS, LAGCORR, COLS, COUNTS, LIVE = range(8)
IMAGE, IMAGE_ALL, GRAM, GRAM_ALL = range(8, 12)
PHASES = 8 + 4 * ITERS
BLOCK = 4


def tables():
    rows = np.arange(2 * HALF)
    owner, part, place = rows // (2 * PER), rows // PER % 2, rows % PER
    lag_row = owner * PER + place
    first = np.arange(FIRST)
    lane = np.arange(LANES)
    turn = 2.0 * math.pi * (np.outer(first, lag_row) % FIRST) / FIRST
    cosine, sine = np.cos(turn), np.sin(turn)
    real = part[None, :] == 0
    forward = np.concatenate([np.where(real, cosine, sine), np.where(real, -sine, cosine)], 0)
    backward = np.concatenate(
        [np.where(real, cosine, sine).T, np.where(real, -sine, cosine).T], 1
    )
    small = 2.0 * math.pi * (np.outer(lane, lane) % LANES) / LANES
    c, s = np.cos(small), np.sin(small)
    across = np.block([[c, -s], [s, c]])
    back = np.block([[c, s], [-s, c]])
    twist = 2.0 * math.pi * np.outer(first, lane) / PADDED
    twists = np.stack([np.cos(twist), np.sin(twist)])
    return tuple(t.astype(np.float32) for t in (forward, across, back, backward, twists))


def dot(a, b, precision=lax.Precision.HIGHEST):
    return lax.dot_general(a, b, (((1,), (0,)), ((), ())), precision=precision, preferred_element_type=F32)


def dot_nt(a, b, precision=lax.Precision.HIGHEST):
    return lax.dot_general(a, b, (((1,), (1,)), ((), ())), precision=precision, preferred_element_type=F32)


def inverse_factor(gram):
    shape = (8, LANES)
    sub = lax.broadcasted_iota(jnp.int32, shape, 0)
    lane = lax.broadcasted_iota(jnp.int32, shape, 1)
    tiles = [gram[8 * t : 8 * t + 8, :] for t in range(COLUMNS // 8)]
    pivots = [jnp.ones(shape, F32) for _ in tiles]

    def spread(x):
        return jnp.broadcast_to(x, shape)

    for start in range(0, COLUMNS, BLOCK):
        t, first = divmod(start, 8)
        own = tiles[t]
        inside = (lane >= start) & (lane < start + BLOCK)
        s = [
            [spread(own[first + k : first + k + 1, start + m : start + m + 1]) for m in range(k + 1)]
            for k in range(BLOCK)
        ]
        rows = []
        for k in range(BLOCK):
            row = jnp.where(inside, 0.0, spread(own[first + k : first + k + 1, :]))
            rows.append(jnp.where(lane == start + k, 1.0, row))
        inverses = []
        for m in range(BLOCK):
            inverses.append(1.0 / s[m][m])
            factors = {k: s[k][m] * inverses[m] for k in range(m + 1, BLOCK)}
            for k in range(m + 1, BLOCK):
                for n in range(m + 1, k + 1):
                    s[k][n] = s[k][n] - factors[k] * s[n][m]
                rows[k] = rows[k] - factors[k] * rows[m]
        for u in range(t, len(tiles)):
            if u == t and first + BLOCK == 8:
                continue
            rest = jnp.where(inside, 0.0, tiles[u])
            cols = [spread(tiles[u][:, start + m : start + m + 1]) for m in range(BLOCK)]
            for m in range(BLOCK):
                multiplier = cols[m] * inverses[m]
                for n in range(m + 1, BLOCK):
                    cols[n] = cols[n] - multiplier * s[n][m]
                rest = rest - multiplier * rows[m]
            tiles[u] = rest
        if first + BLOCK == 8:
            kept = own
        else:
            kept = jnp.where(sub < first, own, tiles[t])
        for k in range(BLOCK):
            kept = jnp.where(sub == first + k, rows[k], kept)
            pivots[t] = jnp.where(sub == first + k, s[k][k], pivots[t])
        tiles[t] = kept
    return jnp.concatenate(
        [
            jnp.where(lane <= 8 * t + sub, tile, 0.0) * (1.0 / jnp.sqrt(pivots[t]))
            for t, tile in enumerate(tiles)
        ],
        0,
    )


def far_first(size):
    return sorted(range(1, size), key=lambda d: -min(d, size - d))


def kernel(
    counts, positions_in, snaps_in, initial_in, forward_in, across_in, back_in, backward_in, twists_in,
    lag_out, sub_out,
    positions, snaps, initial, forward, across, back, backward, twists,
    snap_send, snap_recv, corr_send, corr_recv, row_send, row_recv, bin_send, bin_recv,
    count_send, count_recv, live_send, live_recv, high_hot,
    lag_send, lag_recv, col_send, col_recv, image_send, image_all, gram_send, gram_recv,
    strip_send, gram_all, gram_full,
    send_sems, recv_sems, load_sems,
):
    me, block = lax.axis_index("lag"), lax.axis_index("snap")
    deep, wide = me // LAG_Y, lax.rem(me, LAG_Y)
    mine = (3 * me + 7) // 8
    active = (8 * mine) // 3 == me
    idle = jnp.logical_not(active)
    own_col = jnp.minimum(mine, OWN - 1)
    shifts = [(z, y) for z in range(LAG_Z) for y in range(LAG_Y) if z or y]
    shifts.sort(key=lambda d: -(min(d[0], LAG_Z - d[0]) + min(d[1], LAG_Y - d[1])))

    loads = [
        pltpu.make_async_copy(src, dst, load_sems.at[i])
        for i, (src, dst) in enumerate(
            [
                (snaps_in, snaps), (initial_in, initial), (positions_in, positions), (forward_in, forward),
                (across_in, across), (back_in, back), (backward_in, backward), (twists_in, twists),
            ]
        )
    ]
    for load in loads:
        load.start()

    def all_lags(act):
        for z, y in shifts:
            act(lax.rem(deep + z, LAG_Z) * LAG_Y + lax.rem(wide + y, LAG_Y))

    def all_snaps(act):
        for d in far_first(N_SNAP):
            act(lax.rem(block + d, N_SNAP))

    def send(phase, src, dst, axis, peer):
        pltpu.make_async_remote_copy(
            src_ref=src, dst_ref=dst, send_sem=send_sems.at[phase], recv_sem=recv_sems.at[phase],
            device_id={axis: peer}, device_id_type=MESH,
        ).start()

    def wait(sems, phase, ref):
        pltpu.make_async_copy(ref, ref, sems.at[phase]).wait()

    drains = []

    def drain(phase, ref, senders=None):
        def finish():
            if senders is None:
                wait(send_sems, phase, ref)
            else:
                pl.when(senders)(lambda: wait(send_sems, phase, ref))

        drains.append(finish)

    def to_lags(phase, src_of, dst):
        all_lags(lambda p: send(phase, src_of(p), dst, "lag", p))

    def to_snaps(phase, src, dst):
        all_snaps(lambda p: send(phase, src, dst, "snap", p))

    def rows_of(p):
        return pl.ds(pl.multiple_of(p * 8, 8), 8)

    barrier = pltpu.get_barrier_semaphore()
    all_lags(lambda p: pl.semaphore_signal(barrier, inc=1, device_id={"lag": p}, device_id_type=MESH))
    all_snaps(lambda p: pl.semaphore_signal(barrier, inc=1, device_id={"snap": p}, device_id_type=MESH))

    loads[0].wait()
    live = lax.broadcasted_iota(jnp.int32, (8, ROWS), 1) < counts[0]
    for c in range(2):
        snap_send[c] = jnp.where(live, snaps[c].astype(F32), 0.0).astype(BF16)
    loads[1].wait()
    pair_start = pl.multiple_of((block // 2) * (2 * OWN), 2 * OWN)
    odd = lax.rem(block, 2) == 1
    for c in range(2):
        for r in range(PER):
            pair = initial[c, pl.ds(pair_start, 2 * OWN), r * LANES : (r + 1) * LANES]
            col_send[:, c * PER + r, :] = jnp.where(odd, pair[OWN:], pair[:OWN])
    live_send[...] = jnp.full((8, LANES), counts[0].astype(F32), F32)
    live_recv[block] = live_send[...]
    pl.semaphore_wait(barrier, N_LAG + N_SNAP - 2)

    def snap_piece(p):
        return snap_send.at[:, :, pl.ds(pl.multiple_of(p * LANES, LANES), LANES)]

    to_lags(SNAPS, snap_piece, snap_recv.at[me])
    drain(SNAPS, snap_recv.at[pl.ds(0, N_LAG - 1)])
    snap_recv[me] = snap_send[:, :, pl.ds(pl.multiple_of(me * LANES, LANES), LANES)]
    to_snaps(LIVE, live_send, live_recv.at[block])
    drain(LIVE, live_recv.at[pl.ds(0, N_SNAP - 1)])

    loads[2].wait()
    strip = (8, SENSORS)
    sensor = me * 8 + lax.broadcasted_iota(jnp.int32, strip, 0)
    other = lax.broadcasted_iota(jnp.int32, strip, 1)
    place = jnp.broadcast_to(positions[...], strip).astype(F32)
    own_place = jnp.sum(jnp.where(sensor == other, place, 0.0), axis=1, keepdims=True)
    gap = own_place - place
    lags = jnp.abs(gap).astype(jnp.int32)
    lower = sensor >= other
    high = lags // LANES
    target = (high // PER) * (2 * PER) + jnp.where(lower, 0, PER) + high % PER
    low = lags % LANES
    sign = jnp.where(lower | (gap > 0.0), 1.0, -1.0)
    row_ids = lax.broadcasted_iota(jnp.int32, (2 * HALF, SENSORS), 0)
    lane_ids = lax.broadcasted_iota(jnp.int32, (LANES, SENSORS), 0)
    for r in range(8):
        high_hot[:, r * SENSORS : (r + 1) * SENSORS] = jnp.where(
            row_ids == target[r : r + 1], 1.0, 0.0
        ).astype(BF16)
    hits = jnp.concatenate(
        [jnp.where(lane_ids == low[r : r + 1], 1.0, 0.0).astype(BF16) for r in range(8)], 1
    )
    count_send[...] = dot_nt(high_hot[...], hits, None)
    count_recv[me] = count_send[rows_of(me), :]

    wait(recv_sems, SNAPS, snap_recv.at[pl.ds(0, N_LAG - 1)])
    x = [snap_recv[:, c].astype(F32).reshape(SENSORS, LANES) for c in range(2)]
    left = jnp.concatenate([x[0], x[1]], 1).astype(BF16)
    turned = jnp.concatenate([x[1], -x[0]], 1).astype(BF16)
    real = dot_nt(left, left, None)
    imag = dot_nt(turned, left, None)
    square = (SENSORS, SENSORS)
    below = lax.broadcasted_iota(jnp.int32, square, 0) >= lax.broadcasted_iota(jnp.int32, square, 1)
    corr_send[...] = jnp.where(below, real, imag)
    to_lags(CORR, lambda p: corr_send.at[rows_of(p)], corr_recv.at[me])
    drain(CORR, corr_recv.at[pl.ds(0, N_LAG - 1)])
    corr_recv[me] = corr_send[rows_of(me), :]
    to_lags(COUNTS, lambda p: count_send.at[rows_of(p)], count_recv.at[me])
    drain(COUNTS, count_recv.at[pl.ds(0, N_LAG - 1)])
    for k in range(OWN):
        j = lax.rem(own_col + k, OWN)
        owner = (8 * j) // 3
        pl.when(owner != me)(functools.partial(send, COLS, col_send.at[j], col_recv.at[me], "lag", owner))
    drain(COLS, col_recv.at[pl.ds(0, OWN - 1)], active)
    drain(COLS, col_recv.at[pl.ds(0, OWN)], idle)

    @pl.when(active)
    def _():
        col_recv[me] = col_send[own_col]

    wait(recv_sems, LIVE, live_recv.at[pl.ds(0, N_SNAP - 1)])
    total = jnp.sum(live_recv[...], axis=0)

    wait(recv_sems, CORR, corr_recv.at[pl.ds(0, N_LAG - 1)])
    row_send[...] = jnp.sum(corr_recv[...], axis=0)
    to_snaps(CORR_ALL, row_send, row_recv.at[block])
    drain(CORR_ALL, row_recv.at[pl.ds(0, N_SNAP - 1)])
    row_recv[block] = row_send[...]
    wait(recv_sems, CORR_ALL, row_recv.at[pl.ds(0, N_SNAP - 1)])
    values = jnp.sum(row_recv[...], axis=0) * sign
    part_0 = values.astype(BF16).astype(F32)
    part_1 = (values - part_0).astype(BF16).astype(F32)
    part_2 = values - part_0 - part_1
    low_hot = []
    for r in range(8):
        hit = lane_ids == low[r : r + 1]
        low_hot.append(
            jnp.concatenate(
                [jnp.where(hit, part[r : r + 1], 0.0).astype(BF16) for part in (part_0, part_1, part_2)], 0
            )
        )
    bins = dot_nt(high_hot[...], jnp.concatenate(low_hot, 1), None)
    bin_send[...] = bins[:, :LANES] + bins[:, LANES : 2 * LANES] + bins[:, 2 * LANES :]
    to_lags(BINS, lambda p: bin_send.at[rows_of(p)], bin_recv.at[me])
    drain(BINS, bin_recv.at[pl.ds(0, N_LAG - 1)])
    bin_recv[me] = bin_send[rows_of(me), :]
    wait(recv_sems, COUNTS, count_recv.at[pl.ds(0, N_LAG - 1)])
    divisor = jnp.maximum(jnp.sum(count_recv[...], axis=0), 1.0) * total
    wait(recv_sems, BINS, bin_recv.at[pl.ds(0, N_LAG - 1)])
    lag_corr = jnp.sum(bin_recv[...], axis=0) / divisor
    lag_send[...] = lag_corr
    to_lags(LAGCORR, lambda p: lag_send, lag_recv.at[me])
    drain(LAGCORR, lag_recv.at[pl.ds(0, N_LAG - 1)])
    lag_recv[me] = lag_corr
    for c in range(2):
        for r in range(PER):
            lag_out[c : c + 1, r * LANES : (r + 1) * LANES] = lag_corr[c * PER + r : c * PER + r + 1, :]

    for load in loads[3:]:
        load.wait()

    def rising(v):
        a = dot(forward[...], v)
        ar, ai = a[:FIRST], a[FIRST:]
        tc, ts = twists[0], twists[1]
        return jnp.concatenate([ar * tc + ai * ts, ai * tc - ar * ts], 1)

    def apply(v, spectrum):
        e = dot(dot(rising(v), across[...]) * spectrum, back[...])
        er, ei = e[:, :LANES], e[:, LANES:]
        tc, ts = twists[0], twists[1]
        return dot(backward[...], jnp.concatenate([er * tc - ei * ts, ei * tc + er * ts], 0))

    pl.when(active)(lambda: wait(recv_sems, COLS, col_recv.at[pl.ds(0, N_LAG - 1)]))
    column = jnp.where(active, col_recv[...].reshape(2 * HALF, LANES), 0.0)

    wait(recv_sems, LAGCORR, lag_recv.at[pl.ds(0, N_LAG - 1)])
    whole = lag_recv[...].reshape(2 * HALF, LANES)
    ids = [lax.broadcasted_iota(jnp.int32, (2 * HALF, LANES), d) for d in range(2)]
    whole = jnp.where((ids[0] == 0) & (ids[1] == 0), 0.5 * whole, whole)
    half_spectrum = dot(rising(whole), across[:, :LANES]) * (2.0 / PADDED)
    spectrum = jnp.concatenate([half_spectrum, half_spectrum], 1)

    for sweep in range(ITERS):
        if sweep:
            spectrum = spectrum * (1.0 / (jnp.max(jnp.abs(half_spectrum), keepdims=True) * PADDED))
        column = apply(column, spectrum)
        image_send[sweep] = column
        slot = image_all.at[sweep, block * OWN + own_col]

        @pl.when(active)
        def _():
            to_lags(IMAGE + 4 * sweep, lambda p: image_send.at[sweep, rows_of(p)], slot)
            image_all[sweep, block * OWN + own_col] = image_send[sweep, rows_of(me), :]

        drain(IMAGE + 4 * sweep, image_send.at[sweep, pl.ds(0, 2 * HALF - 8)], active)

    for sweep in range(ITERS):
        group = image_all.at[sweep, pl.ds(block * OWN, OWN)]
        some, every = (image_all.at[sweep, pl.ds(0, n)] for n in (OWN - 1, OWN))
        pl.when(active)(functools.partial(wait, recv_sems, IMAGE + 4 * sweep, some))
        pl.when(idle)(functools.partial(wait, recv_sems, IMAGE + 4 * sweep, every))
        to_snaps(IMAGE_ALL + 4 * sweep, group, group)
        drain(IMAGE_ALL + 4 * sweep, image_all.at[sweep, pl.ds(0, COLUMNS - OWN)])

    images = []
    for sweep in range(ITERS):
        wait(recv_sems, IMAGE_ALL + 4 * sweep, image_all.at[sweep, pl.ds(0, COLUMNS - OWN)])
        image = jnp.concatenate([image_all[sweep, :, i, :] for i in range(2 * PER)], 1)
        own = jnp.concatenate(
            [image_all[sweep, pl.ds(block * OWN, OWN), i, :] for i in range(2 * PER)], 1
        )
        images.append(image)
        gram_send[sweep, :, :COLUMNS] = dot_nt(own, image) * (1.0 / LAGS)
        gram_send[sweep, :, COLUMNS:] = jnp.zeros((OWN, LANES - COLUMNS), F32)
        to_lags(GRAM + 4 * sweep, lambda p: gram_send.at[sweep], gram_recv.at[sweep, me])
        drain(GRAM + 4 * sweep, gram_recv.at[sweep, pl.ds(0, N_LAG - 1)])
        gram_recv[sweep, me] = gram_send[sweep]

    for sweep in range(ITERS):
        wait(recv_sems, GRAM + 4 * sweep, gram_recv.at[sweep, pl.ds(0, N_LAG - 1)])
        strip_send[sweep] = jnp.sum(gram_recv[sweep], axis=0)
        to_snaps(GRAM_ALL + 4 * sweep, strip_send.at[sweep], gram_all.at[sweep, block])
        drain(GRAM_ALL + 4 * sweep, gram_all.at[sweep, pl.ds(0, N_SNAP - 1)])
        gram_all[sweep, block] = strip_send[sweep]

    def whole_gram(sweep):
        wait(recv_sems, GRAM_ALL + 4 * sweep, gram_all.at[sweep, pl.ds(0, N_SNAP - 1)])
        for s in range(N_SNAP):
            gram_full[sweep, s * OWN : (s + 1) * OWN, :] = gram_all[sweep, s]
        return gram_full[sweep]

    inverse = inverse_factor(whole_gram(0))[:, :COLUMNS]
    mapped = dot(inverse, images[1])
    gram = dot_nt(dot(inverse, whole_gram(1)[:, :COLUMNS]), inverse)
    gram = jnp.concatenate([gram, jnp.zeros((COLUMNS, LANES - COLUMNS), F32)], 1)
    result = dot(inverse_factor(gram)[:, :COLUMNS], mapped)
    for c in range(2):
        sub_out[c] = result[:, c * PER * LANES : (c + 1) * PER * LANES]

    for finish in drains:
        finish()


def on_device(snapshots, positions, counts, initial):
    constants = [jnp.asarray(t) for t in tables()]
    operands = (positions.reshape(1, SENSORS), jnp.transpose(snapshots, (0, 2, 1)), initial, *constants)
    vmem = pl.BlockSpec(memory_space=pltpu.VMEM)
    tile = (2 * PER, LANES)
    return pl.pallas_call(
        kernel,
        out_shape=(
            jax.ShapeDtypeStruct((2, PER * LANES), F32),
            jax.ShapeDtypeStruct((2, COLUMNS, PER * LANES), F32),
        ),
        in_specs=[pl.BlockSpec(memory_space=pltpu.SMEM)]
        + [pl.BlockSpec(memory_space=pltpu.HBM)] * len(operands),
        out_specs=(vmem, vmem),
        scratch_shapes=[pltpu.VMEM(a.shape, a.dtype) for a in operands]
        + [
            pltpu.VMEM((2, 8, ROWS), BF16),
            pltpu.VMEM((N_LAG, 2, 8, LANES), BF16),
            pltpu.VMEM((SENSORS, SENSORS), F32),
            pltpu.VMEM((N_LAG, 8, SENSORS), F32),
            pltpu.VMEM((8, SENSORS), F32),
            pltpu.VMEM((N_SNAP, 8, SENSORS), F32),
            pltpu.VMEM((2 * HALF, LANES), F32),
            pltpu.VMEM((N_LAG, *tile), F32),
            pltpu.VMEM((2 * HALF, LANES), F32),
            pltpu.VMEM((N_LAG, *tile), F32),
            pltpu.VMEM((8, LANES), F32),
            pltpu.VMEM((N_SNAP, 8, LANES), F32),
            pltpu.VMEM((2 * HALF, 8 * SENSORS), BF16),
            pltpu.VMEM(tile, F32),
            pltpu.VMEM((N_LAG, *tile), F32),
            pltpu.VMEM((OWN, *tile), F32),
            pltpu.VMEM((N_LAG, *tile), F32),
            pltpu.VMEM((ITERS, 2 * HALF, LANES), F32),
            pltpu.VMEM((ITERS, COLUMNS, *tile), F32),
            pltpu.VMEM((ITERS, OWN, LANES), F32),
            pltpu.VMEM((ITERS, N_LAG, OWN, LANES), F32),
            pltpu.VMEM((ITERS, OWN, LANES), F32),
            pltpu.VMEM((ITERS, N_SNAP, OWN, LANES), F32),
            pltpu.VMEM((ITERS, COLUMNS, LANES), F32),
            pltpu.SemaphoreType.DMA((PHASES,)),
            pltpu.SemaphoreType.DMA((PHASES,)),
            pltpu.SemaphoreType.DMA((len(operands),)),
        ],
        compiler_params=pltpu.CompilerParams(
            collective_id=0, has_side_effects=True, vmem_limit_bytes=48 << 20
        ),
        name="coarray_subspace",
    )(counts, *operands)


def solution(mesh):
    return jax.shard_map(
        on_device,
        mesh=mesh,
        in_specs=(P(None, "snap", "lag"), P(None), P("snap"), P(None, None, "lag")),
        out_specs=(P(None, "lag"), P(None, None, "lag")),
        check_vma=False,
    )
```

```python
import functools
import math

import jax
import jax.numpy as jnp
import ml_dtypes
import numpy as np
from jax import lax
from jax.experimental import pallas as pl
from jax.experimental.pallas import tpu as pltpu
from jax.sharding import PartitionSpec as P

MESH = pl.DeviceIdType.MESH
F32 = jnp.float32
BF16 = jnp.bfloat16
ITERS = 2
SENSORS = 256
LAGS = 16384
ROWS = 4096
COLUMNS = 96
N_SNAP = 8
LAG_Z, LAG_Y = 8, 4
N_LAG = LAG_Z * LAG_Y
OWN = COLUMNS // N_SNAP
LANES = 128
PADDED = 2 * LAGS
FIRST = PADDED // LANES
HALF = LAGS // LANES
PER = HALF // N_LAG

SNAPS, CORR, CORR_ALL, BINS, LAGCORR, COLS, COUNTS, LIVE = range(8)
IMAGE, IMAGE_ALL, GRAM, GRAM_ALL = range(8, 12)
PHASES = 8 + 4 * ITERS
BLOCK = 4
PARTS = 3


def tables():
    rows = np.arange(2 * HALF)
    owner, part, place = rows // (2 * PER), rows // PER % 2, rows % PER
    lag_row = owner * PER + place
    first = np.arange(FIRST)
    lane = np.arange(LANES)
    turn = 2.0 * math.pi * (np.outer(first, lag_row) % FIRST) / FIRST
    cosine, sine = np.cos(turn), np.sin(turn)
    real = part[None, :] == 0
    forward = np.concatenate([np.where(real, cosine, sine), np.where(real, -sine, cosine)], 0)
    backward = np.concatenate(
        [np.where(real, cosine, sine).T, np.where(real, -sine, cosine).T], 1
    )
    small = 2.0 * math.pi * (np.outer(lane, lane) % LANES) / LANES
    c, s = np.cos(small), np.sin(small)
    across = np.block([[c, -s], [s, c]])
    back = np.block([[c, s], [-s, c]])
    twist = 2.0 * math.pi * np.outer(first, lane) / PADDED
    twists = np.stack([np.cos(twist), np.sin(twist)])
    split = []
    for table in (forward, across, back, backward):
        parts = []
        for _ in range(PARTS):
            parts.append(table.astype(ml_dtypes.bfloat16))
            table = table - parts[-1].astype(np.float64)
        split.append(np.stack(parts))
    return (*split, twists.astype(np.float32))


def dot(a, b, precision=lax.Precision.HIGHEST):
    return lax.dot_general(a, b, (((1,), (0,)), ((), ())), precision=precision, preferred_element_type=F32)


def dot_nt(a, b, precision=lax.Precision.HIGHEST):
    return lax.dot_general(a, b, (((1,), (1,)), ((), ())), precision=precision, preferred_element_type=F32)


def parts_of(x):
    parts = []
    for _ in range(PARTS):
        parts.append(x.astype(BF16))
        x = x - parts[-1].astype(F32)
    return parts


def table_dot(table, x):
    p = parts_of(x)
    pair = jnp.concatenate(p[:2], 1)
    top = dot(table[0], pair, None)
    if PARTS == 2:
        return top[:, :LANES] + (top[:, LANES:] + dot(table[1], p[0], None))
    low = dot(table[1], pair, None)
    last = dot(table[0], p[2], None) + dot(table[2], p[0], None)
    return top[:, :LANES] + ((top[:, LANES:] + low[:, :LANES]) + (low[:, LANES:] + last))


def dot_table(x, table):
    p = parts_of(x)
    pairs = [(i, k - i) for k in reversed(range(PARTS)) for i in range(k + 1)]
    return functools.reduce(jnp.add, [dot(p[i], table[j], None) for i, j in pairs])


def inverse_factor(gram):
    shape = (8, LANES)
    sub = lax.broadcasted_iota(jnp.int32, shape, 0)
    lane = lax.broadcasted_iota(jnp.int32, shape, 1)
    tiles = [gram[8 * t : 8 * t + 8, :] for t in range(COLUMNS // 8)]
    pivots = [jnp.ones(shape, F32) for _ in tiles]

    def spread(x):
        return jnp.broadcast_to(x, shape)

    for start in range(0, COLUMNS, BLOCK):
        t, first = divmod(start, 8)
        own = tiles[t]
        inside = (lane >= start) & (lane < start + BLOCK)
        s = [
            [spread(own[first + k : first + k + 1, start + m : start + m + 1]) for m in range(k + 1)]
            for k in range(BLOCK)
        ]
        rows = []
        for k in range(BLOCK):
            row = jnp.where(inside, 0.0, spread(own[first + k : first + k + 1, :]))
            rows.append(jnp.where(lane == start + k, 1.0, row))
        inverses = []
        for m in range(BLOCK):
            inverses.append(1.0 / s[m][m])
            factors = {k: s[k][m] * inverses[m] for k in range(m + 1, BLOCK)}
            for k in range(m + 1, BLOCK):
                for n in range(m + 1, k + 1):
                    s[k][n] = s[k][n] - factors[k] * s[n][m]
                rows[k] = rows[k] - factors[k] * rows[m]
        for u in range(t, len(tiles)):
            if u == t and first + BLOCK == 8:
                continue
            rest = jnp.where(inside, 0.0, tiles[u])
            cols = [spread(tiles[u][:, start + m : start + m + 1]) for m in range(BLOCK)]
            for m in range(BLOCK):
                multiplier = cols[m] * inverses[m]
                for n in range(m + 1, BLOCK):
                    cols[n] = cols[n] - multiplier * s[n][m]
                rest = rest - multiplier * rows[m]
            tiles[u] = rest
        if first + BLOCK == 8:
            kept = own
        else:
            kept = jnp.where(sub < first, own, tiles[t])
        for k in range(BLOCK):
            kept = jnp.where(sub == first + k, rows[k], kept)
            pivots[t] = jnp.where(sub == first + k, s[k][k], pivots[t])
        tiles[t] = kept
    return jnp.concatenate(
        [
            jnp.where(lane <= 8 * t + sub, tile, 0.0) * (1.0 / jnp.sqrt(pivots[t]))
            for t, tile in enumerate(tiles)
        ],
        0,
    )


def far_first(size):
    return sorted(range(1, size), key=lambda d: -min(d, size - d))


def kernel(
    counts, positions_in, snaps_in, initial_in, forward_in, across_in, back_in, backward_in, twists_in,
    lag_out, sub_out,
    positions, snaps, initial, forward, across, back, backward, twists,
    snap_send, snap_recv, corr_send, corr_recv, row_send, row_recv, bin_send, bin_recv,
    count_send, count_recv, live_send, live_recv, high_hot,
    lag_send, lag_recv, col_send, col_recv, image_send, image_all, gram_send, gram_recv,
    strip_send, gram_all, gram_full,
    send_sems, recv_sems, load_sems,
):
    me, block = lax.axis_index("lag"), lax.axis_index("snap")
    deep, wide = me // LAG_Y, lax.rem(me, LAG_Y)
    mine = (3 * me + 7) // 8
    active = (8 * mine) // 3 == me
    idle = jnp.logical_not(active)
    own_col = jnp.minimum(mine, OWN - 1)
    shifts = [(z, y) for z in range(LAG_Z) for y in range(LAG_Y) if z or y]
    shifts.sort(key=lambda d: -(min(d[0], LAG_Z - d[0]) + min(d[1], LAG_Y - d[1])))

    loads = [
        pltpu.make_async_copy(src, dst, load_sems.at[i])
        for i, (src, dst) in enumerate(
            [
                (snaps_in, snaps), (initial_in, initial), (positions_in, positions), (forward_in, forward),
                (across_in, across), (back_in, back), (backward_in, backward), (twists_in, twists),
            ]
        )
    ]
    for load in loads:
        load.start()

    def all_lags(act):
        for z, y in shifts:
            act(lax.rem(deep + z, LAG_Z) * LAG_Y + lax.rem(wide + y, LAG_Y))

    def all_snaps(act):
        for d in far_first(N_SNAP):
            act(lax.rem(block + d, N_SNAP))

    def send(phase, src, dst, axis, peer):
        pltpu.make_async_remote_copy(
            src_ref=src, dst_ref=dst, send_sem=send_sems.at[phase], recv_sem=recv_sems.at[phase],
            device_id={axis: peer}, device_id_type=MESH,
        ).start()

    def wait(sems, phase, ref):
        pltpu.make_async_copy(ref, ref, sems.at[phase]).wait()

    drains = []

    def drain(phase, ref, senders=None):
        def finish():
            if senders is None:
                wait(send_sems, phase, ref)
            else:
                pl.when(senders)(lambda: wait(send_sems, phase, ref))

        drains.append(finish)

    def to_lags(phase, src_of, dst):
        all_lags(lambda p: send(phase, src_of(p), dst, "lag", p))

    def to_snaps(phase, src, dst):
        all_snaps(lambda p: send(phase, src, dst, "snap", p))

    def rows_of(p):
        return pl.ds(pl.multiple_of(p * 8, 8), 8)

    barrier = pltpu.get_barrier_semaphore()
    all_lags(lambda p: pl.semaphore_signal(barrier, inc=1, device_id={"lag": p}, device_id_type=MESH))
    all_snaps(lambda p: pl.semaphore_signal(barrier, inc=1, device_id={"snap": p}, device_id_type=MESH))

    loads[0].wait()
    live = lax.broadcasted_iota(jnp.int32, (8, ROWS), 1) < counts[0]
    for c in range(2):
        snap_send[c] = jnp.where(live, snaps[c].astype(F32), 0.0).astype(BF16)
    loads[1].wait()
    pair_start = pl.multiple_of((block // 2) * (2 * OWN), 2 * OWN)
    odd = lax.rem(block, 2) == 1
    for c in range(2):
        for r in range(PER):
            pair = initial[c, pl.ds(pair_start, 2 * OWN), r * LANES : (r + 1) * LANES]
            col_send[:, c * PER + r, :] = jnp.where(odd, pair[OWN:], pair[:OWN])
    live_send[...] = jnp.full((8, LANES), counts[0].astype(F32), F32)
    live_recv[block] = live_send[...]
    pl.semaphore_wait(barrier, N_LAG + N_SNAP - 2)

    def snap_piece(p):
        return snap_send.at[:, :, pl.ds(pl.multiple_of(p * LANES, LANES), LANES)]

    to_lags(SNAPS, snap_piece, snap_recv.at[me])
    drain(SNAPS, snap_recv.at[pl.ds(0, N_LAG - 1)])
    snap_recv[me] = snap_send[:, :, pl.ds(pl.multiple_of(me * LANES, LANES), LANES)]
    to_snaps(LIVE, live_send, live_recv.at[block])
    drain(LIVE, live_recv.at[pl.ds(0, N_SNAP - 1)])

    loads[2].wait()
    strip = (8, SENSORS)
    sensor = me * 8 + lax.broadcasted_iota(jnp.int32, strip, 0)
    other = lax.broadcasted_iota(jnp.int32, strip, 1)
    place = jnp.broadcast_to(positions[...], strip).astype(F32)
    own_place = jnp.sum(jnp.where(sensor == other, place, 0.0), axis=1, keepdims=True)
    gap = own_place - place
    lags = jnp.abs(gap).astype(jnp.int32)
    lower = sensor >= other
    high = lags // LANES
    target = (high // PER) * (2 * PER) + jnp.where(lower, 0, PER) + high % PER
    low = lags % LANES
    sign = jnp.where(lower | (gap > 0.0), 1.0, -1.0)
    row_ids = lax.broadcasted_iota(jnp.int32, (2 * HALF, SENSORS), 0)
    lane_ids = lax.broadcasted_iota(jnp.int32, (LANES, SENSORS), 0)
    for r in range(8):
        high_hot[:, r * SENSORS : (r + 1) * SENSORS] = jnp.where(
            row_ids == target[r : r + 1], 1.0, 0.0
        ).astype(BF16)
    hits = jnp.concatenate(
        [jnp.where(lane_ids == low[r : r + 1], 1.0, 0.0).astype(BF16) for r in range(8)], 1
    )
    count_send[...] = dot_nt(high_hot[...], hits, None)
    to_lags(COUNTS, lambda p: count_send.at[rows_of(p)], count_recv.at[me])
    drain(COUNTS, count_recv.at[pl.ds(0, N_LAG - 1)])
    count_recv[me] = count_send[rows_of(me), :]

    wait(recv_sems, SNAPS, snap_recv.at[pl.ds(0, N_LAG - 1)])
    x = [snap_recv[:, c].astype(F32).reshape(SENSORS, LANES) for c in range(2)]
    left = jnp.concatenate([x[0], x[1]], 1).astype(BF16)
    turned = jnp.concatenate([x[1], -x[0]], 1).astype(BF16)
    real = dot_nt(left, left, None)
    imag = dot_nt(turned, left, None)
    square = (SENSORS, SENSORS)
    below = lax.broadcasted_iota(jnp.int32, square, 0) >= lax.broadcasted_iota(jnp.int32, square, 1)
    corr_send[...] = jnp.where(below, real, imag)
    to_lags(CORR, lambda p: corr_send.at[rows_of(p)], corr_recv.at[me])
    drain(CORR, corr_recv.at[pl.ds(0, N_LAG - 1)])
    corr_recv[me] = corr_send[rows_of(me), :]
    wait(recv_sems, LIVE, live_recv.at[pl.ds(0, N_SNAP - 1)])
    total = jnp.sum(live_recv[...], axis=0)

    wait(recv_sems, CORR, corr_recv.at[pl.ds(0, N_LAG - 1)])
    row_send[...] = jnp.sum(corr_recv[...], axis=0)
    to_snaps(CORR_ALL, row_send, row_recv.at[block])
    drain(CORR_ALL, row_recv.at[pl.ds(0, N_SNAP - 1)])
    row_recv[block] = row_send[...]
    wait(recv_sems, CORR_ALL, row_recv.at[pl.ds(0, N_SNAP - 1)])
    values = jnp.sum(row_recv[...], axis=0) * sign
    part_0 = values.astype(BF16).astype(F32)
    part_1 = (values - part_0).astype(BF16).astype(F32)
    part_2 = values - part_0 - part_1
    low_hot = []
    for r in range(8):
        hit = lane_ids == low[r : r + 1]
        low_hot.append(
            jnp.concatenate(
                [jnp.where(hit, part[r : r + 1], 0.0).astype(BF16) for part in (part_0, part_1, part_2)], 0
            )
        )
    bins = dot_nt(high_hot[...], jnp.concatenate(low_hot, 1), None)
    bin_send[...] = bins[:, :LANES] + bins[:, LANES : 2 * LANES] + bins[:, 2 * LANES :]
    to_lags(BINS, lambda p: bin_send.at[rows_of(p)], bin_recv.at[me])
    drain(BINS, bin_recv.at[pl.ds(0, N_LAG - 1)])
    bin_recv[me] = bin_send[rows_of(me), :]
    for k in range(OWN):
        j = lax.rem(own_col + k, OWN)
        owner = (8 * j) // 3
        pl.when(owner != me)(functools.partial(send, COLS, col_send.at[j], col_recv.at[me], "lag", owner))
    drain(COLS, col_recv.at[pl.ds(0, OWN - 1)], active)
    drain(COLS, col_recv.at[pl.ds(0, OWN)], idle)

    @pl.when(active)
    def _():
        col_recv[me] = col_send[own_col]

    wait(recv_sems, COUNTS, count_recv.at[pl.ds(0, N_LAG - 1)])
    divisor = jnp.maximum(jnp.sum(count_recv[...], axis=0), 1.0) * total
    wait(recv_sems, BINS, bin_recv.at[pl.ds(0, N_LAG - 1)])
    lag_corr = jnp.sum(bin_recv[...], axis=0) / divisor
    lag_send[...] = lag_corr
    to_lags(LAGCORR, lambda p: lag_send, lag_recv.at[me])
    drain(LAGCORR, lag_recv.at[pl.ds(0, N_LAG - 1)])
    lag_recv[me] = lag_corr
    for c in range(2):
        for r in range(PER):
            lag_out[c : c + 1, r * LANES : (r + 1) * LANES] = lag_corr[c * PER + r : c * PER + r + 1, :]

    for load in loads[3:]:
        load.wait()

    def rising(v):
        a = table_dot(forward, v)
        ar, ai = a[:FIRST], a[FIRST:]
        tc, ts = twists[0], twists[1]
        return jnp.concatenate([ar * tc + ai * ts, ai * tc - ar * ts], 1)

    def apply(v, spectrum):
        e = dot_table(dot_table(rising(v), across) * spectrum, back)
        er, ei = e[:, :LANES], e[:, LANES:]
        tc, ts = twists[0], twists[1]
        return table_dot(backward, jnp.concatenate([er * tc - ei * ts, ei * tc + er * ts], 0))

    pl.when(active)(lambda: wait(recv_sems, COLS, col_recv.at[pl.ds(0, N_LAG - 1)]))
    column = jnp.where(active, col_recv[...].reshape(2 * HALF, LANES), 0.0)

    wait(recv_sems, LAGCORR, lag_recv.at[pl.ds(0, N_LAG - 1)])
    whole = lag_recv[...].reshape(2 * HALF, LANES)
    ids = [lax.broadcasted_iota(jnp.int32, (2 * HALF, LANES), d) for d in range(2)]
    whole = jnp.where((ids[0] == 0) & (ids[1] == 0), 0.5 * whole, whole)
    half_spectrum = dot_table(rising(whole), across.at[:, :, :LANES]) * (2.0 / PADDED)
    spectrum = jnp.concatenate([half_spectrum, half_spectrum], 1)

    for sweep in range(ITERS):
        if sweep:
            spectrum = spectrum * (1.0 / (jnp.max(jnp.abs(half_spectrum), keepdims=True) * PADDED))
        column = apply(column, spectrum)
        image_send[sweep] = column
        slot = image_all.at[sweep, block * OWN + own_col]

        @pl.when(active)
        def _():
            to_lags(IMAGE + 4 * sweep, lambda p: image_send.at[sweep, rows_of(p)], slot)
            image_all[sweep, block * OWN + own_col] = image_send[sweep, rows_of(me), :]

        drain(IMAGE + 4 * sweep, image_send.at[sweep, pl.ds(0, 2 * HALF - 8)], active)

    images_in = []
    for sweep in range(ITERS):
        group = image_all.at[sweep, pl.ds(block * OWN, OWN)]
        some, every = (image_all.at[sweep, pl.ds(0, n)] for n in (OWN - 1, OWN))
        pl.when(active)(functools.partial(wait, recv_sems, IMAGE + 4 * sweep, some))
        pl.when(idle)(functools.partial(wait, recv_sems, IMAGE + 4 * sweep, every))
        reach = N_SNAP // 2 if sweep == 0 else N_SNAP - 1
        for d in far_first(N_SNAP):
            if N_SNAP - d <= reach:
                send(IMAGE_ALL + 4 * sweep, group, group, "snap", lax.rem(block + d, N_SNAP))
        images_in.append(image_all.at[sweep, pl.ds(0, reach * OWN)])
        drain(IMAGE_ALL + 4 * sweep, images_in[sweep])

    images = []
    for sweep in range(ITERS):
        wait(recv_sems, IMAGE_ALL + 4 * sweep, images_in[sweep])
        image = jnp.concatenate([image_all[sweep, :, i, :] for i in range(2 * PER)], 1)
        own = jnp.concatenate(
            [image_all[sweep, pl.ds(block * OWN, OWN), i, :] for i in range(2 * PER)], 1
        )
        images.append(image)
        gram_send[sweep, :, :COLUMNS] = dot_nt(own, image) * (1.0 / LAGS)
        gram_send[sweep, :, COLUMNS:] = jnp.zeros((OWN, LANES - COLUMNS), F32)
        to_lags(GRAM + 4 * sweep, lambda p: gram_send.at[sweep], gram_recv.at[sweep, me])
        drain(GRAM + 4 * sweep, gram_recv.at[sweep, pl.ds(0, N_LAG - 1)])
        gram_recv[sweep, me] = gram_send[sweep]

    for sweep in range(ITERS):
        wait(recv_sems, GRAM + 4 * sweep, gram_recv.at[sweep, pl.ds(0, N_LAG - 1)])
        strip_send[sweep] = jnp.sum(gram_recv[sweep], axis=0)
        to_snaps(GRAM_ALL + 4 * sweep, strip_send.at[sweep], gram_all.at[sweep, block])
        drain(GRAM_ALL + 4 * sweep, gram_all.at[sweep, pl.ds(0, N_SNAP - 1)])
        gram_all[sweep, block] = strip_send[sweep]

    def whole_gram(sweep):
        wait(recv_sems, GRAM_ALL + 4 * sweep, gram_all.at[sweep, pl.ds(0, N_SNAP - 1)])
        for s in range(N_SNAP):
            gram_full[sweep, s * OWN : (s + 1) * OWN, :] = gram_all[sweep, s]
        if sweep:
            return gram_full[sweep]
        known, spots = gram_full[sweep], (COLUMNS, LANES)
        row_block = lax.broadcasted_iota(jnp.int32, spots, 0) // OWN
        col_block = lax.broadcasted_iota(jnp.int32, spots, 1) // OWN
        own = (col_block + N_SNAP - row_block) % N_SNAP <= N_SNAP // 2
        square = jnp.concatenate([known, jnp.zeros((LANES - COLUMNS, LANES), F32)], 0)
        return jnp.where(own, known, square.T[:COLUMNS])

    inverse = inverse_factor(whole_gram(0))[:, :COLUMNS]
    mapped = dot(inverse, images[1])
    gram = dot_nt(dot(inverse, whole_gram(1)[:, :COLUMNS]), inverse)
    gram = jnp.concatenate([gram, jnp.zeros((COLUMNS, LANES - COLUMNS), F32)], 1)
    result = dot(inverse_factor(gram)[:, :COLUMNS], mapped)
    for c in range(2):
        sub_out[c] = result[:, c * PER * LANES : (c + 1) * PER * LANES]

    for finish in drains:
        finish()


def on_device(snapshots, positions, counts, initial):
    constants = [jnp.asarray(t) for t in tables()]
    operands = (positions.reshape(1, SENSORS), jnp.transpose(snapshots, (0, 2, 1)), initial, *constants)
    vmem = pl.BlockSpec(memory_space=pltpu.VMEM)
    tile = (2 * PER, LANES)
    return pl.pallas_call(
        kernel,
        out_shape=(
            jax.ShapeDtypeStruct((2, PER * LANES), F32),
            jax.ShapeDtypeStruct((2, COLUMNS, PER * LANES), F32),
        ),
        in_specs=[pl.BlockSpec(memory_space=pltpu.SMEM)]
        + [pl.BlockSpec(memory_space=pltpu.HBM)] * len(operands),
        out_specs=(vmem, vmem),
        scratch_shapes=[pltpu.VMEM(a.shape, a.dtype) for a in operands]
        + [
            pltpu.VMEM((2, 8, ROWS), BF16),
            pltpu.VMEM((N_LAG, 2, 8, LANES), BF16),
            pltpu.VMEM((SENSORS, SENSORS), F32),
            pltpu.VMEM((N_LAG, 8, SENSORS), F32),
            pltpu.VMEM((8, SENSORS), F32),
            pltpu.VMEM((N_SNAP, 8, SENSORS), F32),
            pltpu.VMEM((2 * HALF, LANES), F32),
            pltpu.VMEM((N_LAG, *tile), F32),
            pltpu.VMEM((2 * HALF, LANES), F32),
            pltpu.VMEM((N_LAG, *tile), F32),
            pltpu.VMEM((8, LANES), F32),
            pltpu.VMEM((N_SNAP, 8, LANES), F32),
            pltpu.VMEM((2 * HALF, 8 * SENSORS), BF16),
            pltpu.VMEM(tile, F32),
            pltpu.VMEM((N_LAG, *tile), F32),
            pltpu.VMEM((OWN, *tile), F32),
            pltpu.VMEM((N_LAG, *tile), F32),
            pltpu.VMEM((ITERS, 2 * HALF, LANES), F32),
            pltpu.VMEM((ITERS, COLUMNS, *tile), F32),
            pltpu.VMEM((ITERS, OWN, LANES), F32),
            pltpu.VMEM((ITERS, N_LAG, OWN, LANES), F32),
            pltpu.VMEM((ITERS, OWN, LANES), F32),
            pltpu.VMEM((ITERS, N_SNAP, OWN, LANES), F32),
            pltpu.VMEM((ITERS, COLUMNS, LANES), F32),
            pltpu.SemaphoreType.DMA((PHASES,)),
            pltpu.SemaphoreType.DMA((PHASES,)),
            pltpu.SemaphoreType.DMA((len(operands),)),
        ],
        compiler_params=pltpu.CompilerParams(
            collective_id=0, has_side_effects=True, vmem_limit_bytes=56 << 20
        ),
        name="coarray_subspace",
    )(counts, *operands)


def solution(mesh):
    return jax.shard_map(
        on_device,
        mesh=mesh,
        in_specs=(P(None, "snap", "lag"), P(None), P("snap"), P(None, None, "lag")),
        out_specs=(P(None, "lag"), P(None, None, "lag")),
        check_vma=False,
    )
```

```python
import functools
import math

import jax
import jax.numpy as jnp
import ml_dtypes
import numpy as np
from jax import lax
from jax.experimental import pallas as pl
from jax.experimental.pallas import tpu as pltpu
from jax.sharding import PartitionSpec as P

MESH = pl.DeviceIdType.MESH
F32 = jnp.float32
BF16 = jnp.bfloat16
ITERS = 2
SENSORS = 256
LAGS = 16384
ROWS = 4096
COLUMNS = 96
N_SNAP = 8
LAG_Z, LAG_Y = 8, 4
N_LAG = LAG_Z * LAG_Y
OWN = COLUMNS // N_SNAP
LANES = 128
PADDED = 2 * LAGS
FIRST = PADDED // LANES
HALF = LAGS // LANES
PER = HALF // N_LAG

SNAPS, CORR, CORR_ALL, BINS, LAGCORR, COLS, COUNTS, LIVE = range(8)
IMAGE, IMAGE_ALL, GRAM, GRAM_ALL = range(8, 12)
PHASES = 8 + 4 * ITERS
BLOCK = 8
PARTS = 3


def tables():
    rows = np.arange(2 * HALF)
    owner, part, place = rows // (2 * PER), rows // PER % 2, rows % PER
    lag_row = owner * PER + place
    first = np.arange(FIRST)
    lane = np.arange(LANES)
    turn = 2.0 * math.pi * (np.outer(first, lag_row) % FIRST) / FIRST
    cosine, sine = np.cos(turn), np.sin(turn)
    real = part[None, :] == 0
    forward = np.concatenate([np.where(real, cosine, sine), np.where(real, -sine, cosine)], 0)
    backward = np.concatenate(
        [np.where(real, cosine, sine).T, np.where(real, -sine, cosine).T], 1
    )
    small = 2.0 * math.pi * (np.outer(lane, lane) % LANES) / LANES
    c, s = np.cos(small), np.sin(small)
    across = np.block([[c, -s], [s, c]])
    back = np.block([[c, s], [-s, c]])
    twist = 2.0 * math.pi * np.outer(first, lane) / PADDED
    twists = np.stack([np.cos(twist), np.sin(twist)])
    split = []
    for table in (forward, across, back, backward):
        parts = []
        for _ in range(PARTS):
            parts.append(table.astype(ml_dtypes.bfloat16))
            table = table - parts[-1].astype(np.float64)
        split.append(np.stack(parts))
    return (*split, twists.astype(np.float32))


def dot(a, b, precision=lax.Precision.HIGHEST):
    return lax.dot_general(a, b, (((1,), (0,)), ((), ())), precision=precision, preferred_element_type=F32)


def dot_nt(a, b, precision=lax.Precision.HIGHEST):
    return lax.dot_general(a, b, (((1,), (1,)), ((), ())), precision=precision, preferred_element_type=F32)


def parts_of(x):
    parts = []
    for _ in range(PARTS):
        parts.append(x.astype(BF16))
        x = x - parts[-1].astype(F32)
    return parts


def table_dot(table, x):
    p = parts_of(x)
    pair = jnp.concatenate(p[:2], 1)
    top = dot(table[0], pair, None)
    if PARTS == 2:
        return top[:, :LANES] + (top[:, LANES:] + dot(table[1], p[0], None))
    low = dot(table[1], pair, None)
    last = dot(table[0], p[2], None) + dot(table[2], p[0], None)
    return top[:, :LANES] + ((top[:, LANES:] + low[:, :LANES]) + (low[:, LANES:] + last))


def dot_table(x, table):
    p = parts_of(x)
    pairs = [(i, k - i) for k in reversed(range(PARTS)) for i in range(k + 1)]
    return functools.reduce(jnp.add, [dot(p[i], table[j], None) for i, j in pairs])


def inverse_factor(gram):
    shape = (8, LANES)
    sub = lax.broadcasted_iota(jnp.int32, shape, 0)
    lane = lax.broadcasted_iota(jnp.int32, shape, 1)
    tiles = [gram[8 * t : 8 * t + 8, :] for t in range(COLUMNS // 8)]
    pivots = [jnp.ones(shape, F32) for _ in tiles]

    def spread(x):
        return jnp.broadcast_to(x, shape)

    for t in range(COLUMNS // BLOCK):
        start = BLOCK * t
        own = tiles[t]
        inside = (lane >= start) & (lane < start + BLOCK)
        s = [
            [spread(own[k : k + 1, start + m : start + m + 1]) for m in range(k + 1)] for k in range(BLOCK)
        ]
        rows = []
        for k in range(BLOCK):
            row = jnp.where(inside, 0.0, spread(own[k : k + 1, :]))
            rows.append(jnp.where(lane == start + k, 1.0, row))
        inverses = []
        for m in range(BLOCK):
            inverses.append(1.0 / s[m][m])
            factors = {k: s[k][m] * inverses[m] for k in range(m + 1, BLOCK)}
            for k in range(m + 1, BLOCK):
                for n in range(m + 1, k + 1):
                    s[k][n] = s[k][n] - factors[k] * s[n][m]
                rows[k] = rows[k] - factors[k] * rows[m]
        for u in range(t + 1, len(tiles)):
            rest = jnp.where(inside, 0.0, tiles[u])
            cols = [spread(tiles[u][:, start + m : start + m + 1]) for m in range(BLOCK)]
            for m in range(BLOCK):
                multiplier = cols[m] * inverses[m]
                for n in range(m + 1, BLOCK):
                    cols[n] = cols[n] - multiplier * s[n][m]
                rest = rest - multiplier * rows[m]
            tiles[u] = rest
        for k in range(BLOCK):
            tiles[t] = rows[k] if k == 0 else jnp.where(sub == k, rows[k], tiles[t])
            pivots[t] = jnp.where(sub == k, s[k][k], pivots[t])
    return jnp.concatenate(
        [
            jnp.where(lane <= 8 * t + sub, tile, 0.0) * (1.0 / jnp.sqrt(pivots[t]))
            for t, tile in enumerate(tiles)
        ],
        0,
    )


def far_first(size):
    return sorted(range(1, size), key=lambda d: -min(d, size - d))


def kernel(
    counts, positions_in, snaps_in, initial_in, forward_in, across_in, back_in, backward_in, twists_in,
    lag_out, inverse_out, mapped_out,
    positions, snaps, initial, forward, across, back, backward, twists,
    snap_send, snap_recv, corr_send, corr_recv, row_send, row_recv, bin_send, bin_recv,
    count_send, count_recv, live_send, live_recv, high_hot,
    lag_send, lag_recv, col_send, col_recv, image_send, image_all, gram_send, gram_recv,
    strip_send, gram_all, gram_full,
    send_sems, recv_sems, load_sems,
):
    me, block = lax.axis_index("lag"), lax.axis_index("snap")
    deep, wide = me // LAG_Y, lax.rem(me, LAG_Y)
    mine = (3 * me + 7) // 8
    active = (8 * mine) // 3 == me
    idle = jnp.logical_not(active)
    own_col = jnp.minimum(mine, OWN - 1)
    shifts = [(z, y) for z in range(LAG_Z) for y in range(LAG_Y) if z or y]
    shifts.sort(key=lambda d: -(min(d[0], LAG_Z - d[0]) + min(d[1], LAG_Y - d[1])))

    loads = [
        pltpu.make_async_copy(src, dst, load_sems.at[i])
        for i, (src, dst) in enumerate(
            [
                (snaps_in, snaps), (initial_in, initial), (positions_in, positions), (forward_in, forward),
                (across_in, across), (back_in, back), (backward_in, backward), (twists_in, twists),
            ]
        )
    ]

    def all_lags(act):
        for z, y in shifts:
            act(lax.rem(deep + z, LAG_Z) * LAG_Y + lax.rem(wide + y, LAG_Y))

    def all_snaps(act):
        for d in far_first(N_SNAP):
            act(lax.rem(block + d, N_SNAP))

    def send(phase, src, dst, axis, peer):
        pltpu.make_async_remote_copy(
            src_ref=src, dst_ref=dst, send_sem=send_sems.at[phase], recv_sem=recv_sems.at[phase],
            device_id={axis: peer}, device_id_type=MESH,
        ).start()

    def wait(sems, phase, ref):
        pltpu.make_async_copy(ref, ref, sems.at[phase]).wait()

    drains = []

    def drain(phase, ref, senders=None):
        def finish():
            if senders is None:
                wait(send_sems, phase, ref)
            else:
                pl.when(senders)(lambda: wait(send_sems, phase, ref))

        drains.append(finish)

    def to_lags(phase, src_of, dst):
        all_lags(lambda p: send(phase, src_of(p), dst, "lag", p))

    def to_snaps(phase, src, dst):
        all_snaps(lambda p: send(phase, src, dst, "snap", p))

    def rows_of(p):
        return pl.ds(pl.multiple_of(p * 8, 8), 8)

    barrier = pltpu.get_barrier_semaphore()
    all_lags(lambda p: pl.semaphore_signal(barrier, inc=1, device_id={"lag": p}, device_id_type=MESH))
    all_snaps(lambda p: pl.semaphore_signal(barrier, inc=1, device_id={"snap": p}, device_id_type=MESH))

    for load in loads:
        load.start()

    loads[0].wait()
    live = lax.broadcasted_iota(jnp.int32, (8, ROWS), 1) < counts[0]
    for c in range(2):
        snap_send[c] = jnp.where(live, snaps[c].astype(F32), 0.0).astype(BF16)
    loads[1].wait()
    pair_start = pl.multiple_of((block // 2) * (2 * OWN), 2 * OWN)
    odd = lax.rem(block, 2) == 1
    for c in range(2):
        for r in range(PER):
            pair = initial[c, pl.ds(pair_start, 2 * OWN), r * LANES : (r + 1) * LANES]
            col_send[:, c * PER + r, :] = jnp.where(odd, pair[OWN:], pair[:OWN])
    live_send[...] = jnp.full((8, LANES), counts[0].astype(F32), F32)
    live_recv[block] = live_send[...]
    pl.semaphore_wait(barrier, N_LAG + N_SNAP - 2)

    def snap_piece(p):
        return snap_send.at[:, :, pl.ds(pl.multiple_of(p * LANES, LANES), LANES)]

    to_lags(SNAPS, snap_piece, snap_recv.at[me])
    drain(SNAPS, snap_recv.at[pl.ds(0, N_LAG - 1)])
    snap_recv[me] = snap_send[:, :, pl.ds(pl.multiple_of(me * LANES, LANES), LANES)]
    to_snaps(LIVE, live_send, live_recv.at[block])
    drain(LIVE, live_recv.at[pl.ds(0, N_SNAP - 1)])

    loads[2].wait()
    strip = (8, SENSORS)
    sensor = me * 8 + lax.broadcasted_iota(jnp.int32, strip, 0)
    other = lax.broadcasted_iota(jnp.int32, strip, 1)
    place = jnp.broadcast_to(positions[...], strip).astype(F32)
    own_place = jnp.sum(jnp.where(sensor == other, place, 0.0), axis=1, keepdims=True)
    gap = own_place - place
    lags = jnp.abs(gap).astype(jnp.int32)
    lower = sensor >= other
    high = lags // LANES
    target = (high // PER) * (2 * PER) + jnp.where(lower, 0, PER) + high % PER
    low = lags % LANES
    sign = jnp.where(lower | (gap > 0.0), 1.0, -1.0)
    row_ids = lax.broadcasted_iota(jnp.int32, (2 * HALF, SENSORS), 0)
    lane_ids = lax.broadcasted_iota(jnp.int32, (LANES, SENSORS), 0)
    for r in range(8):
        high_hot[:, r * SENSORS : (r + 1) * SENSORS] = jnp.where(
            row_ids == target[r : r + 1], 1.0, 0.0
        ).astype(BF16)
    hits = jnp.concatenate(
        [jnp.where(lane_ids == low[r : r + 1], 1.0, 0.0).astype(BF16) for r in range(8)], 1
    )
    count_send[...] = dot_nt(high_hot[...], hits, None)
    to_lags(COUNTS, lambda p: count_send.at[rows_of(p)], count_recv.at[me])
    drain(COUNTS, count_recv.at[pl.ds(0, N_LAG - 1)])
    count_recv[me] = count_send[rows_of(me), :]

    wait(recv_sems, SNAPS, snap_recv.at[pl.ds(0, N_LAG - 1)])
    x = [snap_recv[:, c].astype(F32).reshape(SENSORS, LANES) for c in range(2)]
    left = jnp.concatenate([x[0], x[1]], 1).astype(BF16)
    turned = jnp.concatenate([x[1], -x[0]], 1).astype(BF16)
    real = dot_nt(left, left, None)
    imag = dot_nt(turned, left, None)
    square = (SENSORS, SENSORS)
    below = lax.broadcasted_iota(jnp.int32, square, 0) >= lax.broadcasted_iota(jnp.int32, square, 1)
    corr_send[...] = jnp.where(below, real, imag)
    to_lags(CORR, lambda p: corr_send.at[rows_of(p)], corr_recv.at[me])
    drain(CORR, corr_recv.at[pl.ds(0, N_LAG - 1)])
    corr_recv[me] = corr_send[rows_of(me), :]
    wait(recv_sems, LIVE, live_recv.at[pl.ds(0, N_SNAP - 1)])
    total = jnp.sum(live_recv[...], axis=0)

    wait(recv_sems, CORR, corr_recv.at[pl.ds(0, N_LAG - 1)])
    row_send[...] = jnp.sum(corr_recv[...], axis=0)
    to_snaps(CORR_ALL, row_send, row_recv.at[block])
    drain(CORR_ALL, row_recv.at[pl.ds(0, N_SNAP - 1)])
    row_recv[block] = row_send[...]
    wait(recv_sems, CORR_ALL, row_recv.at[pl.ds(0, N_SNAP - 1)])
    values = jnp.sum(row_recv[...], axis=0) * sign
    part_0 = values.astype(BF16).astype(F32)
    part_1 = (values - part_0).astype(BF16).astype(F32)
    part_2 = values - part_0 - part_1
    low_hot = []
    for r in range(8):
        hit = lane_ids == low[r : r + 1]
        low_hot.append(
            jnp.concatenate(
                [jnp.where(hit, part[r : r + 1], 0.0).astype(BF16) for part in (part_0, part_1, part_2)], 0
            )
        )
    bins = dot_nt(high_hot[...], jnp.concatenate(low_hot, 1), None)
    bin_send[...] = bins[:, :LANES] + bins[:, LANES : 2 * LANES] + bins[:, 2 * LANES :]
    to_lags(BINS, lambda p: bin_send.at[rows_of(p)], bin_recv.at[me])
    drain(BINS, bin_recv.at[pl.ds(0, N_LAG - 1)])
    bin_recv[me] = bin_send[rows_of(me), :]
    for k in range(OWN):
        j = lax.rem(own_col + k, OWN)
        owner = (8 * j) // 3
        pl.when(owner != me)(functools.partial(send, COLS, col_send.at[j], col_recv.at[me], "lag", owner))
    drain(COLS, col_recv.at[pl.ds(0, OWN - 1)], active)
    drain(COLS, col_recv.at[pl.ds(0, OWN)], idle)

    @pl.when(active)
    def _():
        col_recv[me] = col_send[own_col]

    wait(recv_sems, COUNTS, count_recv.at[pl.ds(0, N_LAG - 1)])
    divisor = jnp.maximum(jnp.sum(count_recv[...], axis=0), 1.0) * total
    wait(recv_sems, BINS, bin_recv.at[pl.ds(0, N_LAG - 1)])
    lag_corr = jnp.sum(bin_recv[...], axis=0) / divisor
    lag_send[...] = lag_corr
    to_lags(LAGCORR, lambda p: lag_send, lag_recv.at[me])
    drain(LAGCORR, lag_recv.at[pl.ds(0, N_LAG - 1)])
    lag_recv[me] = lag_corr
    lag_out[...] = lag_corr

    for load in loads[3:]:
        load.wait()

    def rising(v):
        a = table_dot(forward, v)
        ar, ai = a[:FIRST], a[FIRST:]
        tc, ts = twists[0], twists[1]
        return jnp.concatenate([ar * tc + ai * ts, ai * tc - ar * ts], 1)

    def apply(v, spectrum):
        e = dot_table(dot_table(rising(v), across) * spectrum, back)
        er, ei = e[:, :LANES], e[:, LANES:]
        tc, ts = twists[0], twists[1]
        return table_dot(backward, jnp.concatenate([er * tc - ei * ts, ei * tc + er * ts], 0))

    pl.when(active)(lambda: wait(recv_sems, COLS, col_recv.at[pl.ds(0, N_LAG - 1)]))
    column = jnp.where(active, col_recv[...].reshape(2 * HALF, LANES), 0.0)

    wait(recv_sems, LAGCORR, lag_recv.at[pl.ds(0, N_LAG - 1)])
    whole = lag_recv[...].reshape(2 * HALF, LANES)
    ids = [lax.broadcasted_iota(jnp.int32, (2 * HALF, LANES), d) for d in range(2)]
    whole = jnp.where((ids[0] == 0) & (ids[1] == 0), 0.5 * whole, whole)
    half_spectrum = dot_table(rising(whole), across.at[:, :, :LANES]) * (2.0 / PADDED)
    spectrum = jnp.concatenate([half_spectrum, half_spectrum], 1)

    for sweep in range(ITERS):
        if sweep:
            spectrum = spectrum * (1.0 / (jnp.max(jnp.abs(half_spectrum), keepdims=True) * PADDED))
        column = apply(column, spectrum)
        image_send[sweep] = column
        slot = image_all.at[sweep, block * OWN + own_col]

        @pl.when(active)
        def _():
            to_lags(IMAGE + 4 * sweep, lambda p: image_send.at[sweep, rows_of(p)], slot)
            image_all[sweep, block * OWN + own_col] = image_send[sweep, rows_of(me), :]

        drain(IMAGE + 4 * sweep, image_send.at[sweep, pl.ds(0, 2 * HALF - 8)], active)

    images_in = []
    for sweep in range(ITERS):
        group = image_all.at[sweep, pl.ds(block * OWN, OWN)]
        some, every = (image_all.at[sweep, pl.ds(0, n)] for n in (OWN - 1, OWN))
        pl.when(active)(functools.partial(wait, recv_sems, IMAGE + 4 * sweep, some))
        pl.when(idle)(functools.partial(wait, recv_sems, IMAGE + 4 * sweep, every))
        reach = N_SNAP // 2 if sweep == 0 else N_SNAP - 1
        for d in far_first(N_SNAP):
            if N_SNAP - d <= reach:
                send(IMAGE_ALL + 4 * sweep, group, group, "snap", lax.rem(block + d, N_SNAP))
        images_in.append(image_all.at[sweep, pl.ds(0, reach * OWN)])
        drain(IMAGE_ALL + 4 * sweep, images_in[sweep])

    images = []
    for sweep in range(ITERS):
        wait(recv_sems, IMAGE_ALL + 4 * sweep, images_in[sweep])
        image = jnp.concatenate([image_all[sweep, :, i, :] for i in range(2 * PER)], 1)
        own = jnp.concatenate(
            [image_all[sweep, pl.ds(block * OWN, OWN), i, :] for i in range(2 * PER)], 1
        )
        images.append(image)
        gram_send[sweep, :, :COLUMNS] = dot_nt(own, image) * (1.0 / LAGS)
        gram_send[sweep, :, COLUMNS:] = jnp.zeros((OWN, LANES - COLUMNS), F32)
        to_lags(GRAM + 4 * sweep, lambda p: gram_send.at[sweep], gram_recv.at[sweep, me])
        drain(GRAM + 4 * sweep, gram_recv.at[sweep, pl.ds(0, N_LAG - 1)])
        gram_recv[sweep, me] = gram_send[sweep]

    for sweep in range(ITERS):
        wait(recv_sems, GRAM + 4 * sweep, gram_recv.at[sweep, pl.ds(0, N_LAG - 1)])
        strip_send[sweep] = jnp.sum(gram_recv[sweep], axis=0)
        to_snaps(GRAM_ALL + 4 * sweep, strip_send.at[sweep], gram_all.at[sweep, block])
        drain(GRAM_ALL + 4 * sweep, gram_all.at[sweep, pl.ds(0, N_SNAP - 1)])
        gram_all[sweep, block] = strip_send[sweep]

    def whole_gram(sweep):
        wait(recv_sems, GRAM_ALL + 4 * sweep, gram_all.at[sweep, pl.ds(0, N_SNAP - 1)])
        for s in range(N_SNAP):
            gram_full[sweep, s * OWN : (s + 1) * OWN, :] = gram_all[sweep, s]
        if sweep:
            return gram_full[sweep]
        known, spots = gram_full[sweep], (COLUMNS, LANES)
        row_block = lax.broadcasted_iota(jnp.int32, spots, 0) // OWN
        col_block = lax.broadcasted_iota(jnp.int32, spots, 1) // OWN
        own = (col_block + N_SNAP - row_block) % N_SNAP <= N_SNAP // 2
        square = jnp.concatenate([known, jnp.zeros((LANES - COLUMNS, LANES), F32)], 0)
        return jnp.where(own, known, square.T[:COLUMNS])

    inverse = inverse_factor(whole_gram(0))[:, :COLUMNS]
    mapped_out[...] = dot(inverse, images[1])
    gram = dot_nt(dot(inverse, whole_gram(1)[:, :COLUMNS]), inverse)
    gram = jnp.concatenate([gram, jnp.zeros((COLUMNS, LANES - COLUMNS), F32)], 1)
    inverse_out[...] = inverse_factor(gram)

    for finish in drains:
        finish()


def combine(lag_corr, inverse, mapped, lag_out, sub_out):
    for c in range(2):
        for r in range(PER):
            row = c * PER + r
            lag_out[c : c + 1, r * LANES : (r + 1) * LANES] = lag_corr[row : row + 1, :]
    result = dot(inverse[:, :COLUMNS], mapped[...])
    for c in range(2):
        sub_out[c] = result[:, c * PER * LANES : (c + 1) * PER * LANES]


def on_device(snapshots, positions, counts, initial):
    constants = [jnp.asarray(t) for t in tables()]
    operands = tuple(pltpu.with_memory_space_constraint(a, pltpu.HBM) for a in (positions.reshape(1, SENSORS), jnp.transpose(snapshots, (0, 2, 1)), initial, *constants))
    vmem = pl.BlockSpec(memory_space=pltpu.VMEM)
    tile = (2 * PER, LANES)
    pieces = pl.pallas_call(
        kernel,
        out_shape=(
            jax.ShapeDtypeStruct(tile, F32),
            jax.ShapeDtypeStruct((COLUMNS, LANES), F32),
            jax.ShapeDtypeStruct((COLUMNS, 2 * PER * LANES), F32),
        ),
        in_specs=[pl.BlockSpec(memory_space=pltpu.SMEM)]
        + [pl.BlockSpec(memory_space=pltpu.HBM)] * len(operands),
        out_specs=(vmem, vmem, vmem),
        scratch_shapes=[pltpu.VMEM(a.shape, a.dtype) for a in operands]
        + [
            pltpu.VMEM((2, 8, ROWS), BF16),
            pltpu.VMEM((N_LAG, 2, 8, LANES), BF16),
            pltpu.VMEM((SENSORS, SENSORS), F32),
            pltpu.VMEM((N_LAG, 8, SENSORS), F32),
            pltpu.VMEM((8, SENSORS), F32),
            pltpu.VMEM((N_SNAP, 8, SENSORS), F32),
            pltpu.VMEM((2 * HALF, LANES), F32),
            pltpu.VMEM((N_LAG, *tile), F32),
            pltpu.VMEM((2 * HALF, LANES), F32),
            pltpu.VMEM((N_LAG, *tile), F32),
            pltpu.VMEM((8, LANES), F32),
            pltpu.VMEM((N_SNAP, 8, LANES), F32),
            pltpu.VMEM((2 * HALF, 8 * SENSORS), BF16),
            pltpu.VMEM(tile, F32),
            pltpu.VMEM((N_LAG, *tile), F32),
            pltpu.VMEM((OWN, *tile), F32),
            pltpu.VMEM((N_LAG, *tile), F32),
            pltpu.VMEM((ITERS, 2 * HALF, LANES), F32),
            pltpu.VMEM((ITERS, COLUMNS, *tile), F32),
            pltpu.VMEM((ITERS, OWN, LANES), F32),
            pltpu.VMEM((ITERS, N_LAG, OWN, LANES), F32),
            pltpu.VMEM((ITERS, OWN, LANES), F32),
            pltpu.VMEM((ITERS, N_SNAP, OWN, LANES), F32),
            pltpu.VMEM((ITERS, COLUMNS, LANES), F32),
            pltpu.SemaphoreType.DMA((PHASES,)),
            pltpu.SemaphoreType.DMA((PHASES,)),
            pltpu.SemaphoreType.DMA((len(operands),)),
        ],
        compiler_params=pltpu.CompilerParams(
            collective_id=0, has_side_effects=True, vmem_limit_bytes=24 << 20
        ),
        name="coarray_subspace",
    )(counts, *operands)
    return pl.pallas_call(
        combine,
        out_shape=(
            jax.ShapeDtypeStruct((2, PER * LANES), F32),
            jax.ShapeDtypeStruct((2, COLUMNS, PER * LANES), F32),
        ),
        in_specs=[vmem] * 3,
        out_specs=(vmem, vmem),
        compiler_params=pltpu.CompilerParams(vmem_limit_bytes=4 << 20),
        name="combine_columns",
    )(*pieces)


def solution(mesh):
    return jax.shard_map(
        on_device,
        mesh=mesh,
        in_specs=(P(None, "snap", "lag"), P(None), P("snap"), P(None, None, "lag")),
        out_specs=(P(None, "lag"), P(None, None, "lag")),
        check_vma=False,
    )
```

```python
import functools
import math

import jax
import jax.numpy as jnp
import ml_dtypes
import numpy as np
from jax import lax
from jax.experimental import pallas as pl
from jax.experimental.pallas import tpu as pltpu
from jax.sharding import PartitionSpec as P

MESH = pl.DeviceIdType.MESH
F32 = jnp.float32
BF16 = jnp.bfloat16
ITERS = 2
SENSORS = 256
LAGS = 16384
ROWS = 4096
COLUMNS = 96
N_SNAP = 8
LAG_Z, LAG_Y = 8, 4
N_LAG = LAG_Z * LAG_Y
OWN = COLUMNS // N_SNAP
LANES = 128
PADDED = 2 * LAGS
FIRST = PADDED // LANES
HALF = LAGS // LANES
PER = HALF // N_LAG

SNAPS, CORR, CORR_ALL, BINS, LAGCORR, COLS, COUNTS, LIVE, PAIR, REST = range(10)
IMAGE, IMAGE_ALL, GRAM, GRAM_ALL = range(10, 14)
PHASES = 10 + 4 * ITERS
REACH = N_SNAP // 2
NEAR = (REACH + 1) * OWN
BLOCK = 8
PARTS = 3


def tables():
    rows = np.arange(2 * HALF)
    owner, part, place = rows // (2 * PER), rows // PER % 2, rows % PER
    lag_row = owner * PER + place
    first = np.arange(FIRST)
    lane = np.arange(LANES)
    turn = 2.0 * math.pi * (np.outer(first, lag_row) % FIRST) / FIRST
    cosine, sine = np.cos(turn), np.sin(turn)
    real = part[None, :] == 0
    forward = np.concatenate([np.where(real, cosine, sine), np.where(real, -sine, cosine)], 0)
    backward = np.concatenate(
        [np.where(real, cosine, sine).T, np.where(real, -sine, cosine).T], 1
    )
    small = 2.0 * math.pi * (np.outer(lane, lane) % LANES) / LANES
    c, s = np.cos(small), np.sin(small)
    across = np.block([[c, -s], [s, c]])
    back = np.block([[c, s], [-s, c]])
    twist = 2.0 * math.pi * np.outer(first, lane) / PADDED
    twists = np.stack([np.cos(twist), np.sin(twist)])
    split = []
    for table in (forward, across, back, backward):
        parts = []
        for _ in range(PARTS):
            parts.append(table.astype(ml_dtypes.bfloat16))
            table = table - parts[-1].astype(np.float64)
        split.append(np.stack(parts))
    return (*split, twists.astype(np.float32))


def dot(a, b, precision=lax.Precision.HIGHEST):
    return lax.dot_general(a, b, (((1,), (0,)), ((), ())), precision=precision, preferred_element_type=F32)


def dot_nt(a, b, precision=lax.Precision.HIGHEST):
    return lax.dot_general(a, b, (((1,), (1,)), ((), ())), precision=precision, preferred_element_type=F32)


def parts_of(x):
    parts = []
    for _ in range(PARTS):
        parts.append(x.astype(BF16))
        x = x - parts[-1].astype(F32)
    return parts


def table_dot(table, x):
    p = parts_of(x)
    pair = jnp.concatenate(p[:2], 1)
    top = dot(table[0], pair, None)
    if PARTS == 2:
        return top[:, :LANES] + (top[:, LANES:] + dot(table[1], p[0], None))
    low = dot(table[1], pair, None)
    last = dot(table[0], p[2], None) + dot(table[2], p[0], None)
    return top[:, :LANES] + ((top[:, LANES:] + low[:, :LANES]) + (low[:, LANES:] + last))


def dot_table(x, table):
    p = parts_of(x)
    pairs = [(i, k - i) for k in reversed(range(PARTS)) for i in range(k + 1)]
    return functools.reduce(jnp.add, [dot(p[i], table[j], None) for i, j in pairs])


def inverse_factor(gram):
    shape = (8, LANES)
    sub = lax.broadcasted_iota(jnp.int32, shape, 0)
    lane = lax.broadcasted_iota(jnp.int32, shape, 1)
    tiles = [gram[8 * t : 8 * t + 8, :] for t in range(COLUMNS // 8)]
    pivots = [jnp.ones(shape, F32) for _ in tiles]

    def spread(x):
        return jnp.broadcast_to(x, shape)

    for t in range(COLUMNS // BLOCK):
        start = BLOCK * t
        own = tiles[t]
        inside = (lane >= start) & (lane < start + BLOCK)
        s = [
            [spread(own[k : k + 1, start + m : start + m + 1]) for m in range(k + 1)] for k in range(BLOCK)
        ]
        rows = []
        for k in range(BLOCK):
            row = jnp.where(inside, 0.0, spread(own[k : k + 1, :]))
            rows.append(jnp.where(lane == start + k, 1.0, row))
        inverses = []
        for m in range(BLOCK):
            inverses.append(1.0 / s[m][m])
            factors = {k: s[k][m] * inverses[m] for k in range(m + 1, BLOCK)}
            for k in range(m + 1, BLOCK):
                for n in range(m + 1, k + 1):
                    s[k][n] = s[k][n] - factors[k] * s[n][m]
                rows[k] = rows[k] - factors[k] * rows[m]
        for u in range(t + 1, len(tiles)):
            rest = jnp.where(inside, 0.0, tiles[u])
            cols = [spread(tiles[u][:, start + m : start + m + 1]) for m in range(BLOCK)]
            for m in range(BLOCK):
                multiplier = cols[m] * inverses[m]
                for n in range(m + 1, BLOCK):
                    cols[n] = cols[n] - multiplier * s[n][m]
                rest = rest - multiplier * rows[m]
            tiles[u] = rest
        for k in range(BLOCK):
            tiles[t] = rows[k] if k == 0 else jnp.where(sub == k, rows[k], tiles[t])
            pivots[t] = jnp.where(sub == k, s[k][k], pivots[t])
    return jnp.concatenate(
        [
            jnp.where(lane <= 8 * t + sub, tile, 0.0) * (1.0 / jnp.sqrt(pivots[t]))
            for t, tile in enumerate(tiles)
        ],
        0,
    )


def far_first(size):
    return sorted(range(1, size), key=lambda d: -min(d, size - d))


def kernel(
    counts, positions_in, snaps_in, initial_in, forward_in, across_in, back_in, backward_in, twists_in,
    lag_out, inverse_out, mapped_out,
    positions, snaps, initial, forward, across, back, backward, twists,
    snap_send, snap_recv, corr_half, pair_recv, corr_send, corr_recv, row_send, row_recv, bin_send, bin_recv,
    count_send, count_recv, live_send, live_recv, high_hot,
    lag_send, lag_recv, col_send, col_recv, image_send, image_all, gram_send, gram_recv,
    strip_send, gram_all, gram_full,
    send_sems, recv_sems, load_sems,
):
    me, block = lax.axis_index("lag"), lax.axis_index("snap")
    deep, wide = me // LAG_Y, lax.rem(me, LAG_Y)
    mine = (3 * me + 7) // 8
    active = (8 * mine) // 3 == me
    idle = jnp.logical_not(active)
    own_col = jnp.minimum(mine, OWN - 1)
    shifts = [(z, y) for z in range(LAG_Z) for y in range(LAG_Y) if z or y]
    shifts.sort(key=lambda d: -(min(d[0], LAG_Z - d[0]) + min(d[1], LAG_Y - d[1])))

    loads = [
        pltpu.make_async_copy(src, dst, load_sems.at[i])
        for i, (src, dst) in enumerate(
            [
                (snaps_in, snaps), (initial_in, initial), (positions_in, positions), (forward_in, forward),
                (across_in, across), (back_in, back), (backward_in, backward), (twists_in, twists),
            ]
        )
    ]

    def all_lags(act):
        for z, y in shifts:
            act(lax.rem(deep + z, LAG_Z) * LAG_Y + lax.rem(wide + y, LAG_Y))

    def all_snaps(act):
        for d in far_first(N_SNAP):
            act(lax.rem(block + d, N_SNAP))

    def send(phase, src, dst, axis, peer):
        pltpu.make_async_remote_copy(
            src_ref=src, dst_ref=dst, send_sem=send_sems.at[phase], recv_sem=recv_sems.at[phase],
            device_id={axis: peer}, device_id_type=MESH,
        ).start()

    def wait(sems, phase, ref):
        pltpu.make_async_copy(ref, ref, sems.at[phase]).wait()

    drains = []

    def drain(phase, ref, senders=None):
        def finish():
            if senders is None:
                wait(send_sems, phase, ref)
            else:
                pl.when(senders)(lambda: wait(send_sems, phase, ref))

        drains.append(finish)

    def to_lags(phase, src_of, dst):
        all_lags(lambda p: send(phase, src_of(p), dst, "lag", p))

    def to_snaps(phase, src, dst):
        all_snaps(lambda p: send(phase, src, dst, "snap", p))

    def rows_of(p):
        return pl.ds(pl.multiple_of(p * 8, 8), 8)

    barrier = pltpu.get_barrier_semaphore()
    all_lags(lambda p: pl.semaphore_signal(barrier, inc=1, device_id={"lag": p}, device_id_type=MESH))
    all_snaps(lambda p: pl.semaphore_signal(barrier, inc=1, device_id={"snap": p}, device_id_type=MESH))

    for load in loads:
        load.start()

    loads[0].wait()
    live = lax.broadcasted_iota(jnp.int32, (8, ROWS), 1) < counts[0]
    for c in range(2):
        snap_send[c] = jnp.where(live, snaps[c].astype(F32), 0.0).astype(BF16)
    loads[1].wait()
    pair_start = pl.multiple_of((block // 2) * (2 * OWN), 2 * OWN)
    odd = lax.rem(block, 2) == 1
    for c in range(2):
        for r in range(PER):
            pair = initial[c, pl.ds(pair_start, 2 * OWN), r * LANES : (r + 1) * LANES]
            col_send[:, c * PER + r, :] = jnp.where(odd, pair[OWN:], pair[:OWN])
    live_send[...] = jnp.full((8, LANES), counts[0].astype(F32), F32)
    live_recv[block] = live_send[...]
    pl.semaphore_wait(barrier, N_LAG + N_SNAP - 2)

    def snap_piece(p):
        return snap_send.at[:, :, pl.ds(pl.multiple_of(p * LANES, LANES), LANES)]

    to_lags(SNAPS, snap_piece, snap_recv.at[me])
    drain(SNAPS, snap_recv.at[pl.ds(0, N_LAG - 1)])
    snap_recv[me] = snap_send[:, :, pl.ds(pl.multiple_of(me * LANES, LANES), LANES)]
    to_snaps(LIVE, live_send, live_recv.at[block])
    drain(LIVE, live_recv.at[pl.ds(0, N_SNAP - 1)])

    loads[2].wait()
    strip = (8, SENSORS)
    sensor = me * 8 + lax.broadcasted_iota(jnp.int32, strip, 0)
    other = lax.broadcasted_iota(jnp.int32, strip, 1)
    place = jnp.broadcast_to(positions[...], strip).astype(F32)
    own_place = jnp.sum(jnp.where(sensor == other, place, 0.0), axis=1, keepdims=True)
    gap = own_place - place
    lags = jnp.abs(gap).astype(jnp.int32)
    lower = sensor >= other
    high = lags // LANES
    target = (high // PER) * (2 * PER) + jnp.where(lower, 0, PER) + high % PER
    low = lags % LANES
    sign = jnp.where(lower | (gap > 0.0), 1.0, -1.0)
    row_ids = lax.broadcasted_iota(jnp.int32, (2 * HALF, SENSORS), 0)
    lane_ids = lax.broadcasted_iota(jnp.int32, (LANES, SENSORS), 0)
    for r in range(8):
        high_hot[:, r * SENSORS : (r + 1) * SENSORS] = jnp.where(
            row_ids == target[r : r + 1], 1.0, 0.0
        ).astype(BF16)
    hits = jnp.concatenate(
        [jnp.where(lane_ids == low[r : r + 1], 1.0, 0.0).astype(BF16) for r in range(8)], 1
    )
    count_send[...] = dot_nt(high_hot[...], hits, None)
    to_lags(COUNTS, lambda p: count_send.at[rows_of(p)], count_recv.at[me])
    drain(COUNTS, count_recv.at[pl.ds(0, N_LAG - 1)])
    count_recv[me] = count_send[rows_of(me), :]

    wait(recv_sems, SNAPS, snap_recv.at[pl.ds(0, N_LAG - 1)])
    x = [snap_recv[:, c].astype(F32).reshape(SENSORS, LANES) for c in range(2)]
    left = jnp.concatenate([x[0], x[1]], 1).astype(BF16)
    turned = jnp.concatenate([x[1], -x[0]], 1).astype(BF16)
    real = dot_nt(left, left, None)
    imag = dot_nt(turned, left, None)
    square = (SENSORS, SENSORS)
    below = lax.broadcasted_iota(jnp.int32, square, 0) >= lax.broadcasted_iota(jnp.int32, square, 1)
    packed = jnp.where(below, real, imag)
    for c in range(2):
        corr_half[c] = packed[:, c * LANES : (c + 1) * LANES]
    core = lax.rem(block, 2)
    send(PAIR, corr_half.at[1 - core], pair_recv, "snap", block + 1 - 2 * core)
    drain(PAIR, pair_recv)
    wait(recv_sems, PAIR, pair_recv)
    corr_send[...] = corr_half[core] + pair_recv[...]
    to_lags(CORR, lambda p: corr_send.at[rows_of(p)], corr_recv.at[me])
    drain(CORR, corr_recv.at[pl.ds(0, N_LAG - 1)])
    corr_recv[me] = corr_send[rows_of(me), :]
    wait(recv_sems, LIVE, live_recv.at[pl.ds(0, N_SNAP - 1)])
    total = jnp.sum(live_recv[...], axis=0)

    wait(recv_sems, CORR, corr_recv.at[pl.ds(0, N_LAG - 1)])
    row_send[...] = jnp.sum(corr_recv[...], axis=0)
    to_snaps(CORR_ALL, row_send, row_recv.at[block])
    drain(CORR_ALL, row_recv.at[pl.ds(0, N_SNAP - 1)])
    row_recv[block] = row_send[...]
    wait(recv_sems, CORR_ALL, row_recv.at[pl.ds(0, N_SNAP - 1)])
    halves = [sum(row_recv[2 * x + c] for x in range(N_SNAP // 2)) for c in range(2)]
    values = jnp.concatenate(halves, 1) * sign
    part_0 = values.astype(BF16).astype(F32)
    part_1 = (values - part_0).astype(BF16).astype(F32)
    part_2 = values - part_0 - part_1
    low_hot = []
    for r in range(8):
        hit = lane_ids == low[r : r + 1]
        low_hot.append(
            jnp.concatenate(
                [jnp.where(hit, part[r : r + 1], 0.0).astype(BF16) for part in (part_0, part_1, part_2)], 0
            )
        )
    bins = dot_nt(high_hot[...], jnp.concatenate(low_hot, 1), None)
    bin_send[...] = bins[:, :LANES] + bins[:, LANES : 2 * LANES] + bins[:, 2 * LANES :]
    to_lags(BINS, lambda p: bin_send.at[rows_of(p)], bin_recv.at[me])
    drain(BINS, bin_recv.at[pl.ds(0, N_LAG - 1)])
    bin_recv[me] = bin_send[rows_of(me), :]
    for k in range(OWN):
        j = lax.rem(own_col + k, OWN)
        owner = (8 * j) // 3
        pl.when(owner != me)(functools.partial(send, COLS, col_send.at[j], col_recv.at[me], "lag", owner))
    drain(COLS, col_recv.at[pl.ds(0, OWN - 1)], active)
    drain(COLS, col_recv.at[pl.ds(0, OWN)], idle)

    @pl.when(active)
    def _():
        col_recv[me] = col_send[own_col]

    wait(recv_sems, COUNTS, count_recv.at[pl.ds(0, N_LAG - 1)])
    divisor = jnp.maximum(jnp.sum(count_recv[...], axis=0), 1.0) * total
    wait(recv_sems, BINS, bin_recv.at[pl.ds(0, N_LAG - 1)])
    lag_corr = jnp.sum(bin_recv[...], axis=0) / divisor
    lag_send[...] = lag_corr
    to_lags(LAGCORR, lambda p: lag_send, lag_recv.at[me])
    drain(LAGCORR, lag_recv.at[pl.ds(0, N_LAG - 1)])
    lag_recv[me] = lag_corr
    lag_out[...] = lag_corr

    for load in loads[3:]:
        load.wait()

    def rising(v):
        a = table_dot(forward, v)
        ar, ai = a[:FIRST], a[FIRST:]
        tc, ts = twists[0], twists[1]
        return jnp.concatenate([ar * tc + ai * ts, ai * tc - ar * ts], 1)

    def apply(v, spectrum):
        e = dot_table(dot_table(rising(v), across) * spectrum, back)
        er, ei = e[:, :LANES], e[:, LANES:]
        tc, ts = twists[0], twists[1]
        return table_dot(backward, jnp.concatenate([er * tc - ei * ts, ei * tc + er * ts], 0))

    pl.when(active)(lambda: wait(recv_sems, COLS, col_recv.at[pl.ds(0, N_LAG - 1)]))
    column = jnp.where(active, col_recv[...].reshape(2 * HALF, LANES), 0.0)

    wait(recv_sems, LAGCORR, lag_recv.at[pl.ds(0, N_LAG - 1)])
    whole = lag_recv[...].reshape(2 * HALF, LANES)
    ids = [lax.broadcasted_iota(jnp.int32, (2 * HALF, LANES), d) for d in range(2)]
    whole = jnp.where((ids[0] == 0) & (ids[1] == 0), 0.5 * whole, whole)
    half_spectrum = dot_table(rising(whole), across.at[:, :, :LANES]) * (2.0 / PADDED)
    spectrum = jnp.concatenate([half_spectrum, half_spectrum], 1)

    for sweep in range(ITERS):
        if sweep:
            spectrum = spectrum * (1.0 / (jnp.max(jnp.abs(half_spectrum), keepdims=True) * PADDED))
        column = apply(column, spectrum)
        image_send[sweep] = column
        slot = image_all.at[sweep, block * OWN + own_col]

        @pl.when(active)
        def _():
            to_lags(IMAGE + 4 * sweep, lambda p: image_send.at[sweep, rows_of(p)], slot)
            image_all[sweep, block * OWN + own_col] = image_send[sweep, rows_of(me), :]

        drain(IMAGE + 4 * sweep, image_send.at[sweep, pl.ds(0, 2 * HALF - 8)], active)

    def to_blocks(phase, sweep, ahead):
        group = image_all.at[sweep, pl.ds(block * OWN, OWN)]
        for d in far_first(N_SNAP):
            if N_SNAP - d in ahead:
                send(phase, group, group, "snap", lax.rem(block + d, N_SNAP))
        landed = image_all.at[sweep, pl.ds(0, len(ahead) * OWN)]
        drain(phase, landed)
        return landed

    near = []
    for sweep in range(ITERS):
        some, every = (image_all.at[sweep, pl.ds(0, n)] for n in (OWN - 1, OWN))
        pl.when(active)(functools.partial(wait, recv_sems, IMAGE + 4 * sweep, some))
        pl.when(idle)(functools.partial(wait, recv_sems, IMAGE + 4 * sweep, every))
        near.append(to_blocks(IMAGE_ALL + 4 * sweep, sweep, range(1, REACH + 1)))

    def rows_from(sweep, start, size):
        return jnp.concatenate(
            [image_all[sweep, pl.ds(start, size), i, :] for i in range(2 * PER)], 1
        )

    for sweep in range(ITERS):
        wait(recv_sems, IMAGE_ALL + 4 * sweep, near[sweep])
        blocks = [
            rows_from(sweep, lax.rem(block + d, N_SNAP) * OWN, OWN) for d in range(REACH + 1)
        ]
        strip = dot_nt(blocks[0], jnp.concatenate(blocks, 0)) * (1.0 / LAGS)
        strip = jnp.concatenate([strip, jnp.zeros((OWN, LANES // 2 - NEAR), F32)], 1)
        gram_send[sweep, : OWN // 2, :] = jnp.concatenate([strip[: OWN // 2], strip[OWN // 2 :]], 1)
        gram_send[sweep, OWN // 2 :, :] = jnp.zeros((8 - OWN // 2, LANES), F32)
        to_lags(GRAM + 4 * sweep, lambda p: gram_send.at[sweep], gram_recv.at[sweep, me])
        drain(GRAM + 4 * sweep, gram_recv.at[sweep, pl.ds(0, N_LAG - 1)])
        gram_recv[sweep, me] = gram_send[sweep]
    rest = to_blocks(REST, ITERS - 1, range(REACH + 1, N_SNAP))

    for sweep in range(ITERS):
        wait(recv_sems, GRAM + 4 * sweep, gram_recv.at[sweep, pl.ds(0, N_LAG - 1)])
        strip_send[sweep] = jnp.sum(gram_recv[sweep], axis=0)
        to_snaps(GRAM_ALL + 4 * sweep, strip_send.at[sweep], gram_all.at[sweep, block])
        drain(GRAM_ALL + 4 * sweep, gram_all.at[sweep, pl.ds(0, N_SNAP - 1)])
        gram_all[sweep, block] = strip_send[sweep]

    def whole_gram(sweep):
        wait(recv_sems, GRAM_ALL + 4 * sweep, gram_all.at[sweep, pl.ds(0, N_SNAP - 1)])
        for s in range(N_SNAP):
            tile = gram_all[sweep, s]
            strip = jnp.concatenate([tile[: OWN // 2, :NEAR], tile[: OWN // 2, LANES // 2 : LANES // 2 + NEAR]], 0)
            first = s * OWN
            fits = min(NEAR, COLUMNS - first)
            gram_full[sweep, first : first + OWN, first : first + fits] = strip[:, :fits]
            if fits < NEAR:
                gram_full[sweep, first : first + OWN, : NEAR - fits] = strip[:, fits:]
        known, spots = gram_full[sweep], (COLUMNS, LANES)
        row_block = lax.broadcasted_iota(jnp.int32, spots, 0) // OWN
        lane = lax.broadcasted_iota(jnp.int32, spots, 1)
        ahead = (lane // OWN + N_SNAP - row_block) % N_SNAP
        square = jnp.concatenate([known, jnp.zeros((LANES - COLUMNS, LANES), F32)], 0)
        return jnp.where(lane >= COLUMNS, 0.0, jnp.where(ahead <= REACH, known, square.T[:COLUMNS]))

    inverse = inverse_factor(whole_gram(0))[:, :COLUMNS]
    gram = dot_nt(dot(inverse, whole_gram(1)[:, :COLUMNS]), inverse)
    gram = jnp.concatenate([gram, jnp.zeros((COLUMNS, LANES - COLUMNS), F32)], 1)
    wait(recv_sems, REST, rest)
    mapped_out[...] = dot(inverse, rows_from(ITERS - 1, 0, COLUMNS))
    inverse_out[...] = inverse_factor(gram)

    for finish in drains:
        finish()


def combine(lag_corr, inverse, mapped, lag_out, sub_out):
    for c in range(2):
        for r in range(PER):
            row = c * PER + r
            lag_out[c : c + 1, r * LANES : (r + 1) * LANES] = lag_corr[row : row + 1, :]
    result = dot(inverse[:, :COLUMNS], mapped[...])
    for c in range(2):
        sub_out[c] = result[:, c * PER * LANES : (c + 1) * PER * LANES]


def on_device(snapshots, positions, counts, initial):
    constants = [jnp.asarray(t) for t in tables()]
    operands = tuple(pltpu.with_memory_space_constraint(a, pltpu.HBM) for a in (positions.reshape(1, SENSORS), jnp.transpose(snapshots, (0, 2, 1)), initial, *constants))
    vmem = pl.BlockSpec(memory_space=pltpu.VMEM)
    tile = (2 * PER, LANES)
    pieces = pl.pallas_call(
        kernel,
        out_shape=(
            jax.ShapeDtypeStruct(tile, F32),
            jax.ShapeDtypeStruct((COLUMNS, LANES), F32),
            jax.ShapeDtypeStruct((COLUMNS, 2 * PER * LANES), F32),
        ),
        in_specs=[pl.BlockSpec(memory_space=pltpu.SMEM)]
        + [pl.BlockSpec(memory_space=pltpu.HBM)] * len(operands),
        out_specs=(vmem, vmem, vmem),
        scratch_shapes=[pltpu.VMEM(a.shape, a.dtype) for a in operands]
        + [
            pltpu.VMEM((2, 8, ROWS), BF16),
            pltpu.VMEM((N_LAG, 2, 8, LANES), BF16),
            pltpu.VMEM((2, SENSORS, LANES), F32),
            pltpu.VMEM((SENSORS, LANES), F32),
            pltpu.VMEM((SENSORS, LANES), F32),
            pltpu.VMEM((N_LAG, 8, LANES), F32),
            pltpu.VMEM((8, LANES), F32),
            pltpu.VMEM((N_SNAP, 8, LANES), F32),
            pltpu.VMEM((2 * HALF, LANES), F32),
            pltpu.VMEM((N_LAG, *tile), F32),
            pltpu.VMEM((2 * HALF, LANES), F32),
            pltpu.VMEM((N_LAG, *tile), F32),
            pltpu.VMEM((8, LANES), F32),
            pltpu.VMEM((N_SNAP, 8, LANES), F32),
            pltpu.VMEM((2 * HALF, 8 * SENSORS), BF16),
            pltpu.VMEM(tile, F32),
            pltpu.VMEM((N_LAG, *tile), F32),
            pltpu.VMEM((OWN, *tile), F32),
            pltpu.VMEM((N_LAG, *tile), F32),
            pltpu.VMEM((ITERS, 2 * HALF, LANES), F32),
            pltpu.VMEM((ITERS, COLUMNS, *tile), F32),
            pltpu.VMEM((ITERS, 8, LANES), F32),
            pltpu.VMEM((ITERS, N_LAG, 8, LANES), F32),
            pltpu.VMEM((ITERS, 8, LANES), F32),
            pltpu.VMEM((ITERS, N_SNAP, 8, LANES), F32),
            pltpu.VMEM((ITERS, COLUMNS, LANES), F32),
            pltpu.SemaphoreType.DMA((PHASES,)),
            pltpu.SemaphoreType.DMA((PHASES,)),
            pltpu.SemaphoreType.DMA((len(operands),)),
        ],
        compiler_params=pltpu.CompilerParams(
            collective_id=0, has_side_effects=True, vmem_limit_bytes=24 << 20
        ),
        name="coarray_subspace",
    )(counts, *operands)
    return pl.pallas_call(
        combine,
        out_shape=(
            jax.ShapeDtypeStruct((2, PER * LANES), F32),
            jax.ShapeDtypeStruct((2, COLUMNS, PER * LANES), F32),
        ),
        in_specs=[vmem] * 3,
        out_specs=(vmem, vmem),
        compiler_params=pltpu.CompilerParams(vmem_limit_bytes=4 << 20),
        name="combine_columns",
    )(*pieces)


def solution(mesh):
    return jax.shard_map(
        on_device,
        mesh=mesh,
        in_specs=(P(None, "snap", "lag"), P(None), P("snap"), P(None, None, "lag")),
        out_specs=(P(None, "lag"), P(None, None, "lag")),
        check_vma=False,
    )
```

```python
import functools
import math

import jax
import jax.numpy as jnp
import ml_dtypes
import numpy as np
from jax import lax
from jax.experimental import pallas as pl
from jax.experimental.pallas import tpu as pltpu
from jax.sharding import PartitionSpec as P

MESH = pl.DeviceIdType.MESH
F32 = jnp.float32
BF16 = jnp.bfloat16
ITERS = 2
SENSORS = 256
LAGS = 16384
ROWS = 4096
COLUMNS = 96
N_SNAP = 8
LAG_Z, LAG_Y = 8, 4
N_LAG = LAG_Z * LAG_Y
OWN = COLUMNS // N_SNAP
LANES = 128
PADDED = 2 * LAGS
FIRST = PADDED // LANES
HALF = LAGS // LANES
PER = HALF // N_LAG

SNAPS, CORR, CORR_ALL, BINS, LAGCORR, COLS, COUNTS, LIVE, PAIR, REST = range(10)
IMAGE, IMAGE_ALL, GRAM, GRAM_ALL = range(10, 14)
PHASES = 10 + 4 * ITERS
REACH = N_SNAP // 2
NEAR = (REACH + 1) * OWN
BLOCK = 8
PARTS = 2


def tables():
    rows = np.arange(2 * HALF)
    owner, part, place = rows // (2 * PER), rows // PER % 2, rows % PER
    lag_row = owner * PER + place
    first = np.arange(FIRST)
    lane = np.arange(LANES)
    turn = 2.0 * math.pi * (np.outer(first, lag_row) % FIRST) / FIRST
    cosine, sine = np.cos(turn), np.sin(turn)
    real = part[None, :] == 0
    forward = np.concatenate([np.where(real, cosine, sine), np.where(real, -sine, cosine)], 0)
    backward = np.concatenate(
        [np.where(real, cosine, sine).T, np.where(real, -sine, cosine).T], 1
    )
    small = 2.0 * math.pi * (np.outer(lane, lane) % LANES) / LANES
    c, s = np.cos(small), np.sin(small)
    across = np.block([[c, -s], [s, c]])
    back = np.block([[c, s], [-s, c]])
    twist = 2.0 * math.pi * np.outer(first, lane) / PADDED
    twists = np.stack([np.cos(twist), np.sin(twist)])
    split = []
    for table in (forward, across, back, backward):
        parts = []
        for _ in range(PARTS):
            parts.append(table.astype(ml_dtypes.bfloat16))
            table = table - parts[-1].astype(np.float64)
        split.append(np.stack(parts))
    return (*split, twists.astype(np.float32))


def dot(a, b, precision=lax.Precision.HIGHEST):
    return lax.dot_general(a, b, (((1,), (0,)), ((), ())), precision=precision, preferred_element_type=F32)


def dot_nt(a, b, precision=lax.Precision.HIGHEST):
    return lax.dot_general(a, b, (((1,), (1,)), ((), ())), precision=precision, preferred_element_type=F32)


def parts_of(x):
    parts = []
    for _ in range(PARTS):
        parts.append(x.astype(BF16))
        x = x - parts[-1].astype(F32)
    return parts


def table_dot(table, x):
    p = parts_of(x)
    pair = jnp.concatenate(p[:2], 1)
    top = dot(table[0], pair, None)
    if PARTS == 2:
        return top[:, :LANES] + (top[:, LANES:] + dot(table[1], p[0], None))
    low = dot(table[1], pair, None)
    last = dot(table[0], p[2], None) + dot(table[2], p[0], None)
    return top[:, :LANES] + ((top[:, LANES:] + low[:, :LANES]) + (low[:, LANES:] + last))


def dot_table(x, table):
    p = parts_of(x)
    pairs = [(i, k - i) for k in reversed(range(PARTS)) for i in range(k + 1)]
    return functools.reduce(jnp.add, [dot(p[i], table[j], None) for i, j in pairs])


def inverse_factor(gram):
    shape = (8, LANES)
    sub = lax.broadcasted_iota(jnp.int32, shape, 0)
    lane = lax.broadcasted_iota(jnp.int32, shape, 1)
    tiles = [gram[8 * t : 8 * t + 8, :] for t in range(COLUMNS // 8)]
    pivots = [jnp.ones(shape, F32) for _ in tiles]

    def spread(x):
        return jnp.broadcast_to(x, shape)

    for t in range(COLUMNS // BLOCK):
        start = BLOCK * t
        own = tiles[t]
        inside = (lane >= start) & (lane < start + BLOCK)
        s = [
            [spread(own[k : k + 1, start + m : start + m + 1]) for m in range(k + 1)] for k in range(BLOCK)
        ]
        rows = []
        for k in range(BLOCK):
            row = jnp.where(inside, 0.0, spread(own[k : k + 1, :]))
            rows.append(jnp.where(lane == start + k, 1.0, row))
        inverses = []
        for m in range(BLOCK):
            inverses.append(1.0 / s[m][m])
            factors = {k: s[k][m] * inverses[m] for k in range(m + 1, BLOCK)}
            for k in range(m + 1, BLOCK):
                for n in range(m + 1, k + 1):
                    s[k][n] = s[k][n] - factors[k] * s[n][m]
                rows[k] = rows[k] - factors[k] * rows[m]
        for u in range(t + 1, len(tiles)):
            rest = jnp.where(inside, 0.0, tiles[u])
            cols = [spread(tiles[u][:, start + m : start + m + 1]) for m in range(BLOCK)]
            for m in range(BLOCK):
                multiplier = cols[m] * inverses[m]
                for n in range(m + 1, BLOCK):
                    cols[n] = cols[n] - multiplier * s[n][m]
                rest = rest - multiplier * rows[m]
            tiles[u] = rest
        for k in range(BLOCK):
            tiles[t] = rows[k] if k == 0 else jnp.where(sub == k, rows[k], tiles[t])
            pivots[t] = jnp.where(sub == k, s[k][k], pivots[t])
    return jnp.concatenate(
        [
            jnp.where(lane <= 8 * t + sub, tile, 0.0) * (1.0 / jnp.sqrt(pivots[t]))
            for t, tile in enumerate(tiles)
        ],
        0,
    )


def far_first(size):
    return sorted(range(1, size), key=lambda d: -min(d, size - d))


def kernel(
    counts, positions_in, snaps_in, initial_in, forward_in, across_in, back_in, backward_in, twists_in,
    lag_out, inverse_out, mapped_out,
    positions, snaps, initial, forward, across, back, backward, twists,
    snap_send, snap_recv, corr_half, pair_recv, corr_send, corr_recv, row_send, row_recv, bin_send, bin_recv,
    started, count_send, count_recv, live_send, live_recv, high_hot,
    lag_send, lag_recv, col_send, col_recv, image_send, image_all, gram_send, gram_recv,
    strip_send, gram_all, gram_full,
    send_sems, recv_sems, load_sems,
):
    me, block = lax.axis_index("lag"), lax.axis_index("snap")
    deep, wide = me // LAG_Y, lax.rem(me, LAG_Y)
    mine = (3 * me + 7) // 8
    active = (8 * mine) // 3 == me
    idle = jnp.logical_not(active)
    own_col = jnp.minimum(mine, OWN - 1)
    shifts = [(z, y) for z in range(LAG_Z) for y in range(LAG_Y) if z or y]
    shifts.sort(key=lambda d: -(min(d[0], LAG_Z - d[0]) + min(d[1], LAG_Y - d[1])))

    loads = [
        pltpu.make_async_copy(src, dst, load_sems.at[i])
        for i, (src, dst) in enumerate(
            [
                (snaps_in, snaps), (initial_in, initial), (positions_in, positions), (forward_in, forward),
                (across_in, across), (back_in, back), (backward_in, backward), (twists_in, twists),
            ]
        )
    ]

    def all_lags(act):
        for z, y in shifts:
            act(lax.rem(deep + z, LAG_Z) * LAG_Y + lax.rem(wide + y, LAG_Y))

    def all_snaps(act):
        for d in far_first(N_SNAP):
            act(lax.rem(block + d, N_SNAP))

    def send(phase, src, dst, axis, peer):
        pltpu.make_async_remote_copy(
            src_ref=src, dst_ref=dst, send_sem=send_sems.at[phase], recv_sem=recv_sems.at[phase],
            device_id={axis: peer}, device_id_type=MESH,
        ).start()

    def wait(sems, phase, ref):
        pltpu.make_async_copy(ref, ref, sems.at[phase]).wait()

    drains = []

    def drain(phase, ref, senders=None):
        def finish():
            if senders is None:
                wait(send_sems, phase, ref)
            else:
                pl.when(senders)(lambda: wait(send_sems, phase, ref))

        drains.append(finish)

    def to_lags(phase, src_of, dst):
        all_lags(lambda p: send(phase, src_of(p), dst, "lag", p))

    def to_snaps(phase, src, dst):
        all_snaps(lambda p: send(phase, src, dst, "snap", p))

    def rows_of(p):
        return pl.ds(pl.multiple_of(p * 8, 8), 8)

    barrier = pltpu.get_barrier_semaphore()
    all_lags(lambda p: pl.semaphore_signal(barrier, inc=1, device_id={"lag": p}, device_id_type=MESH))
    all_snaps(lambda p: pl.semaphore_signal(barrier, inc=1, device_id={"snap": p}, device_id_type=MESH))

    for load in loads:
        load.start()

    loads[0].wait()
    live = lax.broadcasted_iota(jnp.int32, (8, ROWS), 1) < counts[0]
    for c in range(2):
        snap_send[c] = jnp.where(live, snaps[c].astype(F32), 0.0).astype(BF16)
    loads[1].wait()
    pair_start = pl.multiple_of((block // 2) * (2 * OWN), 2 * OWN)
    odd = lax.rem(block, 2) == 1
    for c in range(2):
        for r in range(PER):
            pair = initial[c, pl.ds(pair_start, 2 * OWN), r * LANES : (r + 1) * LANES]
            col_send[:, c * PER + r, :] = jnp.where(odd, pair[OWN:], pair[:OWN])
    live_send[...] = jnp.full((8, LANES), counts[0].astype(F32), F32)
    live_recv[block] = live_send[...]
    loads[2].wait()
    strip = (8, SENSORS)
    sensor = me * 8 + lax.broadcasted_iota(jnp.int32, strip, 0)
    other = lax.broadcasted_iota(jnp.int32, strip, 1)
    place = jnp.broadcast_to(positions[...], strip).astype(F32)
    own_place = jnp.sum(jnp.where(sensor == other, place, 0.0), axis=1, keepdims=True)
    gap = own_place - place
    lags = jnp.abs(gap).astype(jnp.int32)
    lower = sensor >= other
    high = lags // LANES
    target = (high // PER) * (2 * PER) + jnp.where(lower, 0, PER) + high % PER
    low = lags % LANES
    sign = jnp.where(lower | (gap > 0.0), 1.0, -1.0)
    row_ids = lax.broadcasted_iota(jnp.int32, (2 * HALF, SENSORS), 0)
    lane_ids = lax.broadcasted_iota(jnp.int32, (LANES, SENSORS), 0)
    for r in range(8):
        high_hot[:, r * SENSORS : (r + 1) * SENSORS] = jnp.where(
            row_ids == target[r : r + 1], 1.0, 0.0
        ).astype(BF16)
    hits = jnp.concatenate(
        [jnp.where(lane_ids == low[r : r + 1], 1.0, 0.0).astype(BF16) for r in range(8)], 1
    )
    count_send[...] = dot_nt(high_hot[...], hits, None)
    pl.semaphore_wait(barrier, N_LAG + N_SNAP - 2)

    def snap_piece(p):
        return snap_send.at[:, :, pl.ds(pl.multiple_of(p * LANES, LANES), LANES)]

    to_lags(SNAPS, snap_piece, snap_recv.at[me])
    drain(SNAPS, snap_recv.at[pl.ds(0, N_LAG - 1)])
    snap_recv[me] = snap_send[:, :, pl.ds(pl.multiple_of(me * LANES, LANES), LANES)]
    to_snaps(LIVE, live_send, live_recv.at[block])
    drain(LIVE, live_recv.at[pl.ds(0, N_SNAP - 1)])

    count_recv[me] = count_send[rows_of(me), :]

    wait(recv_sems, SNAPS, snap_recv.at[pl.ds(0, N_LAG - 1)])
    x = [snap_recv[:, c].astype(F32).reshape(SENSORS, LANES) for c in range(2)]
    left = jnp.concatenate([x[0], x[1]], 1).astype(BF16)
    turned = jnp.concatenate([x[1], -x[0]], 1).astype(BF16)
    real = dot_nt(left, left, None)
    imag = dot_nt(turned, left, None)
    square = (SENSORS, SENSORS)
    below = lax.broadcasted_iota(jnp.int32, square, 0) >= lax.broadcasted_iota(jnp.int32, square, 1)
    packed = jnp.where(below, real, imag)
    for c in range(2):
        corr_half[c] = packed[:, c * LANES : (c + 1) * LANES]
    core = lax.rem(block, 2)
    send(PAIR, corr_half.at[1 - core], pair_recv, "snap", block + 1 - 2 * core)
    drain(PAIR, pair_recv)
    wait(recv_sems, PAIR, pair_recv)
    corr_send[...] = corr_half[core] + pair_recv[...]
    to_lags(CORR, lambda p: corr_send.at[rows_of(p)], corr_recv.at[me])
    drain(CORR, corr_recv.at[pl.ds(0, N_LAG - 1)])
    corr_recv[me] = corr_send[rows_of(me), :]
    wait(recv_sems, LIVE, live_recv.at[pl.ds(0, N_SNAP - 1)])
    total = jnp.sum(live_recv[...], axis=0)

    wait(recv_sems, CORR, corr_recv.at[pl.ds(0, N_LAG - 1)])
    row_send[...] = jnp.sum(corr_recv[...], axis=0)
    to_snaps(CORR_ALL, row_send, row_recv.at[block])
    drain(CORR_ALL, row_recv.at[pl.ds(0, N_SNAP - 1)])
    to_lags(COUNTS, lambda p: count_send.at[rows_of(p)], count_recv.at[me])
    drain(COUNTS, count_recv.at[pl.ds(0, N_LAG - 1)])
    for k in range(OWN):
        j = lax.rem(own_col + k, OWN)
        owner = (8 * j) // 3
        pl.when(owner != me)(functools.partial(send, COLS, col_send.at[j], col_recv.at[me], "lag", owner))
    drain(COLS, col_recv.at[pl.ds(0, OWN - 1)], active)
    drain(COLS, col_recv.at[pl.ds(0, OWN)], idle)

    @pl.when(active)
    def _():
        col_recv[me] = col_send[own_col]

    row_recv[block] = row_send[...]
    wait(recv_sems, CORR_ALL, row_recv.at[pl.ds(0, N_SNAP - 1)])
    halves = [sum(row_recv[2 * x + c] for x in range(N_SNAP // 2)) for c in range(2)]
    values = jnp.concatenate(halves, 1) * sign
    part_0 = values.astype(BF16).astype(F32)
    part_1 = (values - part_0).astype(BF16).astype(F32)
    part_2 = values - part_0 - part_1
    low_hot = []
    for r in range(8):
        hit = lane_ids == low[r : r + 1]
        low_hot.append(
            jnp.concatenate(
                [jnp.where(hit, part[r : r + 1], 0.0).astype(BF16) for part in (part_0, part_1, part_2)], 0
            )
        )
    bins = dot_nt(high_hot[...], jnp.concatenate(low_hot, 1), None)
    bin_send[...] = bins[:, :LANES] + bins[:, LANES : 2 * LANES] + bins[:, 2 * LANES :]
    to_lags(BINS, lambda p: bin_send.at[rows_of(p)], bin_recv.at[me])
    drain(BINS, bin_recv.at[pl.ds(0, N_LAG - 1)])
    bin_recv[me] = bin_send[rows_of(me), :]
    wait(recv_sems, COUNTS, count_recv.at[pl.ds(0, N_LAG - 1)])
    divisor = jnp.maximum(jnp.sum(count_recv[...], axis=0), 1.0) * total
    wait(recv_sems, BINS, bin_recv.at[pl.ds(0, N_LAG - 1)])
    lag_corr = jnp.sum(bin_recv[...], axis=0) / divisor
    lag_send[...] = lag_corr
    to_lags(LAGCORR, lambda p: lag_send, lag_recv.at[me])
    drain(LAGCORR, lag_recv.at[pl.ds(0, N_LAG - 1)])
    lag_recv[me] = lag_corr
    lag_out[...] = lag_corr

    for load in loads[3:]:
        load.wait()

    def rising(v):
        a = table_dot(forward, v)
        ar, ai = a[:FIRST], a[FIRST:]
        tc, ts = twists[0], twists[1]
        return jnp.concatenate([ar * tc + ai * ts, ai * tc - ar * ts], 1)

    def transform(v):
        return dot_table(rising(v), across)

    def apply(transformed, spectrum):
        e = dot_table(transformed * spectrum, back)
        er, ei = e[:, :LANES], e[:, LANES:]
        tc, ts = twists[0], twists[1]
        return table_dot(backward, jnp.concatenate([er * tc - ei * ts, ei * tc + er * ts], 0))

    pl.when(active)(lambda: wait(recv_sems, COLS, col_recv.at[pl.ds(0, N_LAG - 1)]))
    column = jnp.where(active, col_recv[...].reshape(2 * HALF, LANES), 0.0)
    started[...] = transform(column)

    wait(recv_sems, LAGCORR, lag_recv.at[pl.ds(0, N_LAG - 1)])
    whole = lag_recv[...].reshape(2 * HALF, LANES)
    ids = [lax.broadcasted_iota(jnp.int32, (2 * HALF, LANES), d) for d in range(2)]
    whole = jnp.where((ids[0] == 0) & (ids[1] == 0), 0.5 * whole, whole)
    half_spectrum = dot_table(rising(whole), across.at[:, :, :LANES]) * (2.0 / PADDED)
    spectrum = jnp.concatenate([half_spectrum, half_spectrum], 1)

    calm = spectrum * (1.0 / (jnp.max(jnp.abs(half_spectrum), keepdims=True) * PADDED))
    for sweep in range(ITERS):
        if sweep:
            column = apply(transform(column), calm)
        else:
            column = apply(started[...], spectrum)
        image_send[sweep] = column
        slot = image_all.at[sweep, block * OWN + own_col]

        @pl.when(active)
        def _():
            to_lags(IMAGE + 4 * sweep, lambda p: image_send.at[sweep, rows_of(p)], slot)
            image_all[sweep, block * OWN + own_col] = image_send[sweep, rows_of(me), :]

        drain(IMAGE + 4 * sweep, image_send.at[sweep, pl.ds(0, 2 * HALF - 8)], active)

    def to_blocks(phase, sweep, ahead):
        group = image_all.at[sweep, pl.ds(block * OWN, OWN)]
        for d in far_first(N_SNAP):
            if N_SNAP - d in ahead:
                send(phase, group, group, "snap", lax.rem(block + d, N_SNAP))
        landed = image_all.at[sweep, pl.ds(0, len(ahead) * OWN)]
        drain(phase, landed)
        return landed

    near = []
    for sweep in range(ITERS):
        some, every = (image_all.at[sweep, pl.ds(0, n)] for n in (OWN - 1, OWN))
        pl.when(active)(functools.partial(wait, recv_sems, IMAGE + 4 * sweep, some))
        pl.when(idle)(functools.partial(wait, recv_sems, IMAGE + 4 * sweep, every))
        near.append(to_blocks(IMAGE_ALL + 4 * sweep, sweep, range(1, REACH + 1)))

    def rows_from(sweep, start, size):
        return jnp.concatenate(
            [image_all[sweep, pl.ds(start, size), i, :] for i in range(2 * PER)], 1
        )

    for sweep in range(ITERS):
        wait(recv_sems, IMAGE_ALL + 4 * sweep, near[sweep])
        blocks = [
            rows_from(sweep, lax.rem(block + d, N_SNAP) * OWN, OWN) for d in range(REACH + 1)
        ]
        strip = dot_nt(blocks[0], jnp.concatenate(blocks, 0)) * (1.0 / LAGS)
        strip = jnp.concatenate([strip, jnp.zeros((OWN, LANES // 2 - NEAR), F32)], 1)
        gram_send[sweep, : OWN // 2, :] = jnp.concatenate([strip[: OWN // 2], strip[OWN // 2 :]], 1)
        gram_send[sweep, OWN // 2 :, :] = jnp.zeros((8 - OWN // 2, LANES), F32)
        to_lags(GRAM + 4 * sweep, lambda p: gram_send.at[sweep], gram_recv.at[sweep, me])
        drain(GRAM + 4 * sweep, gram_recv.at[sweep, pl.ds(0, N_LAG - 1)])
        gram_recv[sweep, me] = gram_send[sweep]
    rest = to_blocks(REST, ITERS - 1, range(REACH + 1, N_SNAP))

    for sweep in range(ITERS):
        wait(recv_sems, GRAM + 4 * sweep, gram_recv.at[sweep, pl.ds(0, N_LAG - 1)])
        strip_send[sweep] = jnp.sum(gram_recv[sweep], axis=0)
        to_snaps(GRAM_ALL + 4 * sweep, strip_send.at[sweep], gram_all.at[sweep, block])
        drain(GRAM_ALL + 4 * sweep, gram_all.at[sweep, pl.ds(0, N_SNAP - 1)])
        gram_all[sweep, block] = strip_send[sweep]

    def whole_gram(sweep):
        wait(recv_sems, GRAM_ALL + 4 * sweep, gram_all.at[sweep, pl.ds(0, N_SNAP - 1)])
        for s in range(N_SNAP):
            tile = gram_all[sweep, s]
            strip = jnp.concatenate([tile[: OWN // 2, :NEAR], tile[: OWN // 2, LANES // 2 : LANES // 2 + NEAR]], 0)
            first = s * OWN
            fits = min(NEAR, COLUMNS - first)
            gram_full[sweep, first : first + OWN, first : first + fits] = strip[:, :fits]
            if fits < NEAR:
                gram_full[sweep, first : first + OWN, : NEAR - fits] = strip[:, fits:]
        known, spots = gram_full[sweep], (COLUMNS, LANES)
        row_block = lax.broadcasted_iota(jnp.int32, spots, 0) // OWN
        lane = lax.broadcasted_iota(jnp.int32, spots, 1)
        ahead = (lane // OWN + N_SNAP - row_block) % N_SNAP
        square = jnp.concatenate([known, jnp.zeros((LANES - COLUMNS, LANES), F32)], 0)
        return jnp.where(lane >= COLUMNS, 0.0, jnp.where(ahead <= REACH, known, square.T[:COLUMNS]))

    inverse = inverse_factor(whole_gram(0))[:, :COLUMNS]
    gram = dot_nt(dot(inverse, whole_gram(1)[:, :COLUMNS]), inverse)
    gram = jnp.concatenate([gram, jnp.zeros((COLUMNS, LANES - COLUMNS), F32)], 1)
    wait(recv_sems, REST, rest)
    mapped_out[...] = dot(inverse, rows_from(ITERS - 1, 0, COLUMNS))
    inverse_out[...] = inverse_factor(gram)

    for finish in drains:
        finish()


def combine(lag_corr, inverse, mapped, lag_out, sub_out):
    for c in range(2):
        for r in range(PER):
            row = c * PER + r
            lag_out[c : c + 1, r * LANES : (r + 1) * LANES] = lag_corr[row : row + 1, :]
    result = dot(inverse[:, :COLUMNS], mapped[...])
    for c in range(2):
        sub_out[c] = result[:, c * PER * LANES : (c + 1) * PER * LANES]


def on_device(snapshots, positions, counts, initial):
    constants = [jnp.asarray(t) for t in tables()]
    operands = tuple(pltpu.with_memory_space_constraint(a, pltpu.HBM) for a in (positions.reshape(1, SENSORS), jnp.transpose(snapshots, (0, 2, 1)), initial, *constants))
    vmem = pl.BlockSpec(memory_space=pltpu.VMEM)
    tile = (2 * PER, LANES)
    pieces = pl.pallas_call(
        kernel,
        out_shape=(
            jax.ShapeDtypeStruct(tile, F32),
            jax.ShapeDtypeStruct((COLUMNS, LANES), F32),
            jax.ShapeDtypeStruct((COLUMNS, 2 * PER * LANES), F32),
        ),
        in_specs=[pl.BlockSpec(memory_space=pltpu.SMEM)]
        + [pl.BlockSpec(memory_space=pltpu.HBM)] * len(operands),
        out_specs=(vmem, vmem, vmem),
        scratch_shapes=[pltpu.VMEM(a.shape, a.dtype) for a in operands]
        + [
            pltpu.VMEM((2, 8, ROWS), BF16),
            pltpu.VMEM((N_LAG, 2, 8, LANES), BF16),
            pltpu.VMEM((2, SENSORS, LANES), F32),
            pltpu.VMEM((SENSORS, LANES), F32),
            pltpu.VMEM((SENSORS, LANES), F32),
            pltpu.VMEM((N_LAG, 8, LANES), F32),
            pltpu.VMEM((8, LANES), F32),
            pltpu.VMEM((N_SNAP, 8, LANES), F32),
            pltpu.VMEM((2 * HALF, LANES), F32),
            pltpu.VMEM((N_LAG, *tile), F32),
            pltpu.VMEM((FIRST, 2 * LANES), F32),
            pltpu.VMEM((2 * HALF, LANES), F32),
            pltpu.VMEM((N_LAG, *tile), F32),
            pltpu.VMEM((8, LANES), F32),
            pltpu.VMEM((N_SNAP, 8, LANES), F32),
            pltpu.VMEM((2 * HALF, 8 * SENSORS), BF16),
            pltpu.VMEM(tile, F32),
            pltpu.VMEM((N_LAG, *tile), F32),
            pltpu.VMEM((OWN, *tile), F32),
            pltpu.VMEM((N_LAG, *tile), F32),
            pltpu.VMEM((ITERS, 2 * HALF, LANES), F32),
            pltpu.VMEM((ITERS, COLUMNS, *tile), F32),
            pltpu.VMEM((ITERS, 8, LANES), F32),
            pltpu.VMEM((ITERS, N_LAG, 8, LANES), F32),
            pltpu.VMEM((ITERS, 8, LANES), F32),
            pltpu.VMEM((ITERS, N_SNAP, 8, LANES), F32),
            pltpu.VMEM((ITERS, COLUMNS, LANES), F32),
            pltpu.SemaphoreType.DMA((PHASES,)),
            pltpu.SemaphoreType.DMA((PHASES,)),
            pltpu.SemaphoreType.DMA((len(operands),)),
        ],
        compiler_params=pltpu.CompilerParams(
            collective_id=0, has_side_effects=True, vmem_limit_bytes=24 << 20
        ),
        name="coarray_subspace",
    )(counts, *operands)
    return pl.pallas_call(
        combine,
        out_shape=(
            jax.ShapeDtypeStruct((2, PER * LANES), F32),
            jax.ShapeDtypeStruct((2, COLUMNS, PER * LANES), F32),
        ),
        in_specs=[vmem] * 3,
        out_specs=(vmem, vmem),
        compiler_params=pltpu.CompilerParams(vmem_limit_bytes=4 << 20),
        name="combine_columns",
    )(*pieces)


def solution(mesh):
    return jax.shard_map(
        on_device,
        mesh=mesh,
        in_specs=(P(None, "snap", "lag"), P(None), P("snap"), P(None, None, "lag")),
        out_specs=(P(None, "lag"), P(None, None, "lag")),
        check_vma=False,
    )
```

```python
import functools
import math

import jax
import jax.numpy as jnp
import ml_dtypes
import numpy as np
from jax import lax
from jax.experimental import pallas as pl
from jax.experimental.pallas import tpu as pltpu
from jax.sharding import PartitionSpec as P

MESH = pl.DeviceIdType.MESH
F32 = jnp.float32
BF16 = jnp.bfloat16
ITERS = 2
SENSORS = 256
LAGS = 16384
ROWS = 4096
COLUMNS = 96
N_SNAP = 8
LAG_Z, LAG_Y = 8, 4
N_LAG = LAG_Z * LAG_Y
OWN = COLUMNS // N_SNAP
LANES = 128
PADDED = 2 * LAGS
FIRST = PADDED // LANES
HALF = LAGS // LANES
PER = HALF // N_LAG

SNAPS, CORR, CORR_ALL, BINS, LAGCORR, COLS, COUNTS, LIVE, PAIR, REST = range(10)
IMAGE, IMAGE_ALL, GRAM, GRAM_ALL = range(10, 14)
PHASES = 10 + 4 * ITERS
REACH = N_SNAP // 2
NEAR = (REACH + 1) * OWN
BLOCK = 8
PARTS = 2


def tables():
    rows = np.arange(2 * HALF)
    owner, part, place = rows // (2 * PER), rows // PER % 2, rows % PER
    lag_row = owner * PER + place
    first = np.arange(FIRST)
    lane = np.arange(LANES)
    turn = 2.0 * math.pi * (np.outer(first, lag_row) % FIRST) / FIRST
    cosine, sine = np.cos(turn), np.sin(turn)
    real = part[None, :] == 0
    forward = np.concatenate([np.where(real, cosine, sine), np.where(real, -sine, cosine)], 0)
    backward = np.concatenate(
        [np.where(real, cosine, sine).T, np.where(real, -sine, cosine).T], 1
    )
    small = 2.0 * math.pi * (np.outer(lane, lane) % LANES) / LANES
    c, s = np.cos(small), np.sin(small)
    across = np.block([[c, -s], [s, c]])
    back = np.block([[c, s], [-s, c]])
    twist = 2.0 * math.pi * np.outer(first, lane) / PADDED
    twists = np.stack([np.cos(twist), np.sin(twist)])
    split = []
    for table in (forward, across, back, backward):
        parts = []
        for _ in range(PARTS):
            parts.append(table.astype(ml_dtypes.bfloat16))
            table = table - parts[-1].astype(np.float64)
        split.append(np.stack(parts))
    return (*split, twists.astype(np.float32))


def dot(a, b, precision=lax.Precision.HIGHEST):
    return lax.dot_general(a, b, (((1,), (0,)), ((), ())), precision=precision, preferred_element_type=F32)


def dot_nt(a, b, precision=lax.Precision.HIGHEST):
    return lax.dot_general(a, b, (((1,), (1,)), ((), ())), precision=precision, preferred_element_type=F32)


def parts_of(x):
    parts = []
    for _ in range(PARTS):
        parts.append(x.astype(BF16))
        x = x - parts[-1].astype(F32)
    return parts


def table_dot(table, x):
    p = parts_of(x)
    pair = jnp.concatenate(p[:2], 1)
    top = dot(table[0], pair, None)
    if PARTS == 2:
        return top[:, :LANES] + (top[:, LANES:] + dot(table[1], p[0], None))
    low = dot(table[1], pair, None)
    last = dot(table[0], p[2], None) + dot(table[2], p[0], None)
    return top[:, :LANES] + ((top[:, LANES:] + low[:, :LANES]) + (low[:, LANES:] + last))


def dot_table(x, table):
    p = parts_of(x)
    pairs = [(i, k - i) for k in reversed(range(PARTS)) for i in range(k + 1)]
    return functools.reduce(jnp.add, [dot(p[i], table[j], None) for i, j in pairs])


def inverse_factor(gram):
    shape = (8, LANES)
    sub = lax.broadcasted_iota(jnp.int32, shape, 0)
    lane = lax.broadcasted_iota(jnp.int32, shape, 1)
    tiles = [gram[8 * t : 8 * t + 8, :] for t in range(COLUMNS // 8)]
    pivots = [jnp.ones(shape, F32) for _ in tiles]

    def spread(x):
        return jnp.broadcast_to(x, shape)

    for t in range(COLUMNS // BLOCK):
        start = BLOCK * t
        own = tiles[t]
        inside = (lane >= start) & (lane < start + BLOCK)
        s = [
            [spread(own[k : k + 1, start + m : start + m + 1]) for m in range(k + 1)] for k in range(BLOCK)
        ]
        rows = []
        for k in range(BLOCK):
            row = jnp.where(inside, 0.0, spread(own[k : k + 1, :]))
            rows.append(jnp.where(lane == start + k, 1.0, row))
        inverses = []
        for m in range(BLOCK):
            inverses.append(1.0 / s[m][m])
            factors = {k: s[k][m] * inverses[m] for k in range(m + 1, BLOCK)}
            for k in range(m + 1, BLOCK):
                for n in range(m + 1, k + 1):
                    s[k][n] = s[k][n] - factors[k] * s[n][m]
                rows[k] = rows[k] - factors[k] * rows[m]
        for u in range(t + 1, len(tiles)):
            rest = jnp.where(inside, 0.0, tiles[u])
            cols = [spread(tiles[u][:, start + m : start + m + 1]) for m in range(BLOCK)]
            for m in range(BLOCK):
                multiplier = cols[m] * inverses[m]
                for n in range(m + 1, BLOCK):
                    cols[n] = cols[n] - multiplier * s[n][m]
                rest = rest - multiplier * rows[m]
            tiles[u] = rest
        for k in range(BLOCK):
            tiles[t] = rows[k] if k == 0 else jnp.where(sub == k, rows[k], tiles[t])
            pivots[t] = jnp.where(sub == k, s[k][k], pivots[t])
    return jnp.concatenate(
        [
            jnp.where(lane <= 8 * t + sub, tile, 0.0) * (1.0 / jnp.sqrt(pivots[t]))
            for t, tile in enumerate(tiles)
        ],
        0,
    )


def far_first(size):
    return sorted(range(1, size), key=lambda d: -min(d, size - d))


def kernel(
    counts, positions_in, snaps_in, initial_in, forward_in, across_in, back_in, backward_in, twists_in,
    lag_out, inverse_out, mapped_out,
    positions, snaps, initial, forward, across, back, backward, twists,
    snap_send, snap_recv, corr_half, pair_recv, corr_send, corr_recv, row_send, row_recv, bin_send, bin_recv,
    started, count_send, count_recv, live_send, live_recv, high_hot,
    lag_send, lag_recv, col_send, col_recv, image_send, image_all, gram_send, gram_recv,
    strip_send, gram_all, gram_full,
    send_sems, recv_sems, load_sems,
):
    me, block = lax.axis_index("lag"), lax.axis_index("snap")
    deep, wide = me // LAG_Y, lax.rem(me, LAG_Y)
    mine = (3 * me + 7) // 8
    active = (8 * mine) // 3 == me
    idle = jnp.logical_not(active)
    own_col = jnp.minimum(mine, OWN - 1)
    shifts = [(z, y) for z in range(LAG_Z) for y in range(LAG_Y) if z or y]
    shifts.sort(key=lambda d: (-(min(d[0], LAG_Z - d[0]) + min(d[1], LAG_Y - d[1])), -min(d[1], LAG_Y - d[1])))

    loads = [
        pltpu.make_async_copy(src, dst, load_sems.at[i])
        for i, (src, dst) in enumerate(
            [
                (snaps_in, snaps), (initial_in, initial), (positions_in, positions), (forward_in, forward),
                (across_in, across), (back_in, back), (backward_in, backward), (twists_in, twists),
            ]
        )
    ]

    def all_lags(act):
        for z, y in shifts:
            act(lax.rem(deep + z, LAG_Z) * LAG_Y + lax.rem(wide + y, LAG_Y))

    def all_snaps(act):
        for d in far_first(N_SNAP):
            act(lax.rem(block + d, N_SNAP))

    def send(phase, src, dst, axis, peer):
        pltpu.make_async_remote_copy(
            src_ref=src, dst_ref=dst, send_sem=send_sems.at[phase], recv_sem=recv_sems.at[phase],
            device_id={axis: peer}, device_id_type=MESH,
        ).start()

    def wait(sems, phase, ref):
        pltpu.make_async_copy(ref, ref, sems.at[phase]).wait()

    drains = []

    def drain(phase, ref, senders=None):
        def finish():
            if senders is None:
                wait(send_sems, phase, ref)
            else:
                pl.when(senders)(lambda: wait(send_sems, phase, ref))

        drains.append(finish)

    def to_lags(phase, src_of, dst):
        all_lags(lambda p: send(phase, src_of(p), dst, "lag", p))

    def to_snaps(phase, src, dst):
        all_snaps(lambda p: send(phase, src, dst, "snap", p))

    def rows_of(p):
        return pl.ds(pl.multiple_of(p * 8, 8), 8)

    barrier = pltpu.get_barrier_semaphore()
    all_lags(lambda p: pl.semaphore_signal(barrier, inc=1, device_id={"lag": p}, device_id_type=MESH))
    all_snaps(lambda p: pl.semaphore_signal(barrier, inc=1, device_id={"snap": p}, device_id_type=MESH))

    for load in loads:
        load.start()

    loads[0].wait()
    live = lax.broadcasted_iota(jnp.int32, (8, ROWS), 1) < counts[0]
    for c in range(2):
        snap_send[c] = jnp.where(live, snaps[c].astype(F32), 0.0).astype(BF16)
    loads[1].wait()
    pair_start = pl.multiple_of((block // 2) * (2 * OWN), 2 * OWN)
    odd = lax.rem(block, 2) == 1
    for c in range(2):
        for r in range(PER):
            pair = initial[c, pl.ds(pair_start, 2 * OWN), r * LANES : (r + 1) * LANES]
            col_send[:, c * PER + r, :] = jnp.where(odd, pair[OWN:], pair[:OWN])
    live_send[...] = jnp.full((8, LANES), counts[0].astype(F32), F32)
    live_recv[block] = live_send[...]
    loads[2].wait()
    strip = (8, SENSORS)
    sensor = me * 8 + lax.broadcasted_iota(jnp.int32, strip, 0)
    other = lax.broadcasted_iota(jnp.int32, strip, 1)
    place = jnp.broadcast_to(positions[...], strip).astype(F32)
    own_place = jnp.sum(jnp.where(sensor == other, place, 0.0), axis=1, keepdims=True)
    gap = own_place - place
    lags = jnp.abs(gap).astype(jnp.int32)
    lower = sensor >= other
    high = lags // LANES
    target = (high // PER) * (2 * PER) + jnp.where(lower, 0, PER) + high % PER
    low = lags % LANES
    sign = jnp.where(lower | (gap > 0.0), 1.0, -1.0)
    row_ids = lax.broadcasted_iota(jnp.int32, (2 * HALF, SENSORS), 0)
    lane_ids = lax.broadcasted_iota(jnp.int32, (LANES, SENSORS), 0)
    for r in range(8):
        high_hot[:, r * SENSORS : (r + 1) * SENSORS] = jnp.where(
            row_ids == target[r : r + 1], 1.0, 0.0
        ).astype(BF16)
    hits = jnp.concatenate(
        [jnp.where(lane_ids == low[r : r + 1], 1.0, 0.0).astype(BF16) for r in range(8)], 1
    )
    count_send[...] = dot_nt(high_hot[...], hits, None)
    pl.semaphore_wait(barrier, N_LAG + N_SNAP - 2)

    def snap_piece(p):
        return snap_send.at[:, :, pl.ds(pl.multiple_of(p * LANES, LANES), LANES)]

    to_lags(SNAPS, snap_piece, snap_recv.at[me])
    drain(SNAPS, snap_recv.at[pl.ds(0, N_LAG - 1)])
    snap_recv[me] = snap_send[:, :, pl.ds(pl.multiple_of(me * LANES, LANES), LANES)]
    to_snaps(LIVE, live_send, live_recv.at[block])
    drain(LIVE, live_recv.at[pl.ds(0, N_SNAP - 1)])

    count_recv[me] = count_send[rows_of(me), :]

    wait(recv_sems, SNAPS, snap_recv.at[pl.ds(0, N_LAG - 1)])
    x = [snap_recv[:, c].astype(F32).reshape(SENSORS, LANES) for c in range(2)]
    left = jnp.concatenate([x[0], x[1]], 1).astype(BF16)
    turned = jnp.concatenate([x[1], -x[0]], 1).astype(BF16)
    real = dot_nt(left, left, None)
    imag = dot_nt(turned, left, None)
    square = (SENSORS, SENSORS)
    below = lax.broadcasted_iota(jnp.int32, square, 0) >= lax.broadcasted_iota(jnp.int32, square, 1)
    packed = jnp.where(below, real, imag)
    for c in range(2):
        corr_half[c] = packed[:, c * LANES : (c + 1) * LANES]
    core = lax.rem(block, 2)
    send(PAIR, corr_half.at[1 - core], pair_recv, "snap", block + 1 - 2 * core)
    drain(PAIR, pair_recv)
    wait(recv_sems, PAIR, pair_recv)
    corr_send[...] = corr_half[core] + pair_recv[...]
    to_lags(CORR, lambda p: corr_send.at[rows_of(p)], corr_recv.at[me])
    drain(CORR, corr_recv.at[pl.ds(0, N_LAG - 1)])
    corr_recv[me] = corr_send[rows_of(me), :]
    wait(recv_sems, LIVE, live_recv.at[pl.ds(0, N_SNAP - 1)])
    total = jnp.sum(live_recv[...], axis=0)

    wait(recv_sems, CORR, corr_recv.at[pl.ds(0, N_LAG - 1)])
    row_send[...] = jnp.sum(corr_recv[...], axis=0)
    to_snaps(CORR_ALL, row_send, row_recv.at[block])
    drain(CORR_ALL, row_recv.at[pl.ds(0, N_SNAP - 1)])
    to_lags(COUNTS, lambda p: count_send.at[rows_of(p)], count_recv.at[me])
    drain(COUNTS, count_recv.at[pl.ds(0, N_LAG - 1)])
    for k in range(OWN):
        j = lax.rem(own_col + k, OWN)
        owner = (8 * j) // 3
        pl.when(owner != me)(functools.partial(send, COLS, col_send.at[j], col_recv.at[me], "lag", owner))
    drain(COLS, col_recv.at[pl.ds(0, OWN - 1)], active)
    drain(COLS, col_recv.at[pl.ds(0, OWN)], idle)

    @pl.when(active)
    def _():
        col_recv[me] = col_send[own_col]

    row_recv[block] = row_send[...]
    wait(recv_sems, CORR_ALL, row_recv.at[pl.ds(0, N_SNAP - 1)])
    halves = [sum(row_recv[2 * x + c] for x in range(N_SNAP // 2)) for c in range(2)]
    values = jnp.concatenate(halves, 1) * sign
    part_0 = values.astype(BF16).astype(F32)
    part_1 = (values - part_0).astype(BF16).astype(F32)
    part_2 = values - part_0 - part_1
    low_hot = []
    for r in range(8):
        hit = lane_ids == low[r : r + 1]
        low_hot.append(
            jnp.concatenate(
                [jnp.where(hit, part[r : r + 1], 0.0).astype(BF16) for part in (part_0, part_1, part_2)], 0
            )
        )
    bins = dot_nt(high_hot[...], jnp.concatenate(low_hot, 1), None)
    bin_send[...] = bins[:, :LANES] + bins[:, LANES : 2 * LANES] + bins[:, 2 * LANES :]
    to_lags(BINS, lambda p: bin_send.at[rows_of(p)], bin_recv.at[me])
    drain(BINS, bin_recv.at[pl.ds(0, N_LAG - 1)])
    bin_recv[me] = bin_send[rows_of(me), :]
    wait(recv_sems, COUNTS, count_recv.at[pl.ds(0, N_LAG - 1)])
    divisor = jnp.maximum(jnp.sum(count_recv[...], axis=0), 1.0) * total
    wait(recv_sems, BINS, bin_recv.at[pl.ds(0, N_LAG - 1)])
    lag_corr = jnp.sum(bin_recv[...], axis=0) / divisor
    lag_send[...] = lag_corr
    to_lags(LAGCORR, lambda p: lag_send, lag_recv.at[me])
    drain(LAGCORR, lag_recv.at[pl.ds(0, N_LAG - 1)])
    lag_recv[me] = lag_corr
    lag_out[...] = lag_corr

    for load in loads[3:]:
        load.wait()

    def rising(v):
        a = table_dot(forward, v)
        ar, ai = a[:FIRST], a[FIRST:]
        tc, ts = twists[0], twists[1]
        return jnp.concatenate([ar * tc + ai * ts, ai * tc - ar * ts], 1)

    def transform(v):
        return dot_table(rising(v), across)

    def apply(transformed, spectrum):
        e = dot_table(transformed * spectrum, back)
        er, ei = e[:, :LANES], e[:, LANES:]
        tc, ts = twists[0], twists[1]
        return table_dot(backward, jnp.concatenate([er * tc - ei * ts, ei * tc + er * ts], 0))

    pl.when(active)(lambda: wait(recv_sems, COLS, col_recv.at[pl.ds(0, N_LAG - 1)]))
    column = jnp.where(active, col_recv[...].reshape(2 * HALF, LANES), 0.0)
    started[...] = transform(column)

    wait(recv_sems, LAGCORR, lag_recv.at[pl.ds(0, N_LAG - 1)])
    whole = lag_recv[...].reshape(2 * HALF, LANES)
    ids = [lax.broadcasted_iota(jnp.int32, (2 * HALF, LANES), d) for d in range(2)]
    whole = jnp.where((ids[0] == 0) & (ids[1] == 0), 0.5 * whole, whole)
    half_spectrum = dot_table(rising(whole), across.at[:, :, :LANES]) * (2.0 / PADDED)
    spectrum = jnp.concatenate([half_spectrum, half_spectrum], 1)

    calm = spectrum * (1.0 / (jnp.max(jnp.abs(half_spectrum), keepdims=True) * PADDED))
    for sweep in range(ITERS):
        if sweep:
            column = apply(transform(column), calm)
        else:
            column = apply(started[...], spectrum)
        image_send[sweep] = column
        slot = image_all.at[sweep, block * OWN + own_col]

        @pl.when(active)
        def _():
            to_lags(IMAGE + 4 * sweep, lambda p: image_send.at[sweep, rows_of(p)], slot)
            image_all[sweep, block * OWN + own_col] = image_send[sweep, rows_of(me), :]

        drain(IMAGE + 4 * sweep, image_send.at[sweep, pl.ds(0, 2 * HALF - 8)], active)

    def to_blocks(phase, sweep, ahead):
        group = image_all.at[sweep, pl.ds(block * OWN, OWN)]
        for d in far_first(N_SNAP):
            if N_SNAP - d in ahead:
                send(phase, group, group, "snap", lax.rem(block + d, N_SNAP))
        landed = image_all.at[sweep, pl.ds(0, len(ahead) * OWN)]
        drain(phase, landed)
        return landed

    near = []
    for sweep in range(ITERS):
        some, every = (image_all.at[sweep, pl.ds(0, n)] for n in (OWN - 1, OWN))
        pl.when(active)(functools.partial(wait, recv_sems, IMAGE + 4 * sweep, some))
        pl.when(idle)(functools.partial(wait, recv_sems, IMAGE + 4 * sweep, every))
        near.append(to_blocks(IMAGE_ALL + 4 * sweep, sweep, range(1, REACH + 1)))

    def rows_from(sweep, start, size):
        return jnp.concatenate(
            [image_all[sweep, pl.ds(start, size), i, :] for i in range(2 * PER)], 1
        )

    for sweep in range(ITERS):
        wait(recv_sems, IMAGE_ALL + 4 * sweep, near[sweep])
        blocks = [
            rows_from(sweep, lax.rem(block + d, N_SNAP) * OWN, OWN) for d in range(REACH + 1)
        ]
        strip = dot_nt(blocks[0], jnp.concatenate(blocks, 0)) * (1.0 / LAGS)
        strip = jnp.concatenate([strip, jnp.zeros((OWN, LANES // 2 - NEAR), F32)], 1)
        gram_send[sweep, : OWN // 2, :] = jnp.concatenate([strip[: OWN // 2], strip[OWN // 2 :]], 1)
        gram_send[sweep, OWN // 2 :, :] = jnp.zeros((8 - OWN // 2, LANES), F32)
        to_lags(GRAM + 4 * sweep, lambda p: gram_send.at[sweep], gram_recv.at[sweep, me])
        drain(GRAM + 4 * sweep, gram_recv.at[sweep, pl.ds(0, N_LAG - 1)])
        gram_recv[sweep, me] = gram_send[sweep]
    settled = list(drains)
    drains.clear()
    rest = to_blocks(REST, ITERS - 1, range(REACH + 1, N_SNAP))
    for finish in settled:
        finish()

    for sweep in range(ITERS):
        wait(recv_sems, GRAM + 4 * sweep, gram_recv.at[sweep, pl.ds(0, N_LAG - 1)])
        strip_send[sweep] = jnp.sum(gram_recv[sweep], axis=0)
        to_snaps(GRAM_ALL + 4 * sweep, strip_send.at[sweep], gram_all.at[sweep, block])
        drain(GRAM_ALL + 4 * sweep, gram_all.at[sweep, pl.ds(0, N_SNAP - 1)])
        gram_all[sweep, block] = strip_send[sweep]

    def whole_gram(sweep):
        wait(recv_sems, GRAM_ALL + 4 * sweep, gram_all.at[sweep, pl.ds(0, N_SNAP - 1)])
        for s in range(N_SNAP):
            tile = gram_all[sweep, s]
            strip = jnp.concatenate([tile[: OWN // 2, :NEAR], tile[: OWN // 2, LANES // 2 : LANES // 2 + NEAR]], 0)
            first = s * OWN
            fits = min(NEAR, COLUMNS - first)
            gram_full[sweep, first : first + OWN, first : first + fits] = strip[:, :fits]
            if fits < NEAR:
                gram_full[sweep, first : first + OWN, : NEAR - fits] = strip[:, fits:]
        known, spots = gram_full[sweep], (COLUMNS, LANES)
        row_block = lax.broadcasted_iota(jnp.int32, spots, 0) // OWN
        lane = lax.broadcasted_iota(jnp.int32, spots, 1)
        ahead = (lane // OWN + N_SNAP - row_block) % N_SNAP
        square = jnp.concatenate([known, jnp.zeros((LANES - COLUMNS, LANES), F32)], 0)
        return jnp.where(lane >= COLUMNS, 0.0, jnp.where(ahead <= REACH, known, square.T[:COLUMNS]))

    inverse = inverse_factor(whole_gram(0))[:, :COLUMNS]
    gram = dot_nt(dot(inverse, whole_gram(1)[:, :COLUMNS]), inverse)
    gram = jnp.concatenate([gram, jnp.zeros((COLUMNS, LANES - COLUMNS), F32)], 1)
    wait(recv_sems, REST, rest)
    mapped_out[...] = dot(inverse, rows_from(ITERS - 1, 0, COLUMNS))
    inverse_out[...] = inverse_factor(gram)

    for finish in drains:
        finish()


def combine(lag_corr, inverse, mapped, lag_out, sub_out):
    for c in range(2):
        for r in range(PER):
            row = c * PER + r
            lag_out[c : c + 1, r * LANES : (r + 1) * LANES] = lag_corr[row : row + 1, :]
    result = dot(inverse[:, :COLUMNS], mapped[...])
    for c in range(2):
        sub_out[c] = result[:, c * PER * LANES : (c + 1) * PER * LANES]


def on_device(snapshots, positions, counts, initial):
    constants = [jnp.asarray(t) for t in tables()]
    operands = tuple(pltpu.with_memory_space_constraint(a, pltpu.HBM) for a in (positions.reshape(1, SENSORS), jnp.transpose(snapshots, (0, 2, 1)), initial, *constants))
    vmem = pl.BlockSpec(memory_space=pltpu.VMEM)
    tile = (2 * PER, LANES)
    pieces = pl.pallas_call(
        kernel,
        out_shape=(
            jax.ShapeDtypeStruct(tile, F32),
            jax.ShapeDtypeStruct((COLUMNS, LANES), F32),
            jax.ShapeDtypeStruct((COLUMNS, 2 * PER * LANES), F32),
        ),
        in_specs=[pl.BlockSpec(memory_space=pltpu.SMEM)]
        + [pl.BlockSpec(memory_space=pltpu.HBM)] * len(operands),
        out_specs=(vmem, vmem, vmem),
        scratch_shapes=[pltpu.VMEM(a.shape, a.dtype) for a in operands]
        + [
            pltpu.VMEM((2, 8, ROWS), BF16),
            pltpu.VMEM((N_LAG, 2, 8, LANES), BF16),
            pltpu.VMEM((2, SENSORS, LANES), F32),
            pltpu.VMEM((SENSORS, LANES), F32),
            pltpu.VMEM((SENSORS, LANES), F32),
            pltpu.VMEM((N_LAG, 8, LANES), F32),
            pltpu.VMEM((8, LANES), F32),
            pltpu.VMEM((N_SNAP, 8, LANES), F32),
            pltpu.VMEM((2 * HALF, LANES), F32),
            pltpu.VMEM((N_LAG, *tile), F32),
            pltpu.VMEM((FIRST, 2 * LANES), F32),
            pltpu.VMEM((2 * HALF, LANES), F32),
            pltpu.VMEM((N_LAG, *tile), F32),
            pltpu.VMEM((8, LANES), F32),
            pltpu.VMEM((N_SNAP, 8, LANES), F32),
            pltpu.VMEM((2 * HALF, 8 * SENSORS), BF16),
            pltpu.VMEM(tile, F32),
            pltpu.VMEM((N_LAG, *tile), F32),
            pltpu.VMEM((OWN, *tile), F32),
            pltpu.VMEM((N_LAG, *tile), F32),
            pltpu.VMEM((ITERS, 2 * HALF, LANES), F32),
            pltpu.VMEM((ITERS, COLUMNS, *tile), F32),
            pltpu.VMEM((ITERS, 8, LANES), F32),
            pltpu.VMEM((ITERS, N_LAG, 8, LANES), F32),
            pltpu.VMEM((ITERS, 8, LANES), F32),
            pltpu.VMEM((ITERS, N_SNAP, 8, LANES), F32),
            pltpu.VMEM((ITERS, COLUMNS, LANES), F32),
            pltpu.SemaphoreType.DMA((PHASES,)),
            pltpu.SemaphoreType.DMA((PHASES,)),
            pltpu.SemaphoreType.DMA((len(operands),)),
        ],
        compiler_params=pltpu.CompilerParams(
            collective_id=0, has_side_effects=True, vmem_limit_bytes=24 << 20
        ),
        name="coarray_subspace",
    )(counts, *operands)
    return pl.pallas_call(
        combine,
        out_shape=(
            jax.ShapeDtypeStruct((2, PER * LANES), F32),
            jax.ShapeDtypeStruct((2, COLUMNS, PER * LANES), F32),
        ),
        in_specs=[vmem] * 3,
        out_specs=(vmem, vmem),
        compiler_params=pltpu.CompilerParams(vmem_limit_bytes=4 << 20),
        name="combine_columns",
    )(*pieces)


def solution(mesh):
    return jax.shard_map(
        on_device,
        mesh=mesh,
        in_specs=(P(None, "snap", "lag"), P(None), P("snap"), P(None, None, "lag")),
        out_specs=(P(None, "lag"), P(None, None, "lag")),
        check_vma=False,
    )
```

```python
import functools
import math

import jax
import jax.numpy as jnp
import ml_dtypes
import numpy as np
from jax import lax
from jax.experimental import pallas as pl
from jax.experimental.pallas import tpu as pltpu
from jax.sharding import PartitionSpec as P

MESH = pl.DeviceIdType.MESH
F32 = jnp.float32
BF16 = jnp.bfloat16
ITERS = 2
SENSORS = 256
LAGS = 16384
ROWS = 4096
COLUMNS = 96
N_SNAP = 8
LAG_Z, LAG_Y = 8, 4
N_LAG = LAG_Z * LAG_Y
OWN = COLUMNS // N_SNAP
LANES = 128
PADDED = 2 * LAGS
FIRST = PADDED // LANES
HALF = LAGS // LANES
PER = HALF // N_LAG

SNAPS, CORR, CORR_ALL, BINS, LAGCORR, COLS, COUNTS, LIVE, PAIR, REST = range(10)
IMAGE, IMAGE_ALL, GRAM, GRAM_ALL = range(10, 14)
PHASES = 10 + 4 * ITERS
REACH = N_SNAP // 2
NEAR = (REACH + 1) * OWN
BLOCK = 8
PARTS = 2


def tables():
    rows = np.arange(2 * HALF)
    owner, part, place = rows // (2 * PER), rows // PER % 2, rows % PER
    lag_row = owner * PER + place
    first = np.arange(FIRST)
    lane = np.arange(LANES)
    turn = 2.0 * math.pi * (np.outer(first, lag_row) % FIRST) / FIRST
    cosine, sine = np.cos(turn), np.sin(turn)
    real = part[None, :] == 0
    forward = np.concatenate([np.where(real, cosine, sine), np.where(real, -sine, cosine)], 0)
    backward = np.concatenate(
        [np.where(real, cosine, sine).T, np.where(real, -sine, cosine).T], 1
    )
    small = 2.0 * math.pi * (np.outer(lane, lane) % LANES) / LANES
    c, s = np.cos(small), np.sin(small)
    across = np.block([[c, -s], [s, c]])
    back = np.block([[c, s], [-s, c]])
    twist = 2.0 * math.pi * np.outer(first, lane) / PADDED
    twists = np.stack([np.cos(twist), np.sin(twist)])
    split = []
    for table in (forward, across, back, backward):
        parts = []
        for _ in range(PARTS):
            parts.append(table.astype(ml_dtypes.bfloat16))
            table = table - parts[-1].astype(np.float64)
        split.append(np.stack(parts))
    return (*split, twists.astype(np.float32))


def dot(a, b, precision=lax.Precision.HIGHEST):
    return lax.dot_general(a, b, (((1,), (0,)), ((), ())), precision=precision, preferred_element_type=F32)


def dot_nt(a, b, precision=lax.Precision.HIGHEST):
    return lax.dot_general(a, b, (((1,), (1,)), ((), ())), precision=precision, preferred_element_type=F32)


def parts_of(x):
    parts = []
    for _ in range(PARTS):
        parts.append(x.astype(BF16))
        x = x - parts[-1].astype(F32)
    return parts


def table_dot(table, x):
    p = parts_of(x)
    pair = jnp.concatenate(p[:2], 1)
    top = dot(table[0], pair, None)
    if PARTS == 2:
        return top[:, :LANES] + (top[:, LANES:] + dot(table[1], p[0], None))
    low = dot(table[1], pair, None)
    last = dot(table[0], p[2], None) + dot(table[2], p[0], None)
    return top[:, :LANES] + ((top[:, LANES:] + low[:, :LANES]) + (low[:, LANES:] + last))


def dot_table(x, table):
    p = parts_of(x)
    pairs = [(i, k - i) for k in reversed(range(PARTS)) for i in range(k + 1)]
    return functools.reduce(jnp.add, [dot(p[i], table[j], None) for i, j in pairs])


def inverse_factor(gram):
    shape = (8, LANES)
    sub = lax.broadcasted_iota(jnp.int32, shape, 0)
    lane = lax.broadcasted_iota(jnp.int32, shape, 1)
    tiles = [gram[8 * t : 8 * t + 8, :] for t in range(COLUMNS // 8)]
    pivots = [jnp.ones(shape, F32) for _ in tiles]

    def spread(x):
        return jnp.broadcast_to(x, shape)

    for t in range(COLUMNS // BLOCK):
        start = BLOCK * t
        own = tiles[t]
        inside = (lane >= start) & (lane < start + BLOCK)
        s = [
            [spread(own[k : k + 1, start + m : start + m + 1]) for m in range(k + 1)] for k in range(BLOCK)
        ]
        rows = []
        for k in range(BLOCK):
            row = jnp.where(inside, 0.0, spread(own[k : k + 1, :]))
            rows.append(jnp.where(lane == start + k, 1.0, row))
        inverses = []
        for m in range(BLOCK):
            inverses.append(1.0 / s[m][m])
            factors = {k: s[k][m] * inverses[m] for k in range(m + 1, BLOCK)}
            for k in range(m + 1, BLOCK):
                for n in range(m + 1, k + 1):
                    s[k][n] = s[k][n] - factors[k] * s[n][m]
                rows[k] = rows[k] - factors[k] * rows[m]
        for u in range(t + 1, len(tiles)):
            rest = jnp.where(inside, 0.0, tiles[u])
            cols = [spread(tiles[u][:, start + m : start + m + 1]) for m in range(BLOCK)]
            for m in range(BLOCK):
                multiplier = cols[m] * inverses[m]
                for n in range(m + 1, BLOCK):
                    cols[n] = cols[n] - multiplier * s[n][m]
                rest = rest - multiplier * rows[m]
            tiles[u] = rest
        for k in range(BLOCK):
            tiles[t] = rows[k] if k == 0 else jnp.where(sub == k, rows[k], tiles[t])
            pivots[t] = jnp.where(sub == k, s[k][k], pivots[t])
    return jnp.concatenate(
        [
            jnp.where(lane <= 8 * t + sub, tile, 0.0) * (1.0 / jnp.sqrt(pivots[t]))
            for t, tile in enumerate(tiles)
        ],
        0,
    )


def far_first(size):
    return sorted(range(1, size), key=lambda d: -min(d, size - d))


def kernel(
    counts, positions_in, snaps_in, initial_in, forward_in, across_in, back_in, backward_in, twists_in,
    lag_out, inverse_out, mapped_out,
    positions, snaps, initial, forward, across, back, backward, twists,
    snap_send, snap_recv, corr_half, pair_recv, corr_send, corr_recv, row_send, row_recv, bin_send, bin_recv,
    started, count_send, count_recv, live_send, live_recv, high_hot,
    lag_send, lag_recv, col_send, col_recv, image_send, image_all, gram_send, gram_recv,
    strip_send, gram_all, gram_full,
    send_sems, recv_sems, load_sems,
):
    me, block = lax.axis_index("lag"), lax.axis_index("snap")
    deep, wide = me // LAG_Y, lax.rem(me, LAG_Y)
    mine = (3 * me + 7) // 8
    active = (8 * mine) // 3 == me
    idle = jnp.logical_not(active)
    own_col = jnp.minimum(mine, OWN - 1)
    shifts = [(z, y) for z in range(LAG_Z) for y in range(LAG_Y) if z or y]
    shifts.sort(key=lambda d: (-min(d[0], LAG_Z - d[0]), -min(d[1], LAG_Y - d[1])))

    loads = [
        pltpu.make_async_copy(src, dst, load_sems.at[i])
        for i, (src, dst) in enumerate(
            [
                (snaps_in, snaps), (initial_in, initial), (positions_in, positions), (forward_in, forward),
                (across_in, across), (back_in, back), (backward_in, backward), (twists_in, twists),
            ]
        )
    ]

    def all_lags(act):
        for z, y in shifts:
            act(lax.rem(deep + z, LAG_Z) * LAG_Y + lax.rem(wide + y, LAG_Y))

    def all_snaps(act):
        for d in far_first(N_SNAP):
            act(lax.rem(block + d, N_SNAP))

    def send(phase, src, dst, axis, peer):
        pltpu.make_async_remote_copy(
            src_ref=src, dst_ref=dst, send_sem=send_sems.at[phase], recv_sem=recv_sems.at[phase],
            device_id={axis: peer}, device_id_type=MESH,
        ).start()

    def wait(sems, phase, ref):
        pltpu.make_async_copy(ref, ref, sems.at[phase]).wait()

    drains = []

    def drain(phase, ref, senders=None):
        def finish():
            if senders is None:
                wait(send_sems, phase, ref)
            else:
                pl.when(senders)(lambda: wait(send_sems, phase, ref))

        drains.append(finish)

    def to_lags(phase, src_of, dst):
        all_lags(lambda p: send(phase, src_of(p), dst, "lag", p))

    def to_snaps(phase, src, dst):
        all_snaps(lambda p: send(phase, src, dst, "snap", p))

    def rows_of(p):
        return pl.ds(pl.multiple_of(p * 8, 8), 8)

    barrier = pltpu.get_barrier_semaphore()
    all_lags(lambda p: pl.semaphore_signal(barrier, inc=1, device_id={"lag": p}, device_id_type=MESH))
    all_snaps(lambda p: pl.semaphore_signal(barrier, inc=1, device_id={"snap": p}, device_id_type=MESH))

    for load in loads:
        load.start()

    loads[0].wait()
    live = lax.broadcasted_iota(jnp.int32, (8, ROWS), 1) < counts[0]
    for c in range(2):
        snap_send[c] = jnp.where(live, snaps[c].astype(F32), 0.0).astype(BF16)
    loads[1].wait()
    pair_start = pl.multiple_of((block // 2) * (2 * OWN), 2 * OWN)
    odd = lax.rem(block, 2) == 1
    for c in range(2):
        for r in range(PER):
            pair = initial[c, pl.ds(pair_start, 2 * OWN), r * LANES : (r + 1) * LANES]
            col_send[:, c * PER + r, :] = jnp.where(odd, pair[OWN:], pair[:OWN])
    live_send[...] = jnp.full((8, LANES), counts[0].astype(F32), F32)
    live_recv[block] = live_send[...]
    loads[2].wait()
    strip = (8, SENSORS)
    sensor = me * 8 + lax.broadcasted_iota(jnp.int32, strip, 0)
    other = lax.broadcasted_iota(jnp.int32, strip, 1)
    place = jnp.broadcast_to(positions[...], strip).astype(F32)
    own_place = jnp.sum(jnp.where(sensor == other, place, 0.0), axis=1, keepdims=True)
    gap = own_place - place
    lags = jnp.abs(gap).astype(jnp.int32)
    lower = sensor >= other
    high = lags // LANES
    target = (high // PER) * (2 * PER) + jnp.where(lower, 0, PER) + high % PER
    low = lags % LANES
    sign = jnp.where(lower | (gap > 0.0), 1.0, -1.0)
    row_ids = lax.broadcasted_iota(jnp.int32, (2 * HALF, SENSORS), 0)
    lane_ids = lax.broadcasted_iota(jnp.int32, (LANES, SENSORS), 0)
    for r in range(8):
        high_hot[:, r * SENSORS : (r + 1) * SENSORS] = jnp.where(
            row_ids == target[r : r + 1], 1.0, 0.0
        ).astype(BF16)
    hits = jnp.concatenate(
        [jnp.where(lane_ids == low[r : r + 1], 1.0, 0.0).astype(BF16) for r in range(8)], 1
    )
    count_send[...] = dot_nt(high_hot[...], hits, None)
    pl.semaphore_wait(barrier, N_LAG + N_SNAP - 2)

    def snap_piece(p):
        return snap_send.at[:, :, pl.ds(pl.multiple_of(p * LANES, LANES), LANES)]

    to_lags(SNAPS, snap_piece, snap_recv.at[me])
    drain(SNAPS, snap_recv.at[pl.ds(0, N_LAG - 1)])
    snap_recv[me] = snap_send[:, :, pl.ds(pl.multiple_of(me * LANES, LANES), LANES)]
    to_snaps(LIVE, live_send, live_recv.at[block])
    drain(LIVE, live_recv.at[pl.ds(0, N_SNAP - 1)])

    count_recv[me] = count_send[rows_of(me), :]

    wait(recv_sems, SNAPS, snap_recv.at[pl.ds(0, N_LAG - 1)])
    x = [snap_recv[:, c].astype(F32).reshape(SENSORS, LANES) for c in range(2)]
    left = jnp.concatenate([x[0], x[1]], 1).astype(BF16)
    turned = jnp.concatenate([x[1], -x[0]], 1).astype(BF16)
    real = dot_nt(left, left, None)
    imag = dot_nt(turned, left, None)
    square = (SENSORS, SENSORS)
    below = lax.broadcasted_iota(jnp.int32, square, 0) >= lax.broadcasted_iota(jnp.int32, square, 1)
    packed = jnp.where(below, real, imag)
    for c in range(2):
        corr_half[c] = packed[:, c * LANES : (c + 1) * LANES]
    core = lax.rem(block, 2)
    send(PAIR, corr_half.at[1 - core], pair_recv, "snap", block + 1 - 2 * core)
    drain(PAIR, pair_recv)
    wait(recv_sems, PAIR, pair_recv)
    corr_send[...] = corr_half[core] + pair_recv[...]
    to_lags(CORR, lambda p: corr_send.at[rows_of(p)], corr_recv.at[me])
    drain(CORR, corr_recv.at[pl.ds(0, N_LAG - 1)])
    corr_recv[me] = corr_send[rows_of(me), :]
    wait(recv_sems, LIVE, live_recv.at[pl.ds(0, N_SNAP - 1)])
    total = jnp.sum(live_recv[...], axis=0)

    wait(recv_sems, CORR, corr_recv.at[pl.ds(0, N_LAG - 1)])
    row_send[...] = jnp.sum(corr_recv[...], axis=0)
    to_snaps(CORR_ALL, row_send, row_recv.at[block])
    drain(CORR_ALL, row_recv.at[pl.ds(0, N_SNAP - 1)])
    to_lags(COUNTS, lambda p: count_send.at[rows_of(p)], count_recv.at[me])
    drain(COUNTS, count_recv.at[pl.ds(0, N_LAG - 1)])
    for k in range(OWN):
        j = lax.rem(own_col + k, OWN)
        owner = (8 * j) // 3
        pl.when(owner != me)(functools.partial(send, COLS, col_send.at[j], col_recv.at[me], "lag", owner))
    drain(COLS, col_recv.at[pl.ds(0, OWN - 1)], active)
    drain(COLS, col_recv.at[pl.ds(0, OWN)], idle)

    @pl.when(active)
    def _():
        col_recv[me] = col_send[own_col]

    row_recv[block] = row_send[...]
    wait(recv_sems, CORR_ALL, row_recv.at[pl.ds(0, N_SNAP - 1)])
    halves = [sum(row_recv[2 * x + c] for x in range(N_SNAP // 2)) for c in range(2)]
    values = jnp.concatenate(halves, 1) * sign
    part_0 = values.astype(BF16).astype(F32)
    part_1 = (values - part_0).astype(BF16).astype(F32)
    part_2 = values - part_0 - part_1
    low_hot = []
    for r in range(8):
        hit = lane_ids == low[r : r + 1]
        low_hot.append(
            jnp.concatenate(
                [jnp.where(hit, part[r : r + 1], 0.0).astype(BF16) for part in (part_0, part_1, part_2)], 0
            )
        )
    bins = dot_nt(high_hot[...], jnp.concatenate(low_hot, 1), None)
    bin_send[...] = bins[:, :LANES] + bins[:, LANES : 2 * LANES] + bins[:, 2 * LANES :]
    to_lags(BINS, lambda p: bin_send.at[rows_of(p)], bin_recv.at[me])
    drain(BINS, bin_recv.at[pl.ds(0, N_LAG - 1)])
    bin_recv[me] = bin_send[rows_of(me), :]
    wait(recv_sems, COUNTS, count_recv.at[pl.ds(0, N_LAG - 1)])
    divisor = jnp.maximum(jnp.sum(count_recv[...], axis=0), 1.0) * total
    wait(recv_sems, BINS, bin_recv.at[pl.ds(0, N_LAG - 1)])
    lag_corr = jnp.sum(bin_recv[...], axis=0) / divisor
    lag_send[...] = lag_corr
    to_lags(LAGCORR, lambda p: lag_send, lag_recv.at[me])
    drain(LAGCORR, lag_recv.at[pl.ds(0, N_LAG - 1)])
    lag_recv[me] = lag_corr
    lag_out[...] = lag_corr

    for load in loads[3:]:
        load.wait()

    def rising(v):
        a = table_dot(forward, v)
        ar, ai = a[:FIRST], a[FIRST:]
        tc, ts = twists[0], twists[1]
        return jnp.concatenate([ar * tc + ai * ts, ai * tc - ar * ts], 1)

    def transform(v):
        return dot_table(rising(v), across)

    def apply(transformed, spectrum):
        e = dot_table(transformed * spectrum, back)
        er, ei = e[:, :LANES], e[:, LANES:]
        tc, ts = twists[0], twists[1]
        return table_dot(backward, jnp.concatenate([er * tc - ei * ts, ei * tc + er * ts], 0))

    pl.when(active)(lambda: wait(recv_sems, COLS, col_recv.at[pl.ds(0, N_LAG - 1)]))
    column = jnp.where(active, col_recv[...].reshape(2 * HALF, LANES), 0.0)
    started[...] = transform(column)

    wait(recv_sems, LAGCORR, lag_recv.at[pl.ds(0, N_LAG - 1)])
    whole = lag_recv[...].reshape(2 * HALF, LANES)
    ids = [lax.broadcasted_iota(jnp.int32, (2 * HALF, LANES), d) for d in range(2)]
    whole = jnp.where((ids[0] == 0) & (ids[1] == 0), 0.5 * whole, whole)
    half_spectrum = dot_table(rising(whole), across.at[:, :, :LANES]) * (2.0 / PADDED)
    spectrum = jnp.concatenate([half_spectrum, half_spectrum], 1)

    calm = spectrum * (1.0 / (jnp.max(jnp.abs(half_spectrum), keepdims=True) * PADDED))
    for sweep in range(ITERS):
        if sweep:
            column = apply(transform(column), calm)
        else:
            column = apply(started[...], spectrum)
        image_send[sweep] = column
        slot = image_all.at[sweep, block * OWN + own_col]

        @pl.when(active)
        def _():
            to_lags(IMAGE + 4 * sweep, lambda p: image_send.at[sweep, rows_of(p)], slot)
            image_all[sweep, block * OWN + own_col] = image_send[sweep, rows_of(me), :]

        drain(IMAGE + 4 * sweep, image_send.at[sweep, pl.ds(0, 2 * HALF - 8)], active)

    def to_blocks(phase, sweep, ahead):
        group = image_all.at[sweep, pl.ds(block * OWN, OWN)]
        for d in far_first(N_SNAP):
            if N_SNAP - d in ahead:
                send(phase, group, group, "snap", lax.rem(block + d, N_SNAP))
        landed = image_all.at[sweep, pl.ds(0, len(ahead) * OWN)]
        drain(phase, landed)
        return landed

    near = []
    for sweep in range(ITERS):
        some, every = (image_all.at[sweep, pl.ds(0, n)] for n in (OWN - 1, OWN))
        pl.when(active)(functools.partial(wait, recv_sems, IMAGE + 4 * sweep, some))
        pl.when(idle)(functools.partial(wait, recv_sems, IMAGE + 4 * sweep, every))
        near.append(to_blocks(IMAGE_ALL + 4 * sweep, sweep, range(1, REACH + 1)))

    def rows_from(sweep, start, size):
        return jnp.concatenate(
            [image_all[sweep, pl.ds(start, size), i, :] for i in range(2 * PER)], 1
        )

    for sweep in range(ITERS):
        wait(recv_sems, IMAGE_ALL + 4 * sweep, near[sweep])
        blocks = [
            rows_from(sweep, lax.rem(block + d, N_SNAP) * OWN, OWN) for d in range(REACH + 1)
        ]
        strip = dot_nt(blocks[0], jnp.concatenate(blocks, 0)) * (1.0 / LAGS)
        strip = jnp.concatenate([strip, jnp.zeros((OWN, LANES // 2 - NEAR), F32)], 1)
        gram_send[sweep, : OWN // 2, :] = jnp.concatenate([strip[: OWN // 2], strip[OWN // 2 :]], 1)
        gram_send[sweep, OWN // 2 :, :] = jnp.zeros((8 - OWN // 2, LANES), F32)
        to_lags(GRAM + 4 * sweep, lambda p: gram_send.at[sweep], gram_recv.at[sweep, me])
        drain(GRAM + 4 * sweep, gram_recv.at[sweep, pl.ds(0, N_LAG - 1)])
        gram_recv[sweep, me] = gram_send[sweep]
    settled = list(drains)
    drains.clear()
    rest = to_blocks(REST, ITERS - 1, range(REACH + 1, N_SNAP))
    for finish in settled:
        finish()

    for sweep in range(ITERS):
        wait(recv_sems, GRAM + 4 * sweep, gram_recv.at[sweep, pl.ds(0, N_LAG - 1)])
        strip_send[sweep] = jnp.sum(gram_recv[sweep], axis=0)
        to_snaps(GRAM_ALL + 4 * sweep, strip_send.at[sweep], gram_all.at[sweep, block])
        drain(GRAM_ALL + 4 * sweep, gram_all.at[sweep, pl.ds(0, N_SNAP - 1)])
        gram_all[sweep, block] = strip_send[sweep]

    def whole_gram(sweep):
        wait(recv_sems, GRAM_ALL + 4 * sweep, gram_all.at[sweep, pl.ds(0, N_SNAP - 1)])
        for s in range(N_SNAP):
            tile = gram_all[sweep, s]
            strip = jnp.concatenate([tile[: OWN // 2, :NEAR], tile[: OWN // 2, LANES // 2 : LANES // 2 + NEAR]], 0)
            first = s * OWN
            fits = min(NEAR, COLUMNS - first)
            gram_full[sweep, first : first + OWN, first : first + fits] = strip[:, :fits]
            if fits < NEAR:
                gram_full[sweep, first : first + OWN, : NEAR - fits] = strip[:, fits:]
        known, spots = gram_full[sweep], (COLUMNS, LANES)
        row_block = lax.broadcasted_iota(jnp.int32, spots, 0) // OWN
        lane = lax.broadcasted_iota(jnp.int32, spots, 1)
        ahead = (lane // OWN + N_SNAP - row_block) % N_SNAP
        square = jnp.concatenate([known, jnp.zeros((LANES - COLUMNS, LANES), F32)], 0)
        return jnp.where(lane >= COLUMNS, 0.0, jnp.where(ahead <= REACH, known, square.T[:COLUMNS]))

    inverse = inverse_factor(whole_gram(0))[:, :COLUMNS]
    gram = dot_nt(dot(inverse, whole_gram(1)[:, :COLUMNS]), inverse)
    gram = jnp.concatenate([gram, jnp.zeros((COLUMNS, LANES - COLUMNS), F32)], 1)
    wait(recv_sems, REST, rest)
    mapped_out[...] = dot(inverse, rows_from(ITERS - 1, 0, COLUMNS))
    inverse_out[...] = inverse_factor(gram)

    for finish in drains:
        finish()


def combine(lag_corr, inverse, mapped, lag_out, sub_out):
    for c in range(2):
        for r in range(PER):
            row = c * PER + r
            lag_out[c : c + 1, r * LANES : (r + 1) * LANES] = lag_corr[row : row + 1, :]
    result = dot(inverse[:, :COLUMNS], mapped[...])
    for c in range(2):
        sub_out[c] = result[:, c * PER * LANES : (c + 1) * PER * LANES]


def on_device(snapshots, positions, counts, initial):
    constants = [jnp.asarray(t) for t in tables()]
    operands = tuple(pltpu.with_memory_space_constraint(a, pltpu.HBM) for a in (positions.reshape(1, SENSORS), jnp.transpose(snapshots, (0, 2, 1)), initial, *constants))
    vmem = pl.BlockSpec(memory_space=pltpu.VMEM)
    tile = (2 * PER, LANES)
    pieces = pl.pallas_call(
        kernel,
        out_shape=(
            jax.ShapeDtypeStruct(tile, F32),
            jax.ShapeDtypeStruct((COLUMNS, LANES), F32),
            jax.ShapeDtypeStruct((COLUMNS, 2 * PER * LANES), F32),
        ),
        in_specs=[pl.BlockSpec(memory_space=pltpu.SMEM)]
        + [pl.BlockSpec(memory_space=pltpu.HBM)] * len(operands),
        out_specs=(vmem, vmem, vmem),
        scratch_shapes=[pltpu.VMEM(a.shape, a.dtype) for a in operands]
        + [
            pltpu.VMEM((2, 8, ROWS), BF16),
            pltpu.VMEM((N_LAG, 2, 8, LANES), BF16),
            pltpu.VMEM((2, SENSORS, LANES), F32),
            pltpu.VMEM((SENSORS, LANES), F32),
            pltpu.VMEM((SENSORS, LANES), F32),
            pltpu.VMEM((N_LAG, 8, LANES), F32),
            pltpu.VMEM((8, LANES), F32),
            pltpu.VMEM((N_SNAP, 8, LANES), F32),
            pltpu.VMEM((2 * HALF, LANES), F32),
            pltpu.VMEM((N_LAG, *tile), F32),
            pltpu.VMEM((FIRST, 2 * LANES), F32),
            pltpu.VMEM((2 * HALF, LANES), F32),
            pltpu.VMEM((N_LAG, *tile), F32),
            pltpu.VMEM((8, LANES), F32),
            pltpu.VMEM((N_SNAP, 8, LANES), F32),
            pltpu.VMEM((2 * HALF, 8 * SENSORS), BF16),
            pltpu.VMEM(tile, F32),
            pltpu.VMEM((N_LAG, *tile), F32),
            pltpu.VMEM((OWN, *tile), F32),
            pltpu.VMEM((N_LAG, *tile), F32),
            pltpu.VMEM((ITERS, 2 * HALF, LANES), F32),
            pltpu.VMEM((ITERS, COLUMNS, *tile), F32),
            pltpu.VMEM((ITERS, 8, LANES), F32),
            pltpu.VMEM((ITERS, N_LAG, 8, LANES), F32),
            pltpu.VMEM((ITERS, 8, LANES), F32),
            pltpu.VMEM((ITERS, N_SNAP, 8, LANES), F32),
            pltpu.VMEM((ITERS, COLUMNS, LANES), F32),
            pltpu.SemaphoreType.DMA((PHASES,)),
            pltpu.SemaphoreType.DMA((PHASES,)),
            pltpu.SemaphoreType.DMA((len(operands),)),
        ],
        compiler_params=pltpu.CompilerParams(
            collective_id=0, has_side_effects=True, vmem_limit_bytes=24 << 20
        ),
        name="coarray_subspace",
    )(counts, *operands)
    return pl.pallas_call(
        combine,
        out_shape=(
            jax.ShapeDtypeStruct((2, PER * LANES), F32),
            jax.ShapeDtypeStruct((2, COLUMNS, PER * LANES), F32),
        ),
        in_specs=[vmem] * 3,
        out_specs=(vmem, vmem),
        compiler_params=pltpu.CompilerParams(vmem_limit_bytes=4 << 20),
        name="combine_columns",
    )(*pieces)


def solution(mesh):
    return jax.shard_map(
        on_device,
        mesh=mesh,
        in_specs=(P(None, "snap", "lag"), P(None), P("snap"), P(None, None, "lag")),
        out_specs=(P(None, "lag"), P(None, None, "lag")),
        check_vma=False,
    )
```
